512 devices in a mesh: chord: 16 (over y, x), wall: 32 (over z, core).
Axes of the slice: x: 4, y: 4, z: 16, core: 2. Of those that a mesh axis runs over, the one named last changes fastest.
Arguments:
- rhs: float32 [5, 16, 64, 2048], P(None, None, 'wall', 'chord'), may hold values from -0.3 to 0.3
- jet_mask: int32 [16, 64, 2048], P(None, 'wall', 'chord'), may hold values 0 or 1
- jet_source: float32 [5], replicated, may hold values from -0.3 to 0.3
- wall_flags: int32 [16, 2048], P(None, 'chord'), may hold values from 0 to 2
- bc_table: float32 [3, 5], replicated, may hold values from 0.2 to 1.5
- xi_lower: float32 [5, 5, 16, 64, 2048], P(None, None, None, 'wall', 'chord'), may hold values from -1.2 to 1.2
- xi_upper: float32 [5, 5, 16, 64, 2048], P(None, None, None, 'wall', 'chord'), may hold values from -1.2 to 1.2
- eta_lower: float32 [5, 5, 16, 64, 2048], P(None, None, None, 'wall', 'chord'), may hold values from -1.2 to 1.2
- eta_upper: float32 [5, 5, 16, 64, 2048], P(None, None, None, 'wall', 'chord'), may hold values from -1.2 to 1.2
Outputs:
- increment: float32 [5, 16, 64, 2048], P(None, None, 'wall', 'chord')
The draws below stay inside these ranges and needn't reach their ends.
All inputs are finite; a program needn't handle non-finite values. No bound on the sum of `jet_mask` on one device may be relied on, other than what follows from the above.
Results may differ from the reference program's by a relative error of at most 0.00019.
Values sent between devices are 32-bit elements; how exact they have to be, the bound alone decides.
No kernel may reach another device: no remote copies, remote signals or barrier semaphores. Data moves between devices by JAX's collectives and lax.ppermute only.
A program may use at most 64 MiB of HBM per device.

```python
import math
import jax
import jax.numpy as jnp
from jax import lax

SPAN = 16
COMP = 5
FLAGS = 3
CHORD_CELLS = 2048
NORMAL_CELLS = 64


def chain_blocks(key, pulse_length, chain_axis):
    random_keys = jax.random.split(key, 6)
    if chain_axis == 4:
        rate_shape = (5, SPAN, NORMAL_CELLS, 1)
        pulse_profile = (1, 1, 1, CHORD_CELLS)
    else:
        rate_shape = (5, SPAN, 1, CHORD_CELLS)
        pulse_profile = (1, 1, NORMAL_CELLS, 1)
    share_slow = 0.5
    slow = jax.random.uniform(random_keys[0], rate_shape) < share_slow
    slow_time = pulse_length * jnp.exp(jax.random.uniform(random_keys[1], rate_shape, minval=math.log(0.5), maxval=math.log(2.0)))
    fast_time = jax.random.uniform(random_keys[2], rate_shape, minval=30.0, maxval=50.0)
    pulse_rates = jnp.exp(-1.0 / jnp.where(slow, slow_time, fast_time))
    pulse_location = jax.random.uniform(random_keys[3], (pulse_length,)) < 3.0 / pulse_length
    pulse_threshold = jax.random.uniform(random_keys[4], (pulse_length,), minval=0.5, maxval=0.8)
    pulse_events = jnp.where(pulse_location, pulse_threshold, 1.0).reshape(pulse_profile)
    pulse_rates = pulse_rates * pulse_events
    raw = jax.random.uniform(random_keys[5], (5, 5, SPAN, NORMAL_CELLS, CHORD_CELLS), minval=-0.1, maxval=0.1)
    skew = raw - jnp.swapaxes(raw, 0, 1)
    frobenius = jnp.sum(skew * skew, axis=(0, 1))
    shrink = 1.0 / jnp.sqrt(1.0 + frobenius / 5.0)
    eye = jnp.eye(5, dtype=jnp.float32).reshape(5, 5, 1, 1, 1)
    blocks = pulse_rates[:, None] * (eye + skew) * shrink[None, None]
    return blocks.astype(jnp.float32)


def draw_xi_lower(key, part):
    return chain_blocks(jax.random.fold_in(key, 11), CHORD_CELLS, 4)


def draw_xi_upper(key, part):
    return chain_blocks(jax.random.fold_in(key, 12), CHORD_CELLS, 4)


def draw_eta_lower(key, part):
    return chain_blocks(jax.random.fold_in(key, 13), NORMAL_CELLS, 3)


def draw_eta_upper(key, part):
    return chain_blocks(jax.random.fold_in(key, 14), NORMAL_CELLS, 3)


def with_ends(values, stream_key, least, top_value):
    index_at = [jax.random.randint(jax.random.fold_in(stream_key, axis), (), 0, length) for axis, length in enumerate(values.shape)]
    widest = values.shape.index(max(values.shape))
    neighbour = index_at[:widest] + [(index_at[widest] + 1) % values.shape[widest]] + index_at[widest + 1:]
    return values.at[tuple(index_at)].set(least).at[tuple(neighbour)].set(top_value)


def block_scale(rng, shape, cuts, least, top_value):
    def one(position, parts):
        draws = jax.random.uniform(jax.random.fold_in(jax.random.fold_in(rng, 6), position), (parts,), jnp.float32, least / len(cuts), top_value / len(cuts))
        return jnp.repeat(jnp.exp(draws), shape[position] // parts).reshape((-1,) + (1,) * (len(shape) - position - 1))

    gain = one(*cuts[0])
    for cut in cuts[1:]:
        gain = gain * one(*cut)
    return gain


def bell_draw(rng, dims, scale, bound, pieces=(), kind=jnp.bfloat16):
    values = jax.random.normal(rng, dims, jnp.float32) * scale
    if len(pieces) > 0:
        values = block_scale(rng, dims, pieces, -0.22, 0.18) * values
    return jnp.clip(values, min=-bound, max=bound).astype(kind)


def setup_inputs(seed: int = 0) -> dict:
    splits = jax.random.split(jax.random.key(seed), 10)
    return {
        "rhs": bell_draw(splits[0], (COMP, SPAN, NORMAL_CELLS, CHORD_CELLS), 0.05, 0.3, ((2, 32), (3, 16)), jnp.float32),
        "jet_mask": with_ends((jax.random.randint(splits[1], (SPAN, NORMAL_CELLS, CHORD_CELLS), 0, 4) < 1).astype(jnp.int32), jax.random.fold_in(splits[1], 1), 0, 1),
        "jet_source": bell_draw(splits[2], (COMP,), 0.05, 0.3, (), jnp.float32),
        "wall_flags": with_ends(jax.random.randint(splits[3], (SPAN, CHORD_CELLS), 0, 3), jax.random.fold_in(splits[3], 1), 0, 2).astype(jnp.int32),
        "bc_table": jnp.clip(jax.random.uniform(splits[4], (FLAGS, COMP), jnp.float32, 0.2, 1.5), 0.2, 1.5),
        "xi_lower": draw_xi_lower(jax.random.fold_in(splits[9], 71), 0),
        "xi_upper": draw_xi_upper(jax.random.fold_in(splits[9], 71), 0),
        "eta_lower": draw_eta_lower(jax.random.fold_in(splits[9], 71), 0),
        "eta_upper": draw_eta_upper(jax.random.fold_in(splits[9], 71), 0),
    }


def run_chain(blocks, values, block_axis, reverse):
    value_axis = block_axis - 1
    blocks_first = jnp.moveaxis(blocks, block_axis, 0)
    values_first = jnp.moveaxis(values, value_axis, 0)

    def advance(carry, item):
        block, value = item
        fresh = jnp.einsum("ab...,b...->a...", block, carry, precision=lax.Precision.HIGHEST) + value
        return fresh, fresh

    start = jnp.zeros(values_first.shape[1:], jnp.float32)
    _, states = lax.scan(advance, start, (blocks_first, values_first), reverse=reverse)
    return jnp.moveaxis(states, 0, value_axis)


def reference(rhs, jet_mask, jet_source, wall_flags, bc_table, xi_lower, xi_upper, eta_lower, eta_upper):
    source = rhs + jet_mask.astype(jnp.float32)[None] * jet_source[:, None, None, None]
    ahead = run_chain(xi_lower, source, 4, False)
    behind = run_chain(xi_upper, ahead, 4, True)
    onehot = (wall_flags[None] == jnp.arange(FLAGS, dtype=jnp.int32)[:, None, None]).astype(jnp.float32)
    factor = jnp.einsum("fa,fki->aki", bc_table, onehot, precision=lax.Precision.HIGHEST)
    first_row = jnp.arange(NORMAL_CELLS, dtype=jnp.int32) == 0
    scaled = jnp.where(first_row[None, None, :, None], factor[:, :, None, :], jnp.float32(1.0)) * behind
    lifted = run_chain(eta_lower, scaled, 3, False)
    return run_chain(eta_upper, lifted, 3, True)
```

```python
import jax
import jax.numpy as jnp
from jax import lax
from jax.experimental import pallas as pl
from jax.experimental.pallas import tpu as pltpu
from jax.sharding import PartitionSpec as P

F32 = jnp.float32
N = 5
ROWS = 48
VEC = 40
ANY = pl.BlockSpec(memory_space=pl.ANY)
HBM = pl.BlockSpec(memory_space=pltpu.HBM)
VM = pl.BlockSpec(memory_space=pltpu.VMEM)
SM = pl.BlockSpec(memory_space=pltpu.SMEM)
LIMIT = 32 << 20
WIDE = 60 << 20
LEAF = 220
STORE = LEAF + 510


def shape(*dims):
    return jax.ShapeDtypeStruct(dims, F32)


def params(limit=LIMIT):
    return pltpu.CompilerParams(vmem_limit_bytes=limit)


def cost(flops, nbytes):
    return pl.CostEstimate(flops=flops, bytes_accessed=nbytes, transcendentals=0)


def square(flat):
    return [[flat[N * i + j] for j in range(N)] for i in range(N)]


def flat(m):
    return [x for row in m for x in row]


def dot(xs, ys, start=None):
    total = start
    for x, y in zip(xs, ys):
        total = x * y if total is None else total + x * y
    return total


def mm(a, b, c=None):
    cols = list(zip(*b))
    return [
        [dot(a[i], cols[j], None if c is None else c[i][j]) for j in range(N)] for i in range(N)
    ]


def mv(a, x, c=None):
    return [dot(a[i], x, None if c is None else c[i]) for i in range(N)]


def lane_iota():
    return lax.broadcasted_iota(jnp.int32, (8, 128), 1)


def roll(x, by):
    return pltpu.roll(x, by % 128, 1)


def place():
    wall = lax.axis_index("wall")
    return lax.axis_index("chord"), wall // 2, wall % 2


def copy_all(copies):
    for c in copies:
        c.start()
    for c in copies:
        c.wait()


def pack_kernel(jet, rhs, mask, xl, xu, el, eu, send, src, rv, mk, out, own, sem):
    _, _, core = place()
    off = pl.multiple_of((1 - core) * 16, 16)
    first = [pltpu.make_async_copy(rhs, rv, sem.at[5]), pltpu.make_async_copy(mask, mk, sem.at[6])]
    copies = [
        pltpu.make_async_copy(ref.at[:, pl.ds(off, 16), :], send.at[pl.ds(25 * n, 25)], sem.at[n])
        for n, ref in enumerate((xl, xu, el, eu))
    ]
    for c in first + copies:
        c.start()
    for c in first:
        c.wait()
    keep = pl.multiple_of(core * 16, 16)
    for dst, at in ((out, off), (own, keep)):
        m = mk[pl.ds(at, 16), :].astype(F32)
        for c in range(N):
            dst[c] = rv[c, pl.ds(at, 16), :] + m * jet[c]
    copies.append(pltpu.make_async_copy(out, send.at[pl.ds(100, N)], sem.at[4]))
    copies.append(pltpu.make_async_copy(own, src, sem.at[7]))
    for c in copies[4:]:
        c.start()
    for c in copies:
        c.wait()


def compose(left, right):
    lb1, lv1, ub1, uv1, w1 = left
    lb2, lv2, ub2, uv2, w2 = right
    lb = mm(lb2, lb1)
    lv = mv(lb2, lv1, lv2)
    ub = mm(ub1, ub2)
    uv = mv(ub1, mv(w2, lv1, uv2), uv1)
    w = mm(ub1, mm(w2, lb1), w1)
    return lb, lv, ub, uv, w


def node(values):
    return (
        square(values[0:25]),
        list(values[25:30]),
        square(values[30:55]),
        list(values[55:60]),
        square(values[60:85]),
    )


def values_of(n):
    return flat(n[0]) + list(n[1]) + flat(n[2]) + list(n[3]) + flat(n[4])


def up_kernel(src, xl, xu, recv, msg, store, sl, su, ss, n1, n2, leaf, tree, sem):
    _, _, core = place()
    off = pl.multiple_of(core * 16, 16)
    copies = [
        pltpu.make_async_copy(xl.at[:, pl.ds(off, 16), :], sl.at[:, core], sem.at[0]),
        pltpu.make_async_copy(xu.at[:, pl.ds(off, 16), :], su.at[:, core], sem.at[1]),
        pltpu.make_async_copy(recv.at[pl.ds(0, 25)], sl.at[:, 1 - core], sem.at[2]),
        pltpu.make_async_copy(recv.at[pl.ds(25, 25)], su.at[:, 1 - core], sem.at[3]),
        pltpu.make_async_copy(recv.at[pl.ds(100, N)], ss.at[:, 1 - core], sem.at[4]),
        pltpu.make_async_copy(src, ss.at[:, core], sem.at[13]),
    ]
    copy_all(copies)
    lane = lane_iota()
    even = lane % 2 == 0
    low = (lane // 2) % 2 == 0

    def split(ref, c, r):
        a = ref[c, r, 0:8, :]
        b = ref[c, r, 8:16, :]
        return jnp.where(even, a, roll(b, 1)), jnp.where(even, roll(a, -1), b)

    saves = []
    for r in range(2):
        l1, l2 = zip(*[split(sl, c, r) for c in range(25)])
        v1, v2 = zip(*[split(ss, c, r) for c in range(N)])
        u1, u2 = zip(*[split(su, c, r) for c in range(25)])
        for c, x in enumerate(l1 + v1 + l2 + v2 + u1 + u2):
            leaf[r, c] = x
        dst = store.at[pl.ds(110 * r, 110)]
        saves.append(pltpu.make_async_copy(leaf.at[r], dst, sem.at[5 + r]))
        saves[-1].start()
        l1, l2, u1, u2 = square(l1), square(l2), square(u1), square(u2)
        lb = mm(l2, l1)
        lv = mv(l2, v1, v2)
        out = (lb, lv, mm(u1, u2), mv(u1, lv, v1), mm(u1, lb, l1))
        for c, x in enumerate(values_of(out)):
            n1[r, c] = x

    left, right = [], []
    for c in range(85):
        a, b = n1[0, c], n1[1, c]
        left.append(jnp.where(low, a, roll(b, 2)))
        right.append(jnp.where(low, roll(a, -2), b))
    for level in range(6):
        if level:
            left = [n2[c] for c in range(85)]
            right = [roll(x, -(2 << level)) for x in left]
        for c in range(30):
            tree[level, c] = left[c]
        for c in range(30, 85):
            tree[level, c] = right[c]
        dst = store.at[pl.ds(LEAF + 85 * level, 85)]
        saves.append(pltpu.make_async_copy(tree.at[level], dst, sem.at[7 + level]))
        saves[-1].start()
        for c, x in enumerate(values_of(compose(node(left), node(right)))):
            n2[c] = x
    group = lane // 4
    for g in range(3):
        acc = None
        for pos in range(min(32, 85 - 32 * g)):
            x = n2[32 * g + pos]
            acc = x if acc is None else jnp.where(group == pos, roll(x, 4 * pos), acc)
        for d in range(16):
            msg[d, 8 * g : 8 * g + 8, :] = acc
    for c in saves:
        c.wait()


def eta_copies(el, eu, recv, sl, su, core, sem):
    off = pl.multiple_of(core * 16, 16)
    return [
        pltpu.make_async_copy(el.at[:, pl.ds(off, 16), :], sl.at[:, core], sem.at[0]),
        pltpu.make_async_copy(eu.at[:, pl.ds(off, 16), :], su.at[:, core], sem.at[1]),
        pltpu.make_async_copy(recv.at[pl.ds(50, 25)], sl.at[:, 1 - core], sem.at[2]),
        pltpu.make_async_copy(recv.at[pl.ds(75, 25)], su.at[:, 1 - core], sem.at[3]),
    ]


def cell(ref, j):
    return square([ref[c, j // 2, pl.ds(j % 2, 8, stride=2), :] for c in range(25)])


def halves(x, y, first):
    return jnp.where(first, x, roll(y, 64)), jnp.where(first, roll(x, 64), y)


def wall_kernel(el, eu, recv, out, sl, su, sem):
    _, _, core = place()
    copy_all(eta_copies(el, eu, recv, sl, su, core, sem))
    first = lane_iota() < 64
    lb = cell(sl, 0)
    w = lb
    ub = cell(su, 0)
    for j in range(1, 4):
        lb = mm(cell(sl, j), lb)
        w = mm(ub, lb, w)
        ub = mm(ub, cell(su, j))
    values = flat(lb) + flat(ub) + flat(w)
    for r in range(38):
        a, b = halves(values[r], values[r + 37], first)
        out[pl.ds(r, 8, stride=ROWS), :] = a
        out[pl.ds(8 * ROWS + r, 8, stride=ROWS), :] = b


def down_kernel(
    table, flags, got, store, el, eu, recv, zin, scaled, zout,
    sl, su, lf, tr, cs, bh, vb, fl, sem,
):
    chord, z, core = place()
    eta = eta_copies(el, eu, recv, sl, su, core, sem)
    pre = [
        pltpu.make_async_copy(store.at[pl.ds(LEAF, 510)], tr, sem.at[4]),
        pltpu.make_async_copy(store.at[pl.ds(0, LEAF)], lf, sem.at[5]),
    ]
    kinds = pltpu.make_async_copy(flags, fl, sem.at[22])
    kinds.start()
    for c in pre + eta:
        c.start()
    lane = lane_iota()
    group = lane // 4
    for g in range(3):
        v = [got[s, 8 * g : 8 * g + 8, :] for s in range(16)]
        for bit in range(4):
            step = 1 << bit
            keep = (group // step) % 2 == 0
            fresh = list(v)
            for s in range(16):
                if s & step:
                    continue
                a, b = v[s], v[s | step]
                fresh[s] = jnp.where(keep, a, roll(b, 4 * step))
                fresh[s | step] = jnp.where(keep, roll(a, -4 * step), b)
            v = fresh
        for lo in range(16):
            if 32 * g + lo < 85:
                cs[32 * g + lo] = v[lo]
            if 32 * g + 16 + lo < 85:
                cs[32 * g + 16 + lo] = roll(v[lo], 64)

    def chain(m, t, sign):
        for bit in range(4):
            step = 1 << bit
            ok = group >= step if sign > 0 else group < 16 - step
            far = [roll(x, sign * 4 * step) for x in t]
            t = [jnp.where(ok, new, old) for new, old in zip(mv(m, far, t), t)]
            if bit < 3:
                fm = [[roll(x, sign * 4 * step) for x in row] for row in m]
                new = mm(m, fm)
                m = [[jnp.where(ok, new[i][j], m[i][j]) for j in range(N)] for i in range(N)]
        return t

    zero = jnp.zeros((8, 128), F32)
    t = chain(square([cs[c] for c in range(25)]), [cs[25 + c] for c in range(N)], 1)
    a = [jnp.where(group >= 1, roll(x, 4), zero) for x in t]
    f = mv(square([cs[60 + c] for c in range(25)]), a, [cs[55 + c] for c in range(N)])
    t = chain(square([cs[30 + c] for c in range(25)]), f, -1)
    b = [jnp.where(group < 15, roll(x, -4), zero) for x in t]
    back = (128 - 4 * chord) % 128
    a = [pltpu.roll(x, back, 1) for x in a]
    b = [pltpu.roll(x, back, 1) for x in b]

    pre[0].wait()
    for level in range(5, -1, -1):
        dist = 2 << level
        a_mid = mv(square([tr[85 * level + c] for c in range(25)]), a, [tr[85 * level + 25 + c] for c in range(N)])
        b_mid = mv(square([tr[85 * level + 30 + c] for c in range(25)]), b, [tr[85 * level + 55 + c] for c in range(N)])
        b_mid = mv(square([tr[85 * level + 60 + c] for c in range(25)]), a_mid, b_mid)
        left = (lane // dist) % 2 == 0
        if level:
            a = [jnp.where(left, x, roll(y, dist)) for x, y in zip(a, a_mid)]
            b = [jnp.where(left, x, roll(y, dist)) for x, y in zip(b_mid, b)]
    pre[1].wait()
    even = lane % 2 == 0
    for r in range(2):
        if r == 0:
            ra = [jnp.where(left, x, roll(y, 2)) for x, y in zip(a, a_mid)]
            rb = [jnp.where(left, x, roll(y, 2)) for x, y in zip(b_mid, b)]
        else:
            ra = [jnp.where(left, roll(x, -2), y) for x, y in zip(a, a_mid)]
            rb = [jnp.where(left, roll(x, -2), y) for x, y in zip(b_mid, b)]

        def part(first, count):
            return [lf[110 * r + first + c] for c in range(count)]

        a1 = mv(square(part(0, 25)), ra, part(25, N))
        a2 = mv(square(part(30, 25)), a1, part(55, N))
        b2 = mv(square(part(85, 25)), rb, a2)
        b1 = mv(square(part(60, 25)), b2, a1)
        for c in range(N):
            bh[c, r, 0:8, :] = jnp.where(even, b1[c], roll(b2[c], 1))
            bh[c, r, 8:16, :] = jnp.where(even, roll(b1[c], -1), b2[c])

    kinds.wait()
    kind = fl[pl.ds(pl.multiple_of(core * 8, 8), 8), :]
    s = []
    for j in range(4):
        s.append([bh[c, j // 2, pl.ds(j % 2, 8, stride=2), :] for c in range(N)])
    for c in range(N):
        factor = zero
        for k in range(3):
            factor = jnp.where(kind == k, table[k, c], factor)
        s[0][c] = jnp.where(z == 0, factor, 1.0) * s[0][c]
    for j in range(4):
        for c in range(N):
            scaled[j, c] = s[j][c]
    for c in eta:
        c.wait()
    t = [s[0]]
    for j in range(1, 4):
        t.append(mv(cell(sl, j), t[-1], s[j]))
    u = t[3]
    for j in range(2, -1, -1):
        u = mv(cell(su, j), u, t[j])
    first = lane < 64
    for c in range(N):
        x, y = halves(t[3][c], u[c], first)
        vb[pl.ds(c, 8, stride=8), :] = x
        vb[pl.ds(64 + c, 8, stride=8), :] = y
    for c in range(N, 8):
        vb[pl.ds(c, 8, stride=8), :] = zero
        vb[pl.ds(64 + c, 8, stride=8), :] = zero
    copy_all([
        pltpu.make_async_copy(
            vb.at[pl.ds(8 * d, 8)], zout.at[pl.ds(ROWS * d + VEC, 8)], sem.at[6 + d]
        )
        for d in range(16)
    ])


def solve_kernel(got, back, turned, ain):
    for n in range(16 * ROWS // 8):
        turned[8 * n : 8 * n + 8, :] = pltpu.roll(got[8 * n : 8 * n + 8, :], 64, 1)

    def value(z, c):
        ref = got if c < 37 else turned
        row = ROWS * z + (c if c < 37 else c - 37)
        return ref[row : row + 1, :]

    def block(z, first):
        return square([value(z, first + c) for c in range(25)])

    def vec(z, ref):
        return [ref[ROWS * z + VEC + c : ROWS * z + VEC + c + 1, :] for c in range(N)]

    zero = jnp.zeros((1, 128), F32)
    for n in range(16):
        back[8 * n : 8 * n + 8, :] = jnp.zeros((8, 128), F32)
    a = [zero] * N
    for z in range(16):
        for c in range(N):
            ain[8 * z + c : 8 * z + c + 1, :] = a[c]
        if z < 15:
            a = mv(block(z, 0), a, vec(z, got)) if z else vec(z, got)
    first = lax.broadcasted_iota(jnp.int32, (1, 128), 1) < 64
    b = [zero] * N
    for z in range(15, -1, -1):
        a = [ain[8 * z + c : 8 * z + c + 1, :] for c in range(N)]
        for c in range(N):
            back[8 * z + c : 8 * z + c + 1, :] = jnp.where(first, a[c], pltpu.roll(b[c], 64, 1))
        if z:
            f = mv(block(z, 50), a, vec(z, turned))
            b = mv(block(z, 25), b, f)


def finish_kernel(got, scaled, el, eu, recv, own, send, sl, su, res, sem):
    _, _, core = place()
    copies = eta_copies(el, eu, recv, sl, su, core, sem)
    for c in copies:
        c.start()
    first = lane_iota() < 64
    a, b = [], []
    for c in range(N):
        x = got[pl.ds(c, 8, stride=8), :]
        y = got[pl.ds(64 + c, 8, stride=8), :]
        a.append(jnp.where(first, x, roll(y, 64)))
        b.append(jnp.where(first, roll(x, 64), y))
    for c in copies:
        c.wait()
    lifted = []
    for j in range(4):
        a = mv(cell(sl, j), a, [scaled[j, c] for c in range(N)])
        lifted.append(a)
    for j in range(3, -1, -1):
        b = mv(cell(su, j), b, lifted[j])
        for c in range(N):
            res[c, j // 2, pl.ds(j % 2, 8, stride=2), :] = b[c]
    for c in range(N):
        own[c] = res[c, core]
        send[c] = res[c, 1 - core]


def dma(n):
    return pltpu.SemaphoreType.DMA((n,))


def per_device(
    rhs, jet_mask, jet_source, wall_flags, bc_table, xi_lower, xi_upper, eta_lower, eta_upper
):
    def far(x, *dims):
        return pltpu.with_memory_space_constraint(x.reshape(dims), pltpu.HBM)

    rhs, mask, flags = far(rhs, N, 32, 128), far(jet_mask, 32, 128), far(wall_flags, 16, 128)
    xl, xu, el, eu = (far(x, 25, 32, 128) for x in (xi_lower, xi_upper, eta_lower, eta_upper))
    swap = [(n, n ^ 1) for n in range(lax.axis_size("wall"))]
    groups = [list(range(c, lax.axis_size("wall"), 2)) for c in range(2)]

    def over_z(x):
        return lax.all_to_all(x, "wall", 0, 0, tiled=True, axis_index_groups=groups)

    side = pltpu.VMEM((25, 2, 16, 128), F32)
    send, src = pl.pallas_call(
        pack_kernel,
        out_shape=(shape(105, 16, 128), pltpu.HBM((N, 16, 128), F32)),
        in_specs=[SM] + [HBM] * 6,
        out_specs=(ANY, HBM),
        scratch_shapes=[
            pltpu.VMEM((N, 32, 128), F32),
            pltpu.VMEM((32, 128), jnp.int32),
            pltpu.VMEM((N, 16, 128), F32),
            pltpu.VMEM((N, 16, 128), F32),
            dma(8),
        ],
        compiler_params=params(WIDE),
        name="pack",
    )(jet_source, rhs, mask, xl, xu, el, eu)
    recv = lax.ppermute(send, "wall", swap)
    msg, store = pl.pallas_call(
        up_kernel,
        out_shape=(shape(16, 24, 128), pltpu.HBM((STORE, 8, 128), F32)),
        in_specs=[HBM, HBM, HBM, ANY],
        out_specs=(VM, HBM),
        scratch_shapes=[
            side,
            side,
            pltpu.VMEM((N, 2, 16, 128), F32),
            pltpu.VMEM((2, 85, 8, 128), F32),
            pltpu.VMEM((85, 8, 128), F32),
            pltpu.VMEM((2, 110, 8, 128), F32),
            pltpu.VMEM((6, 85, 8, 128), F32),
            dma(14),
        ],
        compiler_params=params(),
        name="chord_up",
    )(far(src, N, 16, 128), xl, xu, recv)
    zmat = pl.pallas_call(
        wall_kernel,
        out_shape=shape(16 * ROWS, 128),
        in_specs=[HBM, HBM, ANY],
        out_specs=VM,
        scratch_shapes=[side, side, dma(4)],
        compiler_params=params(),
        cost_estimate=cost(3 * 250 * 3 * 1024, 2 << 20),
        name="wall_blocks",
    )(el, eu, recv)
    got = lax.all_to_all(msg, "chord", 0, 0, tiled=True)
    scaled, zmsg = pl.pallas_call(
        down_kernel,
        out_shape=(shape(4, N, 8, 128), shape(16 * ROWS, 128)),
        in_specs=[SM, HBM, VM, HBM, HBM, HBM, ANY, ANY],
        out_specs=(VM, ANY),
        scratch_shapes=[
            side,
            side,
            pltpu.VMEM((LEAF, 8, 128), F32),
            pltpu.VMEM((510, 8, 128), F32),
            pltpu.VMEM((85, 8, 128), F32),
            pltpu.VMEM((N, 2, 16, 128), F32),
            pltpu.VMEM((128, 128), F32),
            pltpu.VMEM((16, 128), jnp.int32),
            dma(23),
        ],
        input_output_aliases={7: 1},
        compiler_params=params(),
        name="chord_down",
    )(bc_table, flags, got, far(store, STORE, 8, 128), el, eu, recv, zmat)
    zgot = over_z(zmsg.reshape(16, ROWS, 128)).reshape(16 * ROWS, 128)
    back = pl.pallas_call(
        solve_kernel,
        out_shape=shape(128, 128),
        in_specs=[VM],
        out_specs=VM,
        scratch_shapes=[pltpu.VMEM((16 * ROWS, 128), F32), pltpu.VMEM((128, 128), F32)],
        compiler_params=params(),
        name="wall_solve",
    )(zgot)
    inflow = over_z(back.reshape(16, 8, 128)).reshape(128, 128)
    own, other = pl.pallas_call(
        finish_kernel,
        out_shape=(shape(N, 16, 128), shape(N, 16, 128)),
        in_specs=[VM, VM, HBM, HBM, ANY],
        out_specs=(VM, VM),
        scratch_shapes=[side, side, pltpu.VMEM((N, 2, 16, 128), F32), dma(4)],
        compiler_params=params(),
        name="finish",
    )(inflow, scaled, el, eu, recv)
    other = lax.ppermute(other, "wall", swap)
    core = lax.axis_index("wall") % 2
    low = jnp.where(core == 0, own, other)
    high = jnp.where(core == 0, other, own)
    return jnp.concatenate([low, high], axis=1).reshape(N, 16, 2, 128)


def solution(mesh):
    placed = (
        P(None, None, "wall", "chord"),
        P(None, "wall", "chord"),
        P(),
        P(None, "chord"),
        P(),
        P(None, None, None, "wall", "chord"),
        P(None, None, None, "wall", "chord"),
        P(None, None, None, "wall", "chord"),
        P(None, None, None, "wall", "chord"),
    )
    return jax.shard_map(
        per_device,
        mesh=mesh,
        in_specs=placed,
        out_specs=P(None, None, "wall", "chord"),
        check_vma=False,
    )
```

```python
import jax
import jax.numpy as jnp
from jax import lax
from jax.experimental import pallas as pl
from jax.experimental.pallas import tpu as pltpu
from jax.sharding import PartitionSpec as P

F32 = jnp.float32
N = 5
ROWS = 48
VEC = 40
ANY = pl.BlockSpec(memory_space=pl.ANY)
HBM = pl.BlockSpec(memory_space=pltpu.HBM)
VM = pl.BlockSpec(memory_space=pltpu.VMEM)
SM = pl.BlockSpec(memory_space=pltpu.SMEM)
LIMIT = 32 << 20
LEAF = 220
STORE = LEAF + 510


def shape(*dims):
    return jax.ShapeDtypeStruct(dims, F32)


def params(limit=LIMIT):
    return pltpu.CompilerParams(vmem_limit_bytes=limit)


def cost(flops, nbytes):
    return pl.CostEstimate(flops=flops, bytes_accessed=nbytes, transcendentals=0)


def square(flat):
    return [[flat[N * i + j] for j in range(N)] for i in range(N)]


def flat(m):
    return [x for row in m for x in row]


def dot(xs, ys, start=None):
    total = start
    for x, y in zip(xs, ys):
        total = x * y if total is None else total + x * y
    return total


def mm(a, b, c=None):
    cols = list(zip(*b))
    return [
        [dot(a[i], cols[j], None if c is None else c[i][j]) for j in range(N)] for i in range(N)
    ]


def mv(a, x, c=None):
    return [dot(a[i], x, None if c is None else c[i]) for i in range(N)]


def lane_iota():
    return lax.broadcasted_iota(jnp.int32, (8, 128), 1)


def roll(x, by):
    return pltpu.roll(x, by % 128, 1)


def place():
    wall = lax.axis_index("wall")
    return lax.axis_index("chord"), wall // 2, wall % 2


def copy_all(copies):
    for c in copies:
        c.start()
    for c in copies:
        c.wait()


def pack_kernel(jet, rhs, mask, xl, xu, el, eu, send, keep, rv, mk, sem):
    _, _, core = place()
    copies = [pltpu.make_async_copy(rhs, rv, sem.at[8]), pltpu.make_async_copy(mask, mk, sem.at[9])]
    halves = ((send, pl.multiple_of((1 - core) * 16, 16)), (keep, pl.multiple_of(core * 16, 16)))
    for m, (dst, off) in enumerate(halves):
        for n, ref in enumerate((xl, xu, el, eu)):
            copies.append(
                pltpu.make_async_copy(
                    ref.at[:, pl.ds(off, 16), :], dst.at[pl.ds(25 * n, 25)], sem.at[4 * m + n]
                )
            )
    for c in copies:
        c.start()
    copies[0].wait()
    copies[1].wait()
    for dst, off in halves:
        m = mk[pl.ds(off, 16), :].astype(F32)
        for c in range(N):
            dst[100 + c] = rv[c, pl.ds(off, 16), :] + m * jet[c]
    for c in copies[2:]:
        c.wait()


def compose(left, right):
    lb1, lv1, ub1, uv1, w1 = left
    lb2, lv2, ub2, uv2, w2 = right
    lb = mm(lb2, lb1)
    lv = mv(lb2, lv1, lv2)
    ub = mm(ub1, ub2)
    uv = mv(ub1, mv(w2, lv1, uv2), uv1)
    w = mm(ub1, mm(w2, lb1), w1)
    return lb, lv, ub, uv, w


def node(values):
    return (
        square(values[0:25]),
        list(values[25:30]),
        square(values[30:55]),
        list(values[55:60]),
        square(values[60:85]),
    )


def values_of(n):
    return flat(n[0]) + list(n[1]) + flat(n[2]) + list(n[3]) + flat(n[4])


def up_kernel(keep, recv, msg, store, sl, su, ss, n1, n2, leaf, tree, sem):
    _, _, core = place()
    copies = []
    for n, (dst, first, count) in enumerate(((sl, 0, 25), (su, 25, 25), (ss, 100, N))):
        part = pl.ds(first, count)
        copies.append(pltpu.make_async_copy(keep.at[part], dst.at[:, core], sem.at[2 * n]))
        copies.append(pltpu.make_async_copy(recv.at[part], dst.at[:, 1 - core], sem.at[2 * n + 1]))
    copy_all(copies)
    lane = lane_iota()
    even = lane % 2 == 0
    low = (lane // 2) % 2 == 0

    def split(ref, c, r):
        a = ref[c, r, 0:8, :]
        b = ref[c, r, 8:16, :]
        return jnp.where(even, a, roll(b, 1)), jnp.where(even, roll(a, -1), b)

    saves = []
    for r in range(2):
        l1, l2 = zip(*[split(sl, c, r) for c in range(25)])
        v1, v2 = zip(*[split(ss, c, r) for c in range(N)])
        u1, u2 = zip(*[split(su, c, r) for c in range(25)])
        for c, x in enumerate(l1 + v1 + l2 + v2 + u1 + u2):
            leaf[r, c] = x
        dst = store.at[pl.ds(110 * r, 110)]
        saves.append(pltpu.make_async_copy(leaf.at[r], dst, sem.at[6 + r]))
        saves[-1].start()
        l1, l2, u1, u2 = square(l1), square(l2), square(u1), square(u2)
        lb = mm(l2, l1)
        lv = mv(l2, v1, v2)
        out = (lb, lv, mm(u1, u2), mv(u1, lv, v1), mm(u1, lb, l1))
        for c, x in enumerate(values_of(out)):
            n1[r, c] = x

    left, right = [], []
    for c in range(85):
        a, b = n1[0, c], n1[1, c]
        left.append(jnp.where(low, a, roll(b, 2)))
        right.append(jnp.where(low, roll(a, -2), b))
    for level in range(6):
        if level:
            left = [n2[c] for c in range(85)]
            right = [roll(x, -(2 << level)) for x in left]
        for c in range(30):
            tree[level, c] = left[c]
        for c in range(30, 85):
            tree[level, c] = right[c]
        dst = store.at[pl.ds(LEAF + 85 * level, 85)]
        saves.append(pltpu.make_async_copy(tree.at[level], dst, sem.at[8 + level]))
        saves[-1].start()
        for c, x in enumerate(values_of(compose(node(left), node(right)))):
            n2[c] = x
    group = lane // 4
    for g in range(3):
        acc = None
        for pos in range(min(32, 85 - 32 * g)):
            x = n2[32 * g + pos]
            acc = x if acc is None else jnp.where(group == pos, roll(x, 4 * pos), acc)
        for d in range(16):
            msg[d, 8 * g : 8 * g + 8, :] = acc
    for c in saves:
        c.wait()


def eta_copies(keep, recv, sl, su, core, sem):
    return [
        pltpu.make_async_copy(keep.at[pl.ds(50, 25)], sl.at[:, core], sem.at[0]),
        pltpu.make_async_copy(keep.at[pl.ds(75, 25)], su.at[:, core], sem.at[1]),
        pltpu.make_async_copy(recv.at[pl.ds(50, 25)], sl.at[:, 1 - core], sem.at[2]),
        pltpu.make_async_copy(recv.at[pl.ds(75, 25)], su.at[:, 1 - core], sem.at[3]),
    ]


def cell(ref, j):
    return square([ref[c, j // 2, pl.ds(j % 2, 8, stride=2), :] for c in range(25)])


def halves(x, y, first):
    return jnp.where(first, x, roll(y, 64)), jnp.where(first, roll(x, 64), y)


def wall_kernel(keep, recv, out, sl, su, sem):
    _, _, core = place()
    copy_all(eta_copies(keep, recv, sl, su, core, sem))
    first = lane_iota() < 64
    lb = cell(sl, 0)
    w = lb
    ub = cell(su, 0)
    for j in range(1, 4):
        lb = mm(cell(sl, j), lb)
        w = mm(ub, lb, w)
        ub = mm(ub, cell(su, j))
    values = flat(lb) + flat(ub) + flat(w)
    for r in range(38):
        a, b = halves(values[r], values[r + 37], first)
        out[pl.ds(r, 8, stride=ROWS), :] = a
        out[pl.ds(8 * ROWS + r, 8, stride=ROWS), :] = b


def down_kernel(
    table, flags, got, store, keep, recv, zin, scaled, zout,
    sl, su, lf, tr, cs, bh, vb, fl, sem,
):
    chord, z, core = place()
    eta = eta_copies(keep, recv, sl, su, core, sem)
    pre = [
        pltpu.make_async_copy(store.at[pl.ds(LEAF, 510)], tr, sem.at[4]),
        pltpu.make_async_copy(store.at[pl.ds(0, LEAF)], lf, sem.at[5]),
    ]
    kinds = pltpu.make_async_copy(flags, fl, sem.at[22])
    kinds.start()
    for c in pre + eta:
        c.start()
    lane = lane_iota()
    group = lane // 4
    for g in range(3):
        v = [got[s, 8 * g : 8 * g + 8, :] for s in range(16)]
        for bit in range(4):
            step = 1 << bit
            same = (group // step) % 2 == 0
            fresh = list(v)
            for s in range(16):
                if s & step:
                    continue
                a, b = v[s], v[s | step]
                fresh[s] = jnp.where(same, a, roll(b, 4 * step))
                fresh[s | step] = jnp.where(same, roll(a, -4 * step), b)
            v = fresh
        for lo in range(16):
            if 32 * g + lo < 85:
                cs[32 * g + lo] = v[lo]
            if 32 * g + 16 + lo < 85:
                cs[32 * g + 16 + lo] = roll(v[lo], 64)

    def chain(m, t, sign):
        for bit in range(4):
            step = 1 << bit
            ok = group >= step if sign > 0 else group < 16 - step
            far = [roll(x, sign * 4 * step) for x in t]
            t = [jnp.where(ok, new, old) for new, old in zip(mv(m, far, t), t)]
            if bit < 3:
                fm = [[roll(x, sign * 4 * step) for x in row] for row in m]
                new = mm(m, fm)
                m = [[jnp.where(ok, new[i][j], m[i][j]) for j in range(N)] for i in range(N)]
        return t

    zero = jnp.zeros((8, 128), F32)
    t = chain(square([cs[c] for c in range(25)]), [cs[25 + c] for c in range(N)], 1)
    a = [jnp.where(group >= 1, roll(x, 4), zero) for x in t]
    f = mv(square([cs[60 + c] for c in range(25)]), a, [cs[55 + c] for c in range(N)])
    t = chain(square([cs[30 + c] for c in range(25)]), f, -1)
    b = [jnp.where(group < 15, roll(x, -4), zero) for x in t]
    back = (128 - 4 * chord) % 128
    a = [pltpu.roll(x, back, 1) for x in a]
    b = [pltpu.roll(x, back, 1) for x in b]

    pre[0].wait()
    for level in range(5, -1, -1):
        dist = 2 << level
        a_mid = mv(square([tr[85 * level + c] for c in range(25)]), a, [tr[85 * level + 25 + c] for c in range(N)])
        b_mid = mv(square([tr[85 * level + 30 + c] for c in range(25)]), b, [tr[85 * level + 55 + c] for c in range(N)])
        b_mid = mv(square([tr[85 * level + 60 + c] for c in range(25)]), a_mid, b_mid)
        left = (lane // dist) % 2 == 0
        if level:
            a = [jnp.where(left, x, roll(y, dist)) for x, y in zip(a, a_mid)]
            b = [jnp.where(left, x, roll(y, dist)) for x, y in zip(b_mid, b)]
    pre[1].wait()
    even = lane % 2 == 0
    for r in range(2):
        if r == 0:
            ra = [jnp.where(left, x, roll(y, 2)) for x, y in zip(a, a_mid)]
            rb = [jnp.where(left, x, roll(y, 2)) for x, y in zip(b_mid, b)]
        else:
            ra = [jnp.where(left, roll(x, -2), y) for x, y in zip(a, a_mid)]
            rb = [jnp.where(left, roll(x, -2), y) for x, y in zip(b_mid, b)]

        def part(first, count):
            return [lf[110 * r + first + c] for c in range(count)]

        a1 = mv(square(part(0, 25)), ra, part(25, N))
        a2 = mv(square(part(30, 25)), a1, part(55, N))
        b2 = mv(square(part(85, 25)), rb, a2)
        b1 = mv(square(part(60, 25)), b2, a1)
        for c in range(N):
            bh[c, r, 0:8, :] = jnp.where(even, b1[c], roll(b2[c], 1))
            bh[c, r, 8:16, :] = jnp.where(even, roll(b1[c], -1), b2[c])

    kinds.wait()
    kind = fl[pl.ds(pl.multiple_of(core * 8, 8), 8), :]
    s = []
    for j in range(4):
        s.append([bh[c, j // 2, pl.ds(j % 2, 8, stride=2), :] for c in range(N)])
    for c in range(N):
        factor = zero
        for k in range(3):
            factor = jnp.where(kind == k, table[k, c], factor)
        s[0][c] = jnp.where(z == 0, factor, 1.0) * s[0][c]
    for j in range(4):
        for c in range(N):
            scaled[j, c] = s[j][c]
    for c in eta:
        c.wait()
    t = [s[0]]
    for j in range(1, 4):
        t.append(mv(cell(sl, j), t[-1], s[j]))
    u = t[3]
    for j in range(2, -1, -1):
        u = mv(cell(su, j), u, t[j])
    first = lane < 64
    for c in range(N):
        x, y = halves(t[3][c], u[c], first)
        vb[pl.ds(c, 8, stride=8), :] = x
        vb[pl.ds(64 + c, 8, stride=8), :] = y
    for c in range(N, 8):
        vb[pl.ds(c, 8, stride=8), :] = zero
        vb[pl.ds(64 + c, 8, stride=8), :] = zero
    copy_all([
        pltpu.make_async_copy(
            vb.at[pl.ds(8 * d, 8)], zout.at[pl.ds(ROWS * d + VEC, 8)], sem.at[6 + d]
        )
        for d in range(16)
    ])


def solve_kernel(got, back, turned, ain):
    for n in range(16 * ROWS // 8):
        turned[8 * n : 8 * n + 8, :] = pltpu.roll(got[8 * n : 8 * n + 8, :], 64, 1)

    def value(z, c):
        ref = got if c < 37 else turned
        row = ROWS * z + (c if c < 37 else c - 37)
        return ref[row : row + 1, :]

    def block(z, first):
        return square([value(z, first + c) for c in range(25)])

    def vec(z, ref):
        return [ref[ROWS * z + VEC + c : ROWS * z + VEC + c + 1, :] for c in range(N)]

    zero = jnp.zeros((1, 128), F32)
    for n in range(16):
        back[8 * n : 8 * n + 8, :] = jnp.zeros((8, 128), F32)
    a = [zero] * N
    for z in range(16):
        for c in range(N):
            ain[8 * z + c : 8 * z + c + 1, :] = a[c]
        if z < 15:
            a = mv(block(z, 0), a, vec(z, got)) if z else vec(z, got)
    first = lax.broadcasted_iota(jnp.int32, (1, 128), 1) < 64
    b = [zero] * N
    for z in range(15, -1, -1):
        a = [ain[8 * z + c : 8 * z + c + 1, :] for c in range(N)]
        for c in range(N):
            back[8 * z + c : 8 * z + c + 1, :] = jnp.where(first, a[c], pltpu.roll(b[c], 64, 1))
        if z:
            f = mv(block(z, 50), a, vec(z, turned))
            b = mv(block(z, 25), b, f)


def finish_kernel(got, scaled, keep, recv, own, send, sl, su, res, sem):
    _, _, core = place()
    copies = eta_copies(keep, recv, sl, su, core, sem)
    for c in copies:
        c.start()
    first = lane_iota() < 64
    a, b = [], []
    for c in range(N):
        x = got[pl.ds(c, 8, stride=8), :]
        y = got[pl.ds(64 + c, 8, stride=8), :]
        a.append(jnp.where(first, x, roll(y, 64)))
        b.append(jnp.where(first, roll(x, 64), y))
    for c in copies:
        c.wait()
    lifted = []
    for j in range(4):
        a = mv(cell(sl, j), a, [scaled[j, c] for c in range(N)])
        lifted.append(a)
    for j in range(3, -1, -1):
        b = mv(cell(su, j), b, lifted[j])
        for c in range(N):
            res[c, j // 2, pl.ds(j % 2, 8, stride=2), :] = b[c]
    for c in range(N):
        own[c] = res[c, core]
        send[c] = res[c, 1 - core]


def dma(n):
    return pltpu.SemaphoreType.DMA((n,))


def per_device(
    rhs, jet_mask, jet_source, wall_flags, bc_table, xi_lower, xi_upper, eta_lower, eta_upper
):
    def far(x, *dims):
        return pltpu.with_memory_space_constraint(x.reshape(dims), pltpu.HBM)

    rhs, mask, flags = far(rhs, N, 32, 128), far(jet_mask, 32, 128), far(wall_flags, 16, 128)
    xl, xu, el, eu = (far(x, 25, 32, 128) for x in (xi_lower, xi_upper, eta_lower, eta_upper))
    swap = [(n, n ^ 1) for n in range(lax.axis_size("wall"))]
    groups = [list(range(c, lax.axis_size("wall"), 2)) for c in range(2)]

    def over_z(x):
        return lax.all_to_all(x, "wall", 0, 0, tiled=True, axis_index_groups=groups)

    side = pltpu.VMEM((25, 2, 16, 128), F32)
    send, keep = pl.pallas_call(
        pack_kernel,
        out_shape=(shape(105, 16, 128), shape(105, 16, 128)),
        in_specs=[SM] + [HBM] * 6,
        out_specs=(VM, VM),
        scratch_shapes=[pltpu.VMEM((N, 32, 128), F32), pltpu.VMEM((32, 128), jnp.int32), dma(10)],
        compiler_params=params(),
        name="pack",
    )(jet_source, rhs, mask, xl, xu, el, eu)
    recv = lax.ppermute(send, "wall", swap)
    msg, store = pl.pallas_call(
        up_kernel,
        out_shape=(shape(16, 24, 128), pltpu.HBM((STORE, 8, 128), F32)),
        in_specs=[ANY, ANY],
        out_specs=(VM, HBM),
        scratch_shapes=[
            side,
            side,
            pltpu.VMEM((N, 2, 16, 128), F32),
            pltpu.VMEM((2, 85, 8, 128), F32),
            pltpu.VMEM((85, 8, 128), F32),
            pltpu.VMEM((2, 110, 8, 128), F32),
            pltpu.VMEM((6, 85, 8, 128), F32),
            dma(14),
        ],
        compiler_params=params(),
        name="chord_up",
    )(keep, recv)
    zmat = pl.pallas_call(
        wall_kernel,
        out_shape=shape(16 * ROWS, 128),
        in_specs=[ANY, ANY],
        out_specs=VM,
        scratch_shapes=[side, side, dma(4)],
        compiler_params=params(),
        cost_estimate=cost(3 * 250 * 3 * 1024, 2 << 20),
        name="wall_blocks",
    )(keep, recv)
    got = lax.all_to_all(msg, "chord", 0, 0, tiled=True)
    scaled, zmsg = pl.pallas_call(
        down_kernel,
        out_shape=(shape(4, N, 8, 128), shape(16 * ROWS, 128)),
        in_specs=[SM, HBM, VM, HBM, ANY, ANY, ANY],
        out_specs=(VM, ANY),
        scratch_shapes=[
            side,
            side,
            pltpu.VMEM((LEAF, 8, 128), F32),
            pltpu.VMEM((510, 8, 128), F32),
            pltpu.VMEM((85, 8, 128), F32),
            pltpu.VMEM((N, 2, 16, 128), F32),
            pltpu.VMEM((128, 128), F32),
            pltpu.VMEM((16, 128), jnp.int32),
            dma(23),
        ],
        input_output_aliases={6: 1},
        compiler_params=params(),
        name="chord_down",
    )(bc_table, flags, got, far(store, STORE, 8, 128), keep, recv, zmat)
    zgot = over_z(zmsg.reshape(16, ROWS, 128)).reshape(16 * ROWS, 128)
    back = pl.pallas_call(
        solve_kernel,
        out_shape=shape(128, 128),
        in_specs=[VM],
        out_specs=VM,
        scratch_shapes=[pltpu.VMEM((16 * ROWS, 128), F32), pltpu.VMEM((128, 128), F32)],
        compiler_params=params(),
        name="wall_solve",
    )(zgot)
    inflow = over_z(back.reshape(16, 8, 128)).reshape(128, 128)
    own, other = pl.pallas_call(
        finish_kernel,
        out_shape=(shape(N, 16, 128), shape(N, 16, 128)),
        in_specs=[VM, VM, ANY, ANY],
        out_specs=(VM, VM),
        scratch_shapes=[side, side, pltpu.VMEM((N, 2, 16, 128), F32), dma(4)],
        compiler_params=params(),
        name="finish",
    )(inflow, scaled, keep, recv)
    other = lax.ppermute(other, "wall", swap)
    core = lax.axis_index("wall") % 2
    low = jnp.where(core == 0, own, other)
    high = jnp.where(core == 0, other, own)
    return jnp.concatenate([low, high], axis=1).reshape(N, 16, 2, 128)


def solution(mesh):
    placed = (
        P(None, None, "wall", "chord"),
        P(None, "wall", "chord"),
        P(),
        P(None, "chord"),
        P(),
        P(None, None, None, "wall", "chord"),
        P(None, None, None, "wall", "chord"),
        P(None, None, None, "wall", "chord"),
        P(None, None, None, "wall", "chord"),
    )
    return jax.shard_map(
        per_device,
        mesh=mesh,
        in_specs=placed,
        out_specs=P(None, None, "wall", "chord"),
        check_vma=False,
    )
```

```python
import jax
import jax.numpy as jnp
from jax import lax
from jax.experimental import pallas as pl
from jax.experimental.pallas import tpu as pltpu
from jax.sharding import PartitionSpec as P

F32 = jnp.float32
N = 5
ROWS = 24
VEC = 19
ANY = pl.BlockSpec(memory_space=pl.ANY)
HBM = pl.BlockSpec(memory_space=pltpu.HBM)
VM = pl.BlockSpec(memory_space=pltpu.VMEM)
SM = pl.BlockSpec(memory_space=pltpu.SMEM)
LIMIT = 32 << 20
LEAF = 220
STORE = LEAF + 510


def shape(*dims):
    return jax.ShapeDtypeStruct(dims, F32)


def params(limit=LIMIT):
    return pltpu.CompilerParams(vmem_limit_bytes=limit)


def cost(flops, nbytes):
    return pl.CostEstimate(flops=flops, bytes_accessed=nbytes, transcendentals=0)


def square(flat):
    return [[flat[N * i + j] for j in range(N)] for i in range(N)]


def flat(m):
    return [x for row in m for x in row]


def dot(xs, ys, start=None):
    total = start
    for x, y in zip(xs, ys):
        total = x * y if total is None else total + x * y
    return total


def mm(a, b, c=None):
    cols = list(zip(*b))
    return [
        [dot(a[i], cols[j], None if c is None else c[i][j]) for j in range(N)] for i in range(N)
    ]


def mv(a, x, c=None):
    return [dot(a[i], x, None if c is None else c[i]) for i in range(N)]


def lane_iota():
    return lax.broadcasted_iota(jnp.int32, (8, 128), 1)


def roll(x, by):
    return pltpu.roll(x, by % 128, 1)


def place():
    wall = lax.axis_index("wall")
    return lax.axis_index("chord"), wall // 2, wall % 2


def copy_all(copies):
    for c in copies:
        c.start()
    for c in copies:
        c.wait()


def pack_kernel(jet, rhs, mask, xl, xu, el, eu, send, keep, rv, mk, sem):
    _, _, core = place()
    copies = [pltpu.make_async_copy(rhs, rv, sem.at[8]), pltpu.make_async_copy(mask, mk, sem.at[9])]
    halves = ((send, pl.multiple_of((1 - core) * 16, 16)), (keep, pl.multiple_of(core * 16, 16)))
    for m, (dst, off) in enumerate(halves):
        for n, ref in enumerate((xl, xu, el, eu)):
            copies.append(
                pltpu.make_async_copy(
                    ref.at[:, pl.ds(off, 16), :], dst.at[pl.ds(25 * n, 25)], sem.at[4 * m + n]
                )
            )
    for c in copies:
        c.start()
    copies[0].wait()
    copies[1].wait()
    for dst, off in halves:
        m = mk[pl.ds(off, 16), :].astype(F32)
        for c in range(N):
            dst[100 + c] = rv[c, pl.ds(off, 16), :] + m * jet[c]
    for c in copies[2:]:
        c.wait()


def compose(left, right):
    lb1, lv1, ub1, uv1, w1 = left
    lb2, lv2, ub2, uv2, w2 = right
    lb = mm(lb2, lb1)
    lv = mv(lb2, lv1, lv2)
    ub = mm(ub1, ub2)
    uv = mv(ub1, mv(w2, lv1, uv2), uv1)
    w = mm(ub1, mm(w2, lb1), w1)
    return lb, lv, ub, uv, w


def node(values):
    return (
        square(values[0:25]),
        list(values[25:30]),
        square(values[30:55]),
        list(values[55:60]),
        square(values[60:85]),
    )


def values_of(n):
    return flat(n[0]) + list(n[1]) + flat(n[2]) + list(n[3]) + flat(n[4])


def up_kernel(keep, recv, msg, store, sl, su, ss, n1, n2, leaf, tree, sem):
    _, _, core = place()
    copies = []
    for n, (dst, first, count) in enumerate(((sl, 0, 25), (su, 25, 25), (ss, 100, N))):
        part = pl.ds(first, count)
        copies.append(pltpu.make_async_copy(keep.at[part], dst.at[:, core], sem.at[2 * n]))
        copies.append(pltpu.make_async_copy(recv.at[part], dst.at[:, 1 - core], sem.at[2 * n + 1]))
    copy_all(copies)
    lane = lane_iota()
    even = lane % 2 == 0
    low = (lane // 2) % 2 == 0

    def split(ref, c, r):
        a = ref[c, r, 0:8, :]
        b = ref[c, r, 8:16, :]
        return jnp.where(even, a, roll(b, 1)), jnp.where(even, roll(a, -1), b)

    saves = []
    for r in range(2):
        l1, l2 = zip(*[split(sl, c, r) for c in range(25)])
        v1, v2 = zip(*[split(ss, c, r) for c in range(N)])
        u1, u2 = zip(*[split(su, c, r) for c in range(25)])
        for c, x in enumerate(l1 + v1 + l2 + v2 + u1 + u2):
            leaf[r, c] = x
        dst = store.at[pl.ds(110 * r, 110)]
        saves.append(pltpu.make_async_copy(leaf.at[r], dst, sem.at[6 + r]))
        saves[-1].start()
        l1, l2, u1, u2 = square(l1), square(l2), square(u1), square(u2)
        lb = mm(l2, l1)
        lv = mv(l2, v1, v2)
        out = (lb, lv, mm(u1, u2), mv(u1, lv, v1), mm(u1, lb, l1))
        for c, x in enumerate(values_of(out)):
            n1[r, c] = x

    left, right = [], []
    for c in range(85):
        a, b = n1[0, c], n1[1, c]
        left.append(jnp.where(low, a, roll(b, 2)))
        right.append(jnp.where(low, roll(a, -2), b))
    for level in range(6):
        if level:
            left = [n2[c] for c in range(85)]
            right = [roll(x, -(2 << level)) for x in left]
        for c in range(30):
            tree[level, c] = left[c]
        for c in range(30, 85):
            tree[level, c] = right[c]
        dst = store.at[pl.ds(LEAF + 85 * level, 85)]
        saves.append(pltpu.make_async_copy(tree.at[level], dst, sem.at[8 + level]))
        saves[-1].start()
        for c, x in enumerate(values_of(compose(node(left), node(right)))):
            n2[c] = x
    group = lane // 4
    for g in range(3):
        acc = None
        for pos in range(min(32, 85 - 32 * g)):
            x = n2[32 * g + pos]
            acc = x if acc is None else jnp.where(group == pos, roll(x, 4 * pos), acc)
        for d in range(16):
            msg[d, 8 * g : 8 * g + 8, :] = acc
    for c in saves:
        c.wait()


def eta_copies(keep, recv, sl, su, core, sem):
    return [
        pltpu.make_async_copy(keep.at[pl.ds(50, 25)], sl.at[:, core], sem.at[0]),
        pltpu.make_async_copy(keep.at[pl.ds(75, 25)], su.at[:, core], sem.at[1]),
        pltpu.make_async_copy(recv.at[pl.ds(50, 25)], sl.at[:, 1 - core], sem.at[2]),
        pltpu.make_async_copy(recv.at[pl.ds(75, 25)], su.at[:, 1 - core], sem.at[3]),
    ]


def cell(ref, j):
    return square([ref[c, j // 2, pl.ds(j % 2, 8, stride=2), :] for c in range(25)])


def halves(x, y, first):
    return jnp.where(first, x, roll(y, 64)), jnp.where(first, roll(x, 64), y)


def wall_kernel(keep, recv, out, sl, su, sem):
    _, _, core = place()
    copy_all(eta_copies(keep, recv, sl, su, core, sem))
    lb = cell(sl, 0)
    w = lb
    ub = cell(su, 0)
    for j in range(1, 4):
        lb = mm(cell(sl, j), lb)
        w = mm(ub, lb, w)
        ub = mm(ub, cell(su, j))
    for c, x in enumerate(flat(lb) + flat(ub) + flat(w)):
        out[c] = x


def pair_copies(mine, other, both, odd, sem):
    return [
        pltpu.make_async_copy(mine, both.at[odd], sem.at[0]),
        pltpu.make_async_copy(other, both.at[1 - odd], sem.at[1]),
    ]


def pair_kernel(vecs, mine, other, out, give, both, comp, sem):
    _, z, _ = place()
    odd = z % 2
    even = odd == 0
    copy_all(pair_copies(mine, other, both, odd, sem))
    lb_e, ub_e, w_e = [square([both[0, 25 * n + c] for c in range(25)]) for n in range(3)]
    lb_o, ub_o, w_o = [square([both[1, 25 * n + c] for c in range(25)]) for n in range(3)]
    w = mm(ub_e, mm(w_o, lb_e), w_e)
    for c, x in enumerate(flat(mm(lb_o, lb_e)) + flat(mm(ub_e, ub_o)) + flat(w)):
        comp[c] = x
    lv = [vecs[c] for c in range(N)]
    uv = [vecs[N + c] for c in range(N)]
    for c in range(N):
        give[c] = jnp.where(even, lv[c], uv[c])
    new_lv = [jnp.where(even, x, y) for x, y in zip(mv(lb_o, lv), lv)]
    inner = [jnp.where(even, x, y) for x, y in zip(mv(w_o, lv), uv)]
    new_uv = [jnp.where(even, x + y, x) for x, y in zip(mv(ub_e, inner), uv)]
    first = lane_iota() < 64
    base = 37 * odd
    for r in range(ROWS):
        if r < VEC:
            x, y = comp[base + r], comp[base + VEC + r]
        else:
            x, y = new_lv[r - VEC], new_uv[r - VEC]
        x, y = halves(x, y, first)
        out[pl.ds(r, 8, stride=ROWS), :] = x
        out[pl.ds(8 * ROWS + r, 8, stride=ROWS), :] = y


def down_kernel(
    table, flags, got, store, keep, recv, scaled, vecs, sl, su, lf, tr, cs, bh, fl, sem
):
    chord, z, core = place()
    eta = eta_copies(keep, recv, sl, su, core, sem)
    pre = [
        pltpu.make_async_copy(store.at[pl.ds(LEAF, 510)], tr, sem.at[4]),
        pltpu.make_async_copy(store.at[pl.ds(0, LEAF)], lf, sem.at[5]),
    ]
    kinds = pltpu.make_async_copy(flags, fl, sem.at[6])
    kinds.start()
    for c in pre + eta:
        c.start()
    lane = lane_iota()
    group = lane // 4
    for g in range(3):
        v = [got[s, 8 * g : 8 * g + 8, :] for s in range(16)]
        for bit in range(4):
            step = 1 << bit
            same = (group // step) % 2 == 0
            fresh = list(v)
            for s in range(16):
                if s & step:
                    continue
                a, b = v[s], v[s | step]
                fresh[s] = jnp.where(same, a, roll(b, 4 * step))
                fresh[s | step] = jnp.where(same, roll(a, -4 * step), b)
            v = fresh
        for lo in range(16):
            if 32 * g + lo < 85:
                cs[32 * g + lo] = v[lo]
            if 32 * g + 16 + lo < 85:
                cs[32 * g + 16 + lo] = roll(v[lo], 64)

    def chain(m, t, sign):
        for bit in range(4):
            step = 1 << bit
            ok = group >= step if sign > 0 else group < 16 - step
            far = [roll(x, sign * 4 * step) for x in t]
            t = [jnp.where(ok, new, old) for new, old in zip(mv(m, far, t), t)]
            if bit < 3:
                fm = [[roll(x, sign * 4 * step) for x in row] for row in m]
                new = mm(m, fm)
                m = [[jnp.where(ok, new[i][j], m[i][j]) for j in range(N)] for i in range(N)]
        return t

    zero = jnp.zeros((8, 128), F32)
    t = chain(square([cs[c] for c in range(25)]), [cs[25 + c] for c in range(N)], 1)
    a = [jnp.where(group >= 1, roll(x, 4), zero) for x in t]
    f = mv(square([cs[60 + c] for c in range(25)]), a, [cs[55 + c] for c in range(N)])
    t = chain(square([cs[30 + c] for c in range(25)]), f, -1)
    b = [jnp.where(group < 15, roll(x, -4), zero) for x in t]
    back = (128 - 4 * chord) % 128
    a = [pltpu.roll(x, back, 1) for x in a]
    b = [pltpu.roll(x, back, 1) for x in b]

    pre[0].wait()
    for level in range(5, -1, -1):
        dist = 2 << level
        a_mid = mv(square([tr[85 * level + c] for c in range(25)]), a, [tr[85 * level + 25 + c] for c in range(N)])
        b_mid = mv(square([tr[85 * level + 30 + c] for c in range(25)]), b, [tr[85 * level + 55 + c] for c in range(N)])
        b_mid = mv(square([tr[85 * level + 60 + c] for c in range(25)]), a_mid, b_mid)
        left = (lane // dist) % 2 == 0
        if level:
            a = [jnp.where(left, x, roll(y, dist)) for x, y in zip(a, a_mid)]
            b = [jnp.where(left, x, roll(y, dist)) for x, y in zip(b_mid, b)]
    pre[1].wait()
    even = lane % 2 == 0
    for r in range(2):
        if r == 0:
            ra = [jnp.where(left, x, roll(y, 2)) for x, y in zip(a, a_mid)]
            rb = [jnp.where(left, x, roll(y, 2)) for x, y in zip(b_mid, b)]
        else:
            ra = [jnp.where(left, roll(x, -2), y) for x, y in zip(a, a_mid)]
            rb = [jnp.where(left, roll(x, -2), y) for x, y in zip(b_mid, b)]

        def part(first, count):
            return [lf[110 * r + first + c] for c in range(count)]

        a1 = mv(square(part(0, 25)), ra, part(25, N))
        a2 = mv(square(part(30, 25)), a1, part(55, N))
        b2 = mv(square(part(85, 25)), rb, a2)
        b1 = mv(square(part(60, 25)), b2, a1)
        for c in range(N):
            bh[c, r, 0:8, :] = jnp.where(even, b1[c], roll(b2[c], 1))
            bh[c, r, 8:16, :] = jnp.where(even, roll(b1[c], -1), b2[c])

    kinds.wait()
    kind = fl[pl.ds(pl.multiple_of(core * 8, 8), 8), :]
    s = []
    for j in range(4):
        s.append([bh[c, j // 2, pl.ds(j % 2, 8, stride=2), :] for c in range(N)])
    for c in range(N):
        factor = zero
        for k in range(3):
            factor = jnp.where(kind == k, table[k, c], factor)
        s[0][c] = jnp.where(z == 0, factor, 1.0) * s[0][c]
    for j in range(4):
        for c in range(N):
            scaled[j, c] = s[j][c]
    for c in eta:
        c.wait()
    t = [s[0]]
    for j in range(1, 4):
        t.append(mv(cell(sl, j), t[-1], s[j]))
    u = t[3]
    for j in range(2, -1, -1):
        u = mv(cell(su, j), u, t[j])
    for c in range(N):
        vecs[c] = t[3][c]
        vecs[N + c] = u[c]


def solve_kernel(got, back, turned, ain):
    for n in range(16 * ROWS // 8):
        turned[8 * n : 8 * n + 8, :] = pltpu.roll(got[8 * n : 8 * n + 8, :], 64, 1)

    def value(pair, c):
        odd = int(c > 37)
        c -= 37 * odd
        row = ROWS * (2 * pair + odd) + c % VEC
        return (turned if c >= VEC else got)[row : row + 1, :]

    def block(pair, first):
        return square([value(pair, first + c) for c in range(25)])

    def vec(pair, ref):
        row = 2 * ROWS * pair + VEC
        return [
            ref[row + c : row + c + 1, :] + ref[row + ROWS + c : row + ROWS + c + 1, :]
            for c in range(N)
        ]

    zero = jnp.zeros((1, 128), F32)
    for n in range(16):
        back[8 * n : 8 * n + 8, :] = jnp.zeros((8, 128), F32)
    a = [zero] * N
    for m in range(8):
        for c in range(N):
            ain[8 * m + c : 8 * m + c + 1, :] = a[c]
        if m < 7:
            a = mv(block(m, 0), a, vec(m, got)) if m else vec(m, got)
    first = lax.broadcasted_iota(jnp.int32, (1, 128), 1) < 64
    b = [zero] * N
    for m in range(7, -1, -1):
        a = [ain[8 * m + c : 8 * m + c + 1, :] for c in range(N)]
        for c in range(N):
            x = jnp.where(first, a[c], pltpu.roll(b[c], 64, 1))
            back[16 * m + c : 16 * m + c + 1, :] = x
            back[16 * m + 8 + c : 16 * m + 8 + c + 1, :] = x
        if m:
            f = mv(block(m, 50), a, vec(m, turned))
            b = mv(block(m, 25), b, f)


def finish_kernel(
    got, scaled, keep, recv, vecs, taken, mine, other, own, send, sl, su, res, both, sem
):
    _, z, core = place()
    odd = z % 2
    even = odd == 0
    copies = eta_copies(keep, recv, sl, su, core, sem)
    pair = [
        pltpu.make_async_copy(mine, both.at[odd], sem.at[4]),
        pltpu.make_async_copy(other, both.at[1 - odd], sem.at[5]),
    ]
    for c in pair + copies:
        c.start()
    first = lane_iota() < 64
    a, b = [], []
    for c in range(N):
        x = got[pl.ds(c, 8, stride=8), :]
        y = got[pl.ds(64 + c, 8, stride=8), :]
        a.append(jnp.where(first, x, roll(y, 64)))
        b.append(jnp.where(first, roll(x, 64), y))
    for c in pair:
        c.wait()
    lv_e = [jnp.where(even, vecs[c], taken[c]) for c in range(N)]
    mid = mv(square([both[0, c] for c in range(25)]), a, lv_e)
    low = mv(square([both[1, 50 + c] for c in range(25)]), mid, [taken[c] for c in range(N)])
    low = mv(square([both[1, 25 + c] for c in range(25)]), b, low)
    a = [jnp.where(even, x, y) for x, y in zip(a, mid)]
    b = [jnp.where(even, x, y) for x, y in zip(low, b)]
    for c in copies:
        c.wait()
    lifted = []
    for j in range(4):
        a = mv(cell(sl, j), a, [scaled[j, c] for c in range(N)])
        lifted.append(a)
    for j in range(3, -1, -1):
        b = mv(cell(su, j), b, lifted[j])
        for c in range(N):
            res[c, j // 2, pl.ds(j % 2, 8, stride=2), :] = b[c]
    for c in range(N):
        own[c] = res[c, core]
        send[c] = res[c, 1 - core]


def dma(n):
    return pltpu.SemaphoreType.DMA((n,))


def per_device(
    rhs, jet_mask, jet_source, wall_flags, bc_table, xi_lower, xi_upper, eta_lower, eta_upper
):
    def far(x, *dims):
        return pltpu.with_memory_space_constraint(x.reshape(dims), pltpu.HBM)

    rhs, mask, flags = far(rhs, N, 32, 128), far(jet_mask, 32, 128), far(wall_flags, 16, 128)
    xl, xu, el, eu = (far(x, 25, 32, 128) for x in (xi_lower, xi_upper, eta_lower, eta_upper))
    swap = [(n, n ^ 1) for n in range(lax.axis_size("wall"))]
    near = [(n, n ^ 2) for n in range(lax.axis_size("wall"))]
    groups = [list(range(c, lax.axis_size("wall"), 2)) for c in range(2)]

    def over_z(x):
        return lax.all_to_all(x, "wall", 0, 0, tiled=True, axis_index_groups=groups)

    side = pltpu.VMEM((25, 2, 16, 128), F32)
    send, keep = pl.pallas_call(
        pack_kernel,
        out_shape=(shape(105, 16, 128), shape(105, 16, 128)),
        in_specs=[SM] + [HBM] * 6,
        out_specs=(VM, VM),
        scratch_shapes=[pltpu.VMEM((N, 32, 128), F32), pltpu.VMEM((32, 128), jnp.int32), dma(10)],
        compiler_params=params(),
        name="pack",
    )(jet_source, rhs, mask, xl, xu, el, eu)
    recv = lax.ppermute(send, "wall", swap)
    msg, store = pl.pallas_call(
        up_kernel,
        out_shape=(shape(16, 24, 128), pltpu.HBM((STORE, 8, 128), F32)),
        in_specs=[ANY, ANY],
        out_specs=(VM, HBM),
        scratch_shapes=[
            side,
            side,
            pltpu.VMEM((N, 2, 16, 128), F32),
            pltpu.VMEM((2, 85, 8, 128), F32),
            pltpu.VMEM((85, 8, 128), F32),
            pltpu.VMEM((2, 110, 8, 128), F32),
            pltpu.VMEM((6, 85, 8, 128), F32),
            dma(14),
        ],
        compiler_params=params(),
        name="chord_up",
    )(keep, recv)
    mine = pl.pallas_call(
        wall_kernel,
        out_shape=shape(75, 8, 128),
        in_specs=[ANY, ANY],
        out_specs=VM,
        scratch_shapes=[side, side, dma(4)],
        compiler_params=params(),
        cost_estimate=cost(3 * 250 * 3 * 1024, 2 << 20),
        name="wall_blocks",
    )(keep, recv)
    other = lax.ppermute(mine, "wall", near)
    got = lax.all_to_all(msg, "chord", 0, 0, tiled=True)
    scaled, vecs = pl.pallas_call(
        down_kernel,
        out_shape=(shape(4, N, 8, 128), shape(2 * N, 8, 128)),
        in_specs=[SM, HBM, VM, HBM, ANY, ANY],
        out_specs=(VM, VM),
        scratch_shapes=[
            side,
            side,
            pltpu.VMEM((LEAF, 8, 128), F32),
            pltpu.VMEM((510, 8, 128), F32),
            pltpu.VMEM((85, 8, 128), F32),
            pltpu.VMEM((N, 2, 16, 128), F32),
            pltpu.VMEM((16, 128), jnp.int32),
            dma(7),
        ],
        compiler_params=params(),
        name="chord_down",
    )(bc_table, flags, got, far(store, STORE, 8, 128), keep, recv)
    both = pltpu.VMEM((2, 75, 8, 128), F32)
    zmsg, give = pl.pallas_call(
        pair_kernel,
        out_shape=(shape(16 * ROWS, 128), shape(N, 8, 128)),
        in_specs=[VM, ANY, ANY],
        out_specs=(VM, VM),
        scratch_shapes=[both, pltpu.VMEM((75, 8, 128), F32), dma(2)],
        compiler_params=params(),
        name="wall_pair",
    )(vecs, mine, other)
    zgot = over_z(zmsg.reshape(16, ROWS, 128)).reshape(16 * ROWS, 128)
    taken = lax.ppermute(give, "wall", near)
    back = pl.pallas_call(
        solve_kernel,
        out_shape=shape(128, 128),
        in_specs=[VM],
        out_specs=VM,
        scratch_shapes=[pltpu.VMEM((16 * ROWS, 128), F32), pltpu.VMEM((128, 128), F32)],
        compiler_params=params(),
        name="wall_solve",
    )(zgot)
    inflow = over_z(back.reshape(16, 8, 128)).reshape(128, 128)
    own, theirs = pl.pallas_call(
        finish_kernel,
        out_shape=(shape(N, 16, 128), shape(N, 16, 128)),
        in_specs=[VM, VM, ANY, ANY, VM, VM, ANY, ANY],
        out_specs=(VM, VM),
        scratch_shapes=[side, side, pltpu.VMEM((N, 2, 16, 128), F32), both, dma(6)],
        compiler_params=params(),
        name="finish",
    )(inflow, scaled, keep, recv, vecs, taken, mine, other)
    theirs = lax.ppermute(theirs, "wall", swap)
    core = lax.axis_index("wall") % 2
    low = jnp.where(core == 0, own, theirs)
    high = jnp.where(core == 0, theirs, own)
    return jnp.concatenate([low, high], axis=1).reshape(N, 16, 2, 128)


def solution(mesh):
    placed = (
        P(None, None, "wall", "chord"),
        P(None, "wall", "chord"),
        P(),
        P(None, "chord"),
        P(),
        P(None, None, None, "wall", "chord"),
        P(None, None, None, "wall", "chord"),
        P(None, None, None, "wall", "chord"),
        P(None, None, None, "wall", "chord"),
    )
    return jax.shard_map(
        per_device,
        mesh=mesh,
        in_specs=placed,
        out_specs=P(None, None, "wall", "chord"),
        check_vma=False,
    )
```

```python
import jax
import jax.numpy as jnp
from jax import lax
from jax.experimental import pallas as pl
from jax.experimental.pallas import tpu as pltpu
from jax.sharding import PartitionSpec as P

F32 = jnp.float32
N = 5
ROWS = 24
VEC = 19
ANY = pl.BlockSpec(memory_space=pl.ANY)
HBM = pl.BlockSpec(memory_space=pltpu.HBM)
VM = pl.BlockSpec(memory_space=pltpu.VMEM)
SM = pl.BlockSpec(memory_space=pltpu.SMEM)
LIMIT = 32 << 20
LEAF = 220
STORE = LEAF + 510


def shape(*dims):
    return jax.ShapeDtypeStruct(dims, F32)


def params(limit=LIMIT):
    return pltpu.CompilerParams(vmem_limit_bytes=limit)


def cost(flops, nbytes):
    return pl.CostEstimate(flops=flops, bytes_accessed=nbytes, transcendentals=0)


def square(flat):
    return [[flat[N * i + j] for j in range(N)] for i in range(N)]


def flat(m):
    return [x for row in m for x in row]


def dot(xs, ys, start=None):
    total = start
    for x, y in zip(xs, ys):
        total = x * y if total is None else total + x * y
    return total


def mm(a, b, c=None):
    cols = list(zip(*b))
    return [
        [dot(a[i], cols[j], None if c is None else c[i][j]) for j in range(N)] for i in range(N)
    ]


def mv(a, x, c=None):
    return [dot(a[i], x, None if c is None else c[i]) for i in range(N)]


def lane_iota():
    return lax.broadcasted_iota(jnp.int32, (8, 128), 1)


def roll(x, by):
    return pltpu.roll(x, by % 128, 1)


def place():
    wall = lax.axis_index("wall")
    return lax.axis_index("chord"), wall // 2, wall % 2


def copy_all(copies):
    for c in copies:
        c.start()
    for c in copies:
        c.wait()


def compose(left, right):
    lb1, lv1, ub1, uv1, w1 = left
    lb2, lv2, ub2, uv2, w2 = right
    lb = mm(lb2, lb1)
    lv = mv(lb2, lv1, lv2)
    ub = mm(ub1, ub2)
    uv = mv(ub1, mv(w2, lv1, uv2), uv1)
    w = mm(ub1, mm(w2, lb1), w1)
    return lb, lv, ub, uv, w


def node(values):
    return (
        square(values[0:25]),
        list(values[25:30]),
        square(values[30:55]),
        list(values[55:60]),
        square(values[60:85]),
    )


def values_of(n):
    return flat(n[0]) + list(n[1]) + flat(n[2]) + list(n[3]) + flat(n[4])


def up_kernel(
    jet, rhs, mask, xl, xu, el, eu, msg, store, send, keep,
    sl, su, ss, mk, n1, n2, leaf, tree, sem,
):
    core = place()[2]
    copies = [
        pltpu.make_async_copy(src, dst, sem.at[n])
        for n, (src, dst) in enumerate(((rhs, ss), (mask, mk), (xl, sl), (xu, su)))
    ]
    for c in copies:
        c.start()
    copies[0].wait()
    copies[1].wait()
    m = mk[...].astype(F32)
    for c in range(N):
        ss[c] = ss[c] + m * jet[c]
    copies[2].wait()
    copies[3].wait()
    eta = []
    for n, (dst, half) in enumerate(((send, 1 - core), (keep, core))):
        off = pl.multiple_of(half * 16, 16)
        for k, ref in enumerate((el, eu)):
            part = dst.at[pl.ds(25 * k, 25)]
            at = sem.at[14 + 2 * n + k]
            eta.append(pltpu.make_async_copy(ref.at[:, pl.ds(off, 16), :], part, at))
            eta[-1].start()
    lane = lane_iota()
    even = lane % 2 == 0
    low = (lane // 2) % 2 == 0

    def split(ref, c, r):
        a = ref[c, 16 * r : 16 * r + 8, :]
        b = ref[c, 16 * r + 8 : 16 * r + 16, :]
        return jnp.where(even, a, roll(b, 1)), jnp.where(even, roll(a, -1), b)

    saves = []
    for r in range(2):
        l1, l2 = zip(*[split(sl, c, r) for c in range(25)])
        v1, v2 = zip(*[split(ss, c, r) for c in range(N)])
        u1, u2 = zip(*[split(su, c, r) for c in range(25)])
        for c, x in enumerate(l1 + v1 + l2 + v2 + u1 + u2):
            leaf[r, c] = x
        dst = store.at[pl.ds(110 * r, 110)]
        saves.append(pltpu.make_async_copy(leaf.at[r], dst, sem.at[6 + r]))
        saves[-1].start()
        l1, l2, u1, u2 = square(l1), square(l2), square(u1), square(u2)
        lb = mm(l2, l1)
        lv = mv(l2, v1, v2)
        out = (lb, lv, mm(u1, u2), mv(u1, lv, v1), mm(u1, lb, l1))
        for c, x in enumerate(values_of(out)):
            n1[r, c] = x

    left, right = [], []
    for c in range(85):
        a, b = n1[0, c], n1[1, c]
        left.append(jnp.where(low, a, roll(b, 2)))
        right.append(jnp.where(low, roll(a, -2), b))
    for level in range(6):
        if level:
            left = [n2[c] for c in range(85)]
            right = [roll(x, -(2 << level)) for x in left]
        for c in range(30):
            tree[level, c] = left[c]
        for c in range(30, 85):
            tree[level, c] = right[c]
        dst = store.at[pl.ds(LEAF + 85 * level, 85)]
        saves.append(pltpu.make_async_copy(tree.at[level], dst, sem.at[8 + level]))
        saves[-1].start()
        for c, x in enumerate(values_of(compose(node(left), node(right)))):
            n2[c] = x
    group = lane // 4
    for g in range(3):
        acc = None
        for pos in range(min(32, 85 - 32 * g)):
            x = n2[32 * g + pos]
            acc = x if acc is None else jnp.where(group == pos, roll(x, 4 * pos), acc)
        for d in range(16):
            msg[d, 8 * g : 8 * g + 8, :] = acc
    for c in saves + eta:
        c.wait()


def eta_copies(keep, recv, sl, su, core, sem):
    return [
        pltpu.make_async_copy(keep.at[pl.ds(0, 25)], sl.at[:, core], sem.at[0]),
        pltpu.make_async_copy(keep.at[pl.ds(25, 25)], su.at[:, core], sem.at[1]),
        pltpu.make_async_copy(recv.at[pl.ds(0, 25)], sl.at[:, 1 - core], sem.at[2]),
        pltpu.make_async_copy(recv.at[pl.ds(25, 25)], su.at[:, 1 - core], sem.at[3]),
    ]


def cell(ref, j):
    return square([ref[c, j // 2, pl.ds(j % 2, 8, stride=2), :] for c in range(25)])


def halves(x, y, first):
    return jnp.where(first, x, roll(y, 64)), jnp.where(first, roll(x, 64), y)


def wall_kernel(keep, recv, out, sl, su, sem):
    _, _, core = place()
    copy_all(eta_copies(keep, recv, sl, su, core, sem))
    lb = cell(sl, 0)
    w = lb
    ub = cell(su, 0)
    for j in range(1, 4):
        lb = mm(cell(sl, j), lb)
        w = mm(ub, lb, w)
        ub = mm(ub, cell(su, j))
    for c, x in enumerate(flat(lb) + flat(ub) + flat(w)):
        out[c] = x


def sources(here, there, slots, core):
    for c in range(N):
        slots[c, core] = here[c]
        slots[c, 1 - core] = there[c]
    return [
        [slots[c, j // 2, pl.ds(j % 2, 8, stride=2), :] for c in range(N)] for j in range(4)
    ]


def pair_kernel(
    here, there, keep, recv, mine, other, out, give, hold, sl, su, slots, both, comp, sem
):
    _, z, core = place()
    odd = z % 2
    even = odd == 0
    pair = [
        pltpu.make_async_copy(mine, both.at[odd], sem.at[4]),
        pltpu.make_async_copy(other, both.at[1 - odd], sem.at[5]),
    ]
    eta = eta_copies(keep, recv, sl, su, core, sem)
    for c in eta + pair:
        c.start()
    s = sources(here, there, slots, core)
    for c in eta:
        c.wait()
    t = [s[0]]
    for j in range(1, 4):
        t.append(mv(cell(sl, j), t[-1], s[j]))
    lv = t[3]
    uv = t[3]
    for j in range(2, -1, -1):
        uv = mv(cell(su, j), uv, t[j])
    for c in pair:
        c.wait()
    lb_e, ub_e, w_e = [square([both[0, 25 * n + c] for c in range(25)]) for n in range(3)]
    lb_o, ub_o, w_o = [square([both[1, 25 * n + c] for c in range(25)]) for n in range(3)]
    w = mm(ub_e, mm(w_o, lb_e), w_e)
    for c, x in enumerate(flat(mm(lb_o, lb_e)) + flat(mm(ub_e, ub_o)) + flat(w)):
        comp[c] = x
    for c in range(N):
        give[c] = jnp.where(even, lv[c], uv[c])
        hold[c] = lv[c]
    new_lv = [jnp.where(even, x, y) for x, y in zip(mv(lb_o, lv), lv)]
    inner = [jnp.where(even, x, y) for x, y in zip(mv(w_o, lv), uv)]
    new_uv = [jnp.where(even, x + y, x) for x, y in zip(mv(ub_e, inner), uv)]
    first = lane_iota() < 64
    base = 37 * odd
    for r in range(ROWS):
        if r < VEC:
            x, y = comp[base + r], comp[base + VEC + r]
        else:
            x, y = new_lv[r - VEC], new_uv[r - VEC]
        x, y = halves(x, y, first)
        out[pl.ds(r, 8, stride=ROWS), :] = x
        out[pl.ds(8 * ROWS + r, 8, stride=ROWS), :] = y


def down_kernel(
    table, flags, got, store, here, send, lf, tr, cs, bh, fl, sem
):
    chord, z, core = place()
    pre = [
        pltpu.make_async_copy(store.at[pl.ds(LEAF, 510)], tr, sem.at[0]),
        pltpu.make_async_copy(store.at[pl.ds(0, LEAF)], lf, sem.at[1]),
        pltpu.make_async_copy(flags, fl, sem.at[2]),
    ]
    for c in pre:
        c.start()
    lane = lane_iota()
    group = lane // 4
    for g in range(3):
        v = [got[s, 8 * g : 8 * g + 8, :] for s in range(16)]
        for bit in range(4):
            step = 1 << bit
            same = (group // step) % 2 == 0
            fresh = list(v)
            for s in range(16):
                if s & step:
                    continue
                a, b = v[s], v[s | step]
                fresh[s] = jnp.where(same, a, roll(b, 4 * step))
                fresh[s | step] = jnp.where(same, roll(a, -4 * step), b)
            v = fresh
        for lo in range(16):
            if 32 * g + lo < 85:
                cs[32 * g + lo] = v[lo]
            if 32 * g + 16 + lo < 85:
                cs[32 * g + 16 + lo] = roll(v[lo], 64)

    def chain(m, t, sign):
        for bit in range(4):
            step = 1 << bit
            ok = group >= step if sign > 0 else group < 16 - step
            far = [roll(x, sign * 4 * step) for x in t]
            t = [jnp.where(ok, new, old) for new, old in zip(mv(m, far, t), t)]
            if bit < 3:
                fm = [[roll(x, sign * 4 * step) for x in row] for row in m]
                new = mm(m, fm)
                m = [[jnp.where(ok, new[i][j], m[i][j]) for j in range(N)] for i in range(N)]
        return t

    zero = jnp.zeros((8, 128), F32)
    t = chain(square([cs[c] for c in range(25)]), [cs[25 + c] for c in range(N)], 1)
    a = [jnp.where(group >= 1, roll(x, 4), zero) for x in t]
    f = mv(square([cs[60 + c] for c in range(25)]), a, [cs[55 + c] for c in range(N)])
    t = chain(square([cs[30 + c] for c in range(25)]), f, -1)
    b = [jnp.where(group < 15, roll(x, -4), zero) for x in t]
    back = (128 - 4 * chord) % 128
    a = [pltpu.roll(x, back, 1) for x in a]
    b = [pltpu.roll(x, back, 1) for x in b]

    pre[0].wait()
    for level in range(5, -1, -1):
        dist = 2 << level
        a_mid = mv(square([tr[85 * level + c] for c in range(25)]), a, [tr[85 * level + 25 + c] for c in range(N)])
        b_mid = mv(square([tr[85 * level + 30 + c] for c in range(25)]), b, [tr[85 * level + 55 + c] for c in range(N)])
        b_mid = mv(square([tr[85 * level + 60 + c] for c in range(25)]), a_mid, b_mid)
        left = (lane // dist) % 2 == 0
        if level:
            a = [jnp.where(left, x, roll(y, dist)) for x, y in zip(a, a_mid)]
            b = [jnp.where(left, x, roll(y, dist)) for x, y in zip(b_mid, b)]
    pre[1].wait()
    even = lane % 2 == 0
    for r in range(2):
        if r == 0:
            ra = [jnp.where(left, x, roll(y, 2)) for x, y in zip(a, a_mid)]
            rb = [jnp.where(left, x, roll(y, 2)) for x, y in zip(b_mid, b)]
        else:
            ra = [jnp.where(left, roll(x, -2), y) for x, y in zip(a, a_mid)]
            rb = [jnp.where(left, roll(x, -2), y) for x, y in zip(b_mid, b)]

        def part(first, count):
            return [lf[110 * r + first + c] for c in range(count)]

        a1 = mv(square(part(0, 25)), ra, part(25, N))
        a2 = mv(square(part(30, 25)), a1, part(55, N))
        b2 = mv(square(part(85, 25)), rb, a2)
        b1 = mv(square(part(60, 25)), b2, a1)
        for c in range(N):
            bh[c, r, 0:8, :] = jnp.where(even, b1[c], roll(b2[c], 1))
            bh[c, r, 8:16, :] = jnp.where(even, roll(b1[c], -1), b2[c])

    pre[2].wait()
    wall = (z == 0) & (core == 0)
    for half in range(2):
        kind = fl[8 * half : 8 * half + 8, :]
        for c in range(N):
            factor = zero
            for k in range(3):
                factor = jnp.where(kind == k, table[k, c], factor)
            row = bh[c, half, pl.ds(0, 8, stride=2), :]
            bh[c, half, pl.ds(0, 8, stride=2), :] = jnp.where(wall, factor, 1.0) * row
    for c in range(N):
        here[c] = bh[c, core]
        send[c] = bh[c, 1 - core]


def solve_kernel(got, back, turned, ain):
    for n in range(16 * ROWS // 8):
        turned[8 * n : 8 * n + 8, :] = pltpu.roll(got[8 * n : 8 * n + 8, :], 64, 1)

    def value(pair, c):
        odd = int(c > 37)
        c -= 37 * odd
        row = ROWS * (2 * pair + odd) + c % VEC
        return (turned if c >= VEC else got)[row : row + 1, :]

    def block(pair, first):
        return square([value(pair, first + c) for c in range(25)])

    def vec(pair, ref):
        row = 2 * ROWS * pair + VEC
        return [
            ref[row + c : row + c + 1, :] + ref[row + ROWS + c : row + ROWS + c + 1, :]
            for c in range(N)
        ]

    zero = jnp.zeros((1, 128), F32)
    for n in range(16):
        back[8 * n : 8 * n + 8, :] = jnp.zeros((8, 128), F32)
    a = [zero] * N
    for m in range(8):
        for c in range(N):
            ain[8 * m + c : 8 * m + c + 1, :] = a[c]
        if m < 7:
            a = mv(block(m, 0), a, vec(m, got)) if m else vec(m, got)
    first = lax.broadcasted_iota(jnp.int32, (1, 128), 1) < 64
    b = [zero] * N
    for m in range(7, -1, -1):
        a = [ain[8 * m + c : 8 * m + c + 1, :] for c in range(N)]
        for c in range(N):
            x = jnp.where(first, a[c], pltpu.roll(b[c], 64, 1))
            back[16 * m + c : 16 * m + c + 1, :] = x
            back[16 * m + 8 + c : 16 * m + 8 + c + 1, :] = x
        if m:
            f = mv(block(m, 50), a, vec(m, turned))
            b = mv(block(m, 25), b, f)


def finish_kernel(
    got, here, there, keep, recv, hold, taken, mine, other, own, send, sl, su, res, both, sem
):
    _, z, core = place()
    odd = z % 2
    even = odd == 0
    copies = eta_copies(keep, recv, sl, su, core, sem)
    pair = [
        pltpu.make_async_copy(mine, both.at[odd], sem.at[4]),
        pltpu.make_async_copy(other, both.at[1 - odd], sem.at[5]),
    ]
    for c in pair + copies:
        c.start()
    first = lane_iota() < 64
    a, b = [], []
    for c in range(N):
        x = got[pl.ds(c, 8, stride=8), :]
        y = got[pl.ds(64 + c, 8, stride=8), :]
        a.append(jnp.where(first, x, roll(y, 64)))
        b.append(jnp.where(first, roll(x, 64), y))
    for c in pair:
        c.wait()
    lv_e = [jnp.where(even, hold[c], taken[c]) for c in range(N)]
    mid = mv(square([both[0, c] for c in range(25)]), a, lv_e)
    low = mv(square([both[1, 50 + c] for c in range(25)]), mid, [taken[c] for c in range(N)])
    low = mv(square([both[1, 25 + c] for c in range(25)]), b, low)
    a = [jnp.where(even, x, y) for x, y in zip(a, mid)]
    b = [jnp.where(even, x, y) for x, y in zip(low, b)]
    for c in copies:
        c.wait()
    s = sources(here, there, res, core)
    lifted = []
    for j in range(4):
        a = mv(cell(sl, j), a, s[j])
        lifted.append(a)
    for j in range(3, -1, -1):
        b = mv(cell(su, j), b, lifted[j])
        for c in range(N):
            res[c, j // 2, pl.ds(j % 2, 8, stride=2), :] = b[c]
    for c in range(N):
        own[c] = res[c, core]
        send[c] = res[c, 1 - core]


def dma(n):
    return pltpu.SemaphoreType.DMA((n,))


def per_device(
    rhs, jet_mask, jet_source, wall_flags, bc_table, xi_lower, xi_upper, eta_lower, eta_upper
):
    def far(x, *dims):
        return pltpu.with_memory_space_constraint(x.reshape(dims), pltpu.HBM)

    rhs, mask, flags = far(rhs, N, 32, 128), far(jet_mask, 32, 128), far(wall_flags, 16, 128)
    xl, xu, el, eu = (far(x, 25, 32, 128) for x in (xi_lower, xi_upper, eta_lower, eta_upper))
    swap = [(n, n ^ 1) for n in range(lax.axis_size("wall"))]
    near = [(n, n ^ 2) for n in range(lax.axis_size("wall"))]
    groups = [list(range(c, lax.axis_size("wall"), 2)) for c in range(2)]

    def over_z(x):
        return lax.all_to_all(x, "wall", 0, 0, tiled=True, axis_index_groups=groups)

    side = pltpu.VMEM((25, 2, 16, 128), F32)
    cells = pltpu.VMEM((N, 2, 16, 128), F32)
    both = pltpu.VMEM((2, 75, 8, 128), F32)
    msg, store, send, keep = pl.pallas_call(
        up_kernel,
        out_shape=(
            shape(16, 24, 128),
            pltpu.HBM((STORE, 8, 128), F32),
            shape(50, 16, 128),
            shape(50, 16, 128),
        ),
        in_specs=[SM] + [HBM] * 6,
        out_specs=(VM, HBM, VM, VM),
        scratch_shapes=[
            pltpu.VMEM((25, 32, 128), F32),
            pltpu.VMEM((25, 32, 128), F32),
            pltpu.VMEM((N, 32, 128), F32),
            pltpu.VMEM((32, 128), jnp.int32),
            pltpu.VMEM((2, 85, 8, 128), F32),
            pltpu.VMEM((85, 8, 128), F32),
            pltpu.VMEM((2, 110, 8, 128), F32),
            pltpu.VMEM((6, 85, 8, 128), F32),
            dma(18),
        ],
        compiler_params=params(),
        cost_estimate=cost(9000 * 1024, 4 << 20),
        name="chord_up",
    )(jet_source, rhs, mask, xl, xu, el, eu)
    recv = lax.ppermute(send, "wall", swap)
    mine = pl.pallas_call(
        wall_kernel,
        out_shape=shape(75, 8, 128),
        in_specs=[ANY, ANY],
        out_specs=VM,
        scratch_shapes=[side, side, dma(4)],
        compiler_params=params(),
        cost_estimate=cost(3 * 250 * 3 * 1024, 2 << 20),
        name="wall_blocks",
    )(keep, recv)
    other = lax.ppermute(mine, "wall", near)
    got = lax.all_to_all(msg, "chord", 0, 0, tiled=True)
    here, away = pl.pallas_call(
        down_kernel,
        out_shape=(shape(N, 16, 128), shape(N, 16, 128)),
        in_specs=[SM, HBM, VM, HBM],
        out_specs=(VM, VM),
        scratch_shapes=[
            pltpu.VMEM((LEAF, 8, 128), F32),
            pltpu.VMEM((510, 8, 128), F32),
            pltpu.VMEM((85, 8, 128), F32),
            cells,
            pltpu.VMEM((16, 128), jnp.int32),
            dma(3),
        ],
        compiler_params=params(),
        cost_estimate=cost(50_000_000_000, 4 << 20),
        name="chord_down",
    )(bc_table, flags, got, far(store, STORE, 8, 128))
    there = lax.ppermute(away, "wall", swap)
    zmsg, give, hold = pl.pallas_call(
        pair_kernel,
        out_shape=(shape(16 * ROWS, 128), shape(N, 8, 128), shape(N, 8, 128)),
        in_specs=[VM, VM, ANY, ANY, ANY, ANY],
        out_specs=(VM, VM, VM),
        scratch_shapes=[side, side, cells, both, pltpu.VMEM((75, 8, 128), F32), dma(6)],
        compiler_params=params(),
        name="wall_pair",
    )(here, there, keep, recv, mine, other)
    zgot = over_z(zmsg.reshape(16, ROWS, 128)).reshape(16 * ROWS, 128)
    taken = lax.ppermute(give, "wall", near)
    back = pl.pallas_call(
        solve_kernel,
        out_shape=shape(128, 128),
        in_specs=[VM],
        out_specs=VM,
        scratch_shapes=[pltpu.VMEM((16 * ROWS, 128), F32), pltpu.VMEM((128, 128), F32)],
        compiler_params=params(),
        name="wall_solve",
    )(zgot)
    inflow = over_z(back.reshape(16, 8, 128)).reshape(128, 128)
    own, theirs = pl.pallas_call(
        finish_kernel,
        out_shape=(shape(N, 16, 128), shape(N, 16, 128)),
        in_specs=[VM, VM, VM, ANY, ANY, VM, VM, ANY, ANY],
        out_specs=(VM, VM),
        scratch_shapes=[side, side, cells, both, dma(6)],
        compiler_params=params(),
        name="finish",
    )(inflow, here, there, keep, recv, hold, taken, mine, other)
    theirs = lax.ppermute(theirs, "wall", swap)
    core = lax.axis_index("wall") % 2
    low = jnp.where(core == 0, own, theirs)
    high = jnp.where(core == 0, theirs, own)
    return jnp.concatenate([low, high], axis=1).reshape(N, 16, 2, 128)


def solution(mesh):
    placed = (
        P(None, None, "wall", "chord"),
        P(None, "wall", "chord"),
        P(),
        P(None, "chord"),
        P(),
        P(None, None, None, "wall", "chord"),
        P(None, None, None, "wall", "chord"),
        P(None, None, None, "wall", "chord"),
        P(None, None, None, "wall", "chord"),
    )
    return jax.shard_map(
        per_device,
        mesh=mesh,
        in_specs=placed,
        out_specs=P(None, None, "wall", "chord"),
        check_vma=False,
    )
```

```python
import jax
import jax.numpy as jnp
from jax import lax
from jax.experimental import pallas as pl
from jax.experimental.pallas import tpu as pltpu
from jax.sharding import PartitionSpec as P

F32 = jnp.float32
N = 5
ROWS = 24
VEC = 19
ANY = pl.BlockSpec(memory_space=pl.ANY)
HBM = pl.BlockSpec(memory_space=pltpu.HBM)
VM = pl.BlockSpec(memory_space=pltpu.VMEM)
SM = pl.BlockSpec(memory_space=pltpu.SMEM)
LIMIT = 32 << 20
LEVELS = 6


def shape(*dims):
    return jax.ShapeDtypeStruct(dims, F32)


def params(limit=LIMIT):
    return pltpu.CompilerParams(vmem_limit_bytes=limit)


def cost(flops, nbytes):
    return pl.CostEstimate(flops=flops, bytes_accessed=nbytes, transcendentals=0)


def square(flat):
    return [[flat[N * i + j] for j in range(N)] for i in range(N)]


def flat(m):
    return [x for row in m for x in row]


def dot(xs, ys, start=None):
    total = start
    for x, y in zip(xs, ys):
        total = x * y if total is None else total + x * y
    return total


def mm(a, b, c=None):
    cols = list(zip(*b))
    return [
        [dot(a[i], cols[j], None if c is None else c[i][j]) for j in range(N)] for i in range(N)
    ]


def mv(a, x, c=None):
    return [dot(a[i], x, None if c is None else c[i]) for i in range(N)]


def lane_iota():
    return lax.broadcasted_iota(jnp.int32, (8, 128), 1)


def roll(x, by):
    return pltpu.roll(x, by % 128, 1)


def place():
    wall = lax.axis_index("wall")
    return lax.axis_index("chord"), wall // 2, wall % 2


def copy_all(copies):
    for c in copies:
        c.start()
    for c in copies:
        c.wait()


def compose(left, right):
    lb1, lv1, ub1, uv1, w1 = left
    lb2, lv2, ub2, uv2, w2 = right
    lb = mm(lb2, lb1)
    lv = mv(lb2, lv1, lv2)
    ub = mm(ub1, ub2)
    uv = mv(ub1, mv(w2, lv1, uv2), uv1)
    w = mm(ub1, mm(w2, lb1), w1)
    return lb, lv, ub, uv, w


def node(values):
    return (
        square(values[0:25]),
        list(values[25:30]),
        square(values[30:55]),
        list(values[55:60]),
        square(values[60:85]),
    )


def values_of(n):
    return flat(n[0]) + list(n[1]) + flat(n[2]) + list(n[3]) + flat(n[4])


def up_kernel(
    jet, rhs, mask, xl, xu, el, eu, msg, send, keep, leaf0, leaf1, store,
    tree, sl, su, ss, mk, jt, n1, n2, sem,
):
    leaves = (leaf0, leaf1)
    core = place()[2]
    copies = [
        pltpu.make_async_copy(src, dst, sem.at[n])
        for n, (src, dst) in enumerate(((jet, jt), (mask, mk), (rhs, ss)))
    ]
    for r in range(2):
        rows = pl.ds(16 * r, 16)
        for n, (src, dst) in enumerate(((xl, sl), (xu, su))):
            at = sem.at[3 + 2 * r + n]
            copies.append(pltpu.make_async_copy(src.at[:, rows, :], dst.at[:, rows, :], at))
    for c in copies:
        c.start()
    for c in copies[:3]:
        c.wait()
    m = mk[...].astype(F32)
    for c in range(N):
        ss[c] = ss[c] + m * jt[c]
    moves = []
    for n, (dst, half) in enumerate(((send, 1 - core), (keep, core))):
        off = pl.multiple_of(half * 16, 16)
        for k, ref in enumerate((el, eu)):
            part = dst.at[pl.ds(25 * k, 25)]
            at = sem.at[7 + 2 * n + k]
            moves.append(pltpu.make_async_copy(ref.at[:, pl.ds(off, 16), :], part, at))
            moves[-1].start()
    lane = lane_iota()
    even = lane % 2 == 0
    low = (lane // 2) % 2 == 0

    def split(ref, c, r):
        a = ref[c, 16 * r : 16 * r + 8, :]
        b = ref[c, 16 * r + 8 : 16 * r + 16, :]
        return jnp.where(even, a, roll(b, 1)), jnp.where(even, roll(a, -1), b)

    for r in range(2):
        copies[3 + 2 * r].wait()
        copies[4 + 2 * r].wait()
        l1, l2 = zip(*[split(sl, c, r) for c in range(25)])
        v1, v2 = zip(*[split(ss, c, r) for c in range(N)])
        u1, u2 = zip(*[split(su, c, r) for c in range(25)])
        for c, x in enumerate(l1 + v1 + l2 + v2 + u1 + u2):
            leaves[r][c] = x
        l1, l2, u1, u2 = square(l1), square(l2), square(u1), square(u2)
        lb = mm(l2, l1)
        lv = mv(l2, v1, v2)
        out = (lb, lv, mm(u1, u2), mv(u1, lv, v1), mm(u1, lb, l1))
        for c, x in enumerate(values_of(out)):
            n1[r, c] = x

    left, right = [], []
    for c in range(85):
        a, b = n1[0, c], n1[1, c]
        left.append(jnp.where(low, a, roll(b, 2)))
        right.append(jnp.where(low, roll(a, -2), b))
    for level in range(LEVELS):
        if level:
            left = [n2[c] for c in range(85)]
            right = [roll(x, -(2 << level)) for x in left]
        for c in range(30):
            tree[level, c] = left[c]
        for c in range(30, 85):
            tree[level, c] = right[c]
        moves.append(pltpu.make_async_copy(tree.at[level], store.at[level], sem.at[11 + level]))
        moves[-1].start()
        for c, x in enumerate(values_of(compose(node(left), node(right)))):
            n2[c] = x
    group = lane // 4
    for g in range(3):
        acc = None
        for pos in range(min(32, 85 - 32 * g)):
            x = n2[32 * g + pos]
            acc = x if acc is None else jnp.where(group == pos, roll(x, 4 * pos), acc)
        for d in range(16):
            msg[d, 8 * g : 8 * g + 8, :] = acc
    for c in moves:
        c.wait()


def eta_copies(keep, recv, sl, su, core, sem):
    return [
        pltpu.make_async_copy(keep.at[pl.ds(0, 25)], sl.at[:, core], sem.at[0]),
        pltpu.make_async_copy(keep.at[pl.ds(25, 25)], su.at[:, core], sem.at[1]),
        pltpu.make_async_copy(recv.at[pl.ds(0, 25)], sl.at[:, 1 - core], sem.at[2]),
        pltpu.make_async_copy(recv.at[pl.ds(25, 25)], su.at[:, 1 - core], sem.at[3]),
    ]


def cell(ref, j):
    return square([ref[c, j // 2, pl.ds(j % 2, 8, stride=2), :] for c in range(25)])


def halves(x, y, first):
    return jnp.where(first, x, roll(y, 64)), jnp.where(first, roll(x, 64), y)


def wall_kernel(keep, recv, out, sl, su, sem):
    _, _, core = place()
    copy_all(eta_copies(keep, recv, sl, su, core, sem))
    lb = cell(sl, 0)
    w = lb
    ub = cell(su, 0)
    for j in range(1, 4):
        lb = mm(cell(sl, j), lb)
        w = mm(ub, lb, w)
        ub = mm(ub, cell(su, j))
    for c, x in enumerate(flat(lb) + flat(ub) + flat(w)):
        out[c] = x


def sources(here, there, slots, core):
    for c in range(N):
        slots[c, core] = here[c]
        slots[c, 1 - core] = there[c]
    return [
        [slots[c, j // 2, pl.ds(j % 2, 8, stride=2), :] for c in range(N)] for j in range(4)
    ]


def pair_kernel(
    here, there, keep, recv, mine, other, out, give, hold, sl, su, slots, both, comp, sem
):
    _, z, core = place()
    odd = z % 2
    even = odd == 0
    pair = [
        pltpu.make_async_copy(mine, both.at[odd], sem.at[4]),
        pltpu.make_async_copy(other, both.at[1 - odd], sem.at[5]),
    ]
    eta = eta_copies(keep, recv, sl, su, core, sem)
    for c in eta + pair:
        c.start()
    s = sources(here, there, slots, core)
    for c in eta:
        c.wait()
    t = [s[0]]
    for j in range(1, 4):
        t.append(mv(cell(sl, j), t[-1], s[j]))
    lv = t[3]
    uv = t[3]
    for j in range(2, -1, -1):
        uv = mv(cell(su, j), uv, t[j])
    for c in pair:
        c.wait()
    lb_e, ub_e, w_e = [square([both[0, 25 * n + c] for c in range(25)]) for n in range(3)]
    lb_o, ub_o, w_o = [square([both[1, 25 * n + c] for c in range(25)]) for n in range(3)]
    w = mm(ub_e, mm(w_o, lb_e), w_e)
    for c, x in enumerate(flat(mm(lb_o, lb_e)) + flat(mm(ub_e, ub_o)) + flat(w)):
        comp[c] = x
    for c in range(N):
        give[c] = jnp.where(even, lv[c], uv[c])
        hold[c] = lv[c]
    new_lv = [jnp.where(even, x, y) for x, y in zip(mv(lb_o, lv), lv)]
    inner = [jnp.where(even, x, y) for x, y in zip(mv(w_o, lv), uv)]
    new_uv = [jnp.where(even, x + y, x) for x, y in zip(mv(ub_e, inner), uv)]
    first = lane_iota() < 64
    base = 37 * odd
    for r in range(ROWS):
        if r < VEC:
            x, y = comp[base + r], comp[base + VEC + r]
        else:
            x, y = new_lv[r - VEC], new_uv[r - VEC]
        x, y = halves(x, y, first)
        out[pl.ds(r, 8, stride=ROWS), :] = x
        out[pl.ds(8 * ROWS + r, 8, stride=ROWS), :] = y


def down_kernel(
    table, flags, got, leaf0, leaf1, store, here, send, tree, cs, bh, fl, sem
):
    chord, z, core = place()
    fetch = [
        pltpu.make_async_copy(store.at[level], tree.at[level], sem.at[level])
        for level in range(LEVELS)
    ]
    kinds = pltpu.make_async_copy(flags, fl, sem.at[LEVELS])
    for c in fetch[::-1]:
        c.start()
    kinds.start()
    lane = lane_iota()
    group = lane // 4
    for g in range(3):
        v = [got[s, 8 * g : 8 * g + 8, :] for s in range(16)]
        for bit in range(4):
            step = 1 << bit
            same = (group // step) % 2 == 0
            fresh = list(v)
            for s in range(16):
                if s & step:
                    continue
                a, b = v[s], v[s | step]
                fresh[s] = jnp.where(same, a, roll(b, 4 * step))
                fresh[s | step] = jnp.where(same, roll(a, -4 * step), b)
            v = fresh
        for lo in range(16):
            if 32 * g + lo < 85:
                cs[32 * g + lo] = v[lo]
            if 32 * g + 16 + lo < 85:
                cs[32 * g + 16 + lo] = roll(v[lo], 64)

    def chain(m, t, sign):
        for bit in range(4):
            step = 1 << bit
            ok = group >= step if sign > 0 else group < 16 - step
            far = [roll(x, sign * 4 * step) for x in t]
            t = [jnp.where(ok, new, old) for new, old in zip(mv(m, far, t), t)]
            if bit < 3:
                fm = [[roll(x, sign * 4 * step) for x in row] for row in m]
                new = mm(m, fm)
                m = [[jnp.where(ok, new[i][j], m[i][j]) for j in range(N)] for i in range(N)]
        return t

    zero = jnp.zeros((8, 128), F32)
    t = chain(square([cs[c] for c in range(25)]), [cs[25 + c] for c in range(N)], 1)
    a = [jnp.where(group >= 1, roll(x, 4), zero) for x in t]
    f = mv(square([cs[60 + c] for c in range(25)]), a, [cs[55 + c] for c in range(N)])
    t = chain(square([cs[30 + c] for c in range(25)]), f, -1)
    b = [jnp.where(group < 15, roll(x, -4), zero) for x in t]
    back = (128 - 4 * chord) % 128
    a = [pltpu.roll(x, back, 1) for x in a]
    b = [pltpu.roll(x, back, 1) for x in b]

    for level in range(5, -1, -1):
        dist = 2 << level
        fetch[level].wait()
        a_mid = mv(square([tree[level, c] for c in range(25)]), a, [tree[level, 25 + c] for c in range(N)])
        b_mid = mv(square([tree[level, 30 + c] for c in range(25)]), b, [tree[level, 55 + c] for c in range(N)])
        b_mid = mv(square([tree[level, 60 + c] for c in range(25)]), a_mid, b_mid)
        left = (lane // dist) % 2 == 0
        if level:
            a = [jnp.where(left, x, roll(y, dist)) for x, y in zip(a, a_mid)]
            b = [jnp.where(left, x, roll(y, dist)) for x, y in zip(b_mid, b)]
    even = lane % 2 == 0
    for r in range(2):
        if r == 0:
            ra = [jnp.where(left, x, roll(y, 2)) for x, y in zip(a, a_mid)]
            rb = [jnp.where(left, x, roll(y, 2)) for x, y in zip(b_mid, b)]
        else:
            ra = [jnp.where(left, roll(x, -2), y) for x, y in zip(a, a_mid)]
            rb = [jnp.where(left, roll(x, -2), y) for x, y in zip(b_mid, b)]

        def part(first, count):
            return [(leaf0, leaf1)[r][first + c] for c in range(count)]

        a1 = mv(square(part(0, 25)), ra, part(25, N))
        a2 = mv(square(part(30, 25)), a1, part(55, N))
        b2 = mv(square(part(85, 25)), rb, a2)
        b1 = mv(square(part(60, 25)), b2, a1)
        for c in range(N):
            bh[c, r, 0:8, :] = jnp.where(even, b1[c], roll(b2[c], 1))
            bh[c, r, 8:16, :] = jnp.where(even, roll(b1[c], -1), b2[c])

    kinds.wait()
    wall = (z == 0) & (core == 0)
    for half in range(2):
        kind = fl[8 * half : 8 * half + 8, :]
        for c in range(N):
            factor = zero
            for k in range(3):
                factor = jnp.where(kind == k, table[k, c], factor)
            row = bh[c, half, pl.ds(0, 8, stride=2), :]
            bh[c, half, pl.ds(0, 8, stride=2), :] = jnp.where(wall, factor, 1.0) * row
    for c in range(N):
        here[c] = bh[c, core]
        send[c] = bh[c, 1 - core]


def solve_kernel(got, back, turned, ain):
    for n in range(16 * ROWS // 8):
        turned[8 * n : 8 * n + 8, :] = pltpu.roll(got[8 * n : 8 * n + 8, :], 64, 1)

    def value(pair, c):
        odd = int(c > 37)
        c -= 37 * odd
        row = ROWS * (2 * pair + odd) + c % VEC
        return (turned if c >= VEC else got)[row : row + 1, :]

    def block(pair, first):
        return square([value(pair, first + c) for c in range(25)])

    def vec(pair, ref):
        row = 2 * ROWS * pair + VEC
        return [
            ref[row + c : row + c + 1, :] + ref[row + ROWS + c : row + ROWS + c + 1, :]
            for c in range(N)
        ]

    zero = jnp.zeros((1, 128), F32)
    for n in range(16):
        back[8 * n : 8 * n + 8, :] = jnp.zeros((8, 128), F32)
    a = [zero] * N
    for m in range(8):
        for c in range(N):
            ain[8 * m + c : 8 * m + c + 1, :] = a[c]
        if m < 7:
            a = mv(block(m, 0), a, vec(m, got)) if m else vec(m, got)
    first = lax.broadcasted_iota(jnp.int32, (1, 128), 1) < 64
    b = [zero] * N
    for m in range(7, -1, -1):
        a = [ain[8 * m + c : 8 * m + c + 1, :] for c in range(N)]
        for c in range(N):
            x = jnp.where(first, a[c], pltpu.roll(b[c], 64, 1))
            back[16 * m + c : 16 * m + c + 1, :] = x
            back[16 * m + 8 + c : 16 * m + 8 + c + 1, :] = x
        if m:
            f = mv(block(m, 50), a, vec(m, turned))
            b = mv(block(m, 25), b, f)


def finish_kernel(
    got, here, there, keep, recv, hold, taken, mine, other, own, send, sl, su, res, both, sem
):
    _, z, core = place()
    odd = z % 2
    even = odd == 0
    copies = eta_copies(keep, recv, sl, su, core, sem)
    pair = [
        pltpu.make_async_copy(mine, both.at[odd], sem.at[4]),
        pltpu.make_async_copy(other, both.at[1 - odd], sem.at[5]),
    ]
    for c in pair + copies:
        c.start()
    first = lane_iota() < 64
    a, b = [], []
    for c in range(N):
        x = got[pl.ds(c, 8, stride=8), :]
        y = got[pl.ds(64 + c, 8, stride=8), :]
        a.append(jnp.where(first, x, roll(y, 64)))
        b.append(jnp.where(first, roll(x, 64), y))
    for c in pair:
        c.wait()
    lv_e = [jnp.where(even, hold[c], taken[c]) for c in range(N)]
    mid = mv(square([both[0, c] for c in range(25)]), a, lv_e)
    low = mv(square([both[1, 50 + c] for c in range(25)]), mid, [taken[c] for c in range(N)])
    low = mv(square([both[1, 25 + c] for c in range(25)]), b, low)
    a = [jnp.where(even, x, y) for x, y in zip(a, mid)]
    b = [jnp.where(even, x, y) for x, y in zip(low, b)]
    for c in copies:
        c.wait()
    s = sources(here, there, res, core)
    lifted = []
    for j in range(4):
        a = mv(cell(sl, j), a, s[j])
        lifted.append(a)
    for j in range(3, -1, -1):
        b = mv(cell(su, j), b, lifted[j])
        for c in range(N):
            res[c, j // 2, pl.ds(j % 2, 8, stride=2), :] = b[c]
    for c in range(N):
        own[c] = res[c, core]
        send[c] = res[c, 1 - core]


def dma(n):
    return pltpu.SemaphoreType.DMA((n,))


def per_device(
    rhs, jet_mask, jet_source, wall_flags, bc_table, xi_lower, xi_upper, eta_lower, eta_upper
):
    def far(x, *dims):
        return pltpu.with_memory_space_constraint(x.reshape(dims), pltpu.HBM)

    rhs, mask, flags = far(rhs, N, 32, 128), far(jet_mask, 32, 128), far(wall_flags, 16, 128)
    xl, xu, el, eu = (far(x, 25, 32, 128) for x in (xi_lower, xi_upper, eta_lower, eta_upper))
    swap = [(n, n ^ 1) for n in range(lax.axis_size("wall"))]
    near = [(n, n ^ 2) for n in range(lax.axis_size("wall"))]
    groups = [list(range(c, lax.axis_size("wall"), 2)) for c in range(2)]

    def over_z(x):
        return lax.all_to_all(x, "wall", 0, 0, tiled=True, axis_index_groups=groups)

    side = pltpu.VMEM((25, 2, 16, 128), F32)
    cells = pltpu.VMEM((N, 2, 16, 128), F32)
    both = pltpu.VMEM((2, 75, 8, 128), F32)
    msg, send, keep, leaf0, leaf1, store = pl.pallas_call(
        up_kernel,
        out_shape=(
            shape(16, 24, 128),
            shape(50, 16, 128),
            shape(50, 16, 128),
            shape(110, 8, 128),
            shape(110, 8, 128),
            pltpu.HBM((LEVELS, 85, 8, 128), F32),
        ),
        in_specs=[HBM] * 7,
        out_specs=(VM, VM, VM, VM, VM, HBM),
        scratch_shapes=[
            pltpu.VMEM((LEVELS, 85, 8, 128), F32),
            pltpu.VMEM((25, 32, 128), F32),
            pltpu.VMEM((25, 32, 128), F32),
            pltpu.VMEM((N, 32, 128), F32),
            pltpu.VMEM((32, 128), jnp.int32),
            pltpu.SMEM((N,), F32),
            pltpu.VMEM((2, 85, 8, 128), F32),
            pltpu.VMEM((85, 8, 128), F32),
            dma(17),
        ],
        compiler_params=params(),
        cost_estimate=cost(9000 * 1024, 4 << 20),
        name="chord_up",
    )(far(jet_source, N), rhs, mask, xl, xu, el, eu)
    recv = lax.ppermute(send, "wall", swap)
    mine = pl.pallas_call(
        wall_kernel,
        out_shape=shape(75, 8, 128),
        in_specs=[ANY, ANY],
        out_specs=VM,
        scratch_shapes=[side, side, dma(4)],
        compiler_params=params(),
        cost_estimate=cost(3 * 250 * 3 * 1024, 2 << 20),
        name="wall_blocks",
    )(keep, recv)
    other = lax.ppermute(mine, "wall", near)
    got = lax.all_to_all(msg, "chord", 0, 0, tiled=True)
    here, away = pl.pallas_call(
        down_kernel,
        out_shape=(shape(N, 16, 128), shape(N, 16, 128)),
        in_specs=[SM, HBM, VM, VM, VM, HBM],
        out_specs=(VM, VM),
        scratch_shapes=[
            pltpu.VMEM((LEVELS, 85, 8, 128), F32),
            pltpu.VMEM((85, 8, 128), F32),
            cells,
            pltpu.VMEM((16, 128), jnp.int32),
            dma(7),
        ],
        compiler_params=params(),
        cost_estimate=cost(50_000_000_000, 4 << 20),
        name="chord_down",
    )(bc_table, flags, got, leaf0, leaf1, far(store, LEVELS, 85, 8, 128))
    there = lax.ppermute(away, "wall", swap)
    zmsg, give, hold = pl.pallas_call(
        pair_kernel,
        out_shape=(shape(16 * ROWS, 128), shape(N, 8, 128), shape(N, 8, 128)),
        in_specs=[VM, VM, ANY, ANY, ANY, ANY],
        out_specs=(VM, VM, VM),
        scratch_shapes=[side, side, cells, both, pltpu.VMEM((75, 8, 128), F32), dma(6)],
        compiler_params=params(),
        name="wall_pair",
    )(here, there, keep, recv, mine, other)
    zgot = over_z(zmsg.reshape(16, ROWS, 128)).reshape(16 * ROWS, 128)
    taken = lax.ppermute(give, "wall", near)
    back = pl.pallas_call(
        solve_kernel,
        out_shape=shape(128, 128),
        in_specs=[VM],
        out_specs=VM,
        scratch_shapes=[pltpu.VMEM((16 * ROWS, 128), F32), pltpu.VMEM((128, 128), F32)],
        compiler_params=params(),
        name="wall_solve",
    )(zgot)
    inflow = over_z(back.reshape(16, 8, 128)).reshape(128, 128)
    own, theirs = pl.pallas_call(
        finish_kernel,
        out_shape=(shape(N, 16, 128), shape(N, 16, 128)),
        in_specs=[VM, VM, VM, ANY, ANY, VM, VM, ANY, ANY],
        out_specs=(VM, VM),
        scratch_shapes=[side, side, cells, both, dma(6)],
        compiler_params=params(),
        name="finish",
    )(inflow, here, there, keep, recv, hold, taken, mine, other)
    theirs = lax.ppermute(theirs, "wall", swap)
    core = lax.axis_index("wall") % 2
    low = jnp.where(core == 0, own, theirs)
    high = jnp.where(core == 0, theirs, own)
    return jnp.concatenate([low, high], axis=1).reshape(N, 16, 2, 128)


def solution(mesh):
    placed = (
        P(None, None, "wall", "chord"),
        P(None, "wall", "chord"),
        P(),
        P(None, "chord"),
        P(),
        P(None, None, None, "wall", "chord"),
        P(None, None, None, "wall", "chord"),
        P(None, None, None, "wall", "chord"),
        P(None, None, None, "wall", "chord"),
    )
    return jax.shard_map(
        per_device,
        mesh=mesh,
        in_specs=placed,
        out_specs=P(None, None, "wall", "chord"),
        check_vma=False,
    )
```

```python
import jax
import jax.numpy as jnp
from jax import lax
from jax.experimental import pallas as pl
from jax.experimental.pallas import tpu as pltpu
from jax.sharding import PartitionSpec as P

F32 = jnp.float32
N = 5
ROWS = 32
VEC = 19
GIVE = 24
ANY = pl.BlockSpec(memory_space=pl.ANY)
HBM = pl.BlockSpec(memory_space=pltpu.HBM)
VM = pl.BlockSpec(memory_space=pltpu.VMEM)
SM = pl.BlockSpec(memory_space=pltpu.SMEM)
LIMIT = 32 << 20
LEVELS = 6


def shape(*dims):
    return jax.ShapeDtypeStruct(dims, F32)


def params(limit=LIMIT):
    return pltpu.CompilerParams(vmem_limit_bytes=limit)


def cost(flops, nbytes):
    return pl.CostEstimate(flops=flops, bytes_accessed=nbytes, transcendentals=0)


def square(flat):
    return [[flat[N * i + j] for j in range(N)] for i in range(N)]


def flat(m):
    return [x for row in m for x in row]


def dot(xs, ys, start=None):
    total = start
    for x, y in zip(xs, ys):
        total = x * y if total is None else total + x * y
    return total


def mm(a, b, c=None):
    cols = list(zip(*b))
    return [
        [dot(a[i], cols[j], None if c is None else c[i][j]) for j in range(N)] for i in range(N)
    ]


def mv(a, x, c=None):
    return [dot(a[i], x, None if c is None else c[i]) for i in range(N)]


def lane_iota():
    return lax.broadcasted_iota(jnp.int32, (8, 128), 1)


def roll(x, by):
    return pltpu.roll(x, by % 128, 1)


def place():
    wall = lax.axis_index("wall")
    return lax.axis_index("chord"), wall // 2, wall % 2


def copy_all(copies):
    for c in copies:
        c.start()
    for c in copies:
        c.wait()


def compose(left, right):
    lb1, lv1, ub1, uv1, w1 = left
    lb2, lv2, ub2, uv2, w2 = right
    lb = mm(lb2, lb1)
    lv = mv(lb2, lv1, lv2)
    ub = mm(ub1, ub2)
    uv = mv(ub1, mv(w2, lv1, uv2), uv1)
    w = mm(ub1, mm(w2, lb1), w1)
    return lb, lv, ub, uv, w


def node(values):
    return (
        square(values[0:25]),
        list(values[25:30]),
        square(values[30:55]),
        list(values[55:60]),
        square(values[60:85]),
    )


def values_of(n):
    return flat(n[0]) + list(n[1]) + flat(n[2]) + list(n[3]) + flat(n[4])


def up_kernel(
    jet, rhs, mask, xl, xu, el, eu, msg, send, keep, leaf0, leaf1, store,
    tree, sl, su, ss, mk, jt, n1, n2, sem,
):
    leaves = (leaf0, leaf1)
    core = place()[2]
    copies = [
        pltpu.make_async_copy(src, dst, sem.at[n])
        for n, (src, dst) in enumerate(((jet, jt), (mask, mk), (rhs, ss)))
    ]
    for r in range(2):
        rows = pl.ds(16 * r, 16)
        for n, (src, dst) in enumerate(((xl, sl), (xu, su))):
            at = sem.at[3 + 2 * r + n]
            copies.append(pltpu.make_async_copy(src.at[:, rows, :], dst.at[:, rows, :], at))
    for c in copies:
        c.start()
    for c in copies[:3]:
        c.wait()
    m = mk[...].astype(F32)
    for c in range(N):
        ss[c] = ss[c] + m * jt[c]
    moves = []
    for n, (dst, half) in enumerate(((send, 1 - core), (keep, core))):
        off = pl.multiple_of(half * 16, 16)
        for k, ref in enumerate((el, eu)):
            part = dst.at[pl.ds(25 * k, 25)]
            at = sem.at[7 + 2 * n + k]
            moves.append(pltpu.make_async_copy(ref.at[:, pl.ds(off, 16), :], part, at))
            moves[-1].start()
    lane = lane_iota()
    even = lane % 2 == 0
    low = (lane // 2) % 2 == 0

    def split(ref, c, r):
        a = ref[c, 16 * r : 16 * r + 8, :]
        b = ref[c, 16 * r + 8 : 16 * r + 16, :]
        return jnp.where(even, a, roll(b, 1)), jnp.where(even, roll(a, -1), b)

    for r in range(2):
        copies[3 + 2 * r].wait()
        copies[4 + 2 * r].wait()
        l1, l2 = zip(*[split(sl, c, r) for c in range(25)])
        v1, v2 = zip(*[split(ss, c, r) for c in range(N)])
        u1, u2 = zip(*[split(su, c, r) for c in range(25)])
        for c, x in enumerate(l1 + v1 + l2 + v2 + u1 + u2):
            leaves[r][c] = x
        l1, l2, u1, u2 = square(l1), square(l2), square(u1), square(u2)
        lb = mm(l2, l1)
        lv = mv(l2, v1, v2)
        out = (lb, lv, mm(u1, u2), mv(u1, lv, v1), mm(u1, lb, l1))
        for c, x in enumerate(values_of(out)):
            n1[r, c] = x

    left, right = [], []
    for c in range(85):
        a, b = n1[0, c], n1[1, c]
        left.append(jnp.where(low, a, roll(b, 2)))
        right.append(jnp.where(low, roll(a, -2), b))
    for level in range(LEVELS):
        if level:
            left = [n2[c] for c in range(85)]
            right = [roll(x, -(2 << level)) for x in left]
        for c in range(30):
            tree[level, c] = left[c]
        for c in range(30, 85):
            tree[level, c] = right[c]
        moves.append(pltpu.make_async_copy(tree.at[level], store.at[level], sem.at[11 + level]))
        moves[-1].start()
        for c, x in enumerate(values_of(compose(node(left), node(right)))):
            n2[c] = x
    group = lane // 4
    for g in range(3):
        acc = None
        for pos in range(min(32, 85 - 32 * g)):
            x = n2[32 * g + pos]
            acc = x if acc is None else jnp.where(group == pos, roll(x, 4 * pos), acc)
        for d in range(16):
            msg[d, 8 * g : 8 * g + 8, :] = acc
    for c in moves:
        c.wait()


def eta_copies(keep, recv, sl, su, core, sem):
    return [
        pltpu.make_async_copy(keep.at[pl.ds(0, 25)], sl.at[:, core], sem.at[0]),
        pltpu.make_async_copy(keep.at[pl.ds(25, 25)], su.at[:, core], sem.at[1]),
        pltpu.make_async_copy(recv.at[pl.ds(0, 25)], sl.at[:, 1 - core], sem.at[2]),
        pltpu.make_async_copy(recv.at[pl.ds(25, 25)], su.at[:, 1 - core], sem.at[3]),
    ]


def cell(ref, j):
    return square([ref[c, j // 2, pl.ds(j % 2, 8, stride=2), :] for c in range(25)])


def halves(x, y, first):
    return jnp.where(first, x, roll(y, 64)), jnp.where(first, roll(x, 64), y)


def wall_kernel(keep, recv, out, sl, su, sem):
    _, _, core = place()
    copy_all(eta_copies(keep, recv, sl, su, core, sem))
    lb = cell(sl, 0)
    w = lb
    ub = cell(su, 0)
    for j in range(1, 4):
        lb = mm(cell(sl, j), lb)
        w = mm(ub, lb, w)
        ub = mm(ub, cell(su, j))
    for c, x in enumerate(flat(lb) + flat(ub) + flat(w)):
        out[c] = x


def sources(here, there, slots, core):
    for c in range(N):
        slots[c, core] = here[c]
        slots[c, 1 - core] = there[c]
    return [
        [slots[c, j // 2, pl.ds(j % 2, 8, stride=2), :] for c in range(N)] for j in range(4)
    ]


def pair_kernel(
    here, there, keep, recv, mine, other, out, hold, sl, su, slots, both, comp, sem
):
    _, z, core = place()
    odd = z % 2
    even = odd == 0
    pair = [
        pltpu.make_async_copy(mine, both.at[odd], sem.at[4]),
        pltpu.make_async_copy(other, both.at[1 - odd], sem.at[5]),
    ]
    eta = eta_copies(keep, recv, sl, su, core, sem)
    for c in eta + pair:
        c.start()
    s = sources(here, there, slots, core)
    for c in eta:
        c.wait()
    t = [s[0]]
    for j in range(1, 4):
        t.append(mv(cell(sl, j), t[-1], s[j]))
    lv = t[3]
    uv = t[3]
    for j in range(2, -1, -1):
        uv = mv(cell(su, j), uv, t[j])
    for c in pair:
        c.wait()
    lb_e, ub_e, w_e = [square([both[0, 25 * n + c] for c in range(25)]) for n in range(3)]
    lb_o, ub_o, w_o = [square([both[1, 25 * n + c] for c in range(25)]) for n in range(3)]
    w = mm(ub_e, mm(w_o, lb_e), w_e)
    for c, x in enumerate(flat(mm(lb_o, lb_e)) + flat(mm(ub_e, ub_o)) + flat(w)):
        comp[c] = x
    give = [jnp.where(even, x, y) for x, y in zip(lv, uv)] + [lv[0]]
    for c in range(N):
        hold[c] = lv[c]
    new_lv = [jnp.where(even, x, y) for x, y in zip(mv(lb_o, lv), lv)]
    inner = [jnp.where(even, x, y) for x, y in zip(mv(w_o, lv), uv)]
    new_uv = [jnp.where(even, x + y, x) for x, y in zip(mv(ub_e, inner), uv)]
    first = lane_iota() < 64
    base = 37 * odd
    for r in range(GIVE + 3):
        if r < VEC:
            x, y = comp[base + r], comp[base + VEC + r]
        elif r < GIVE:
            x, y = new_lv[r - VEC], new_uv[r - VEC]
        else:
            x, y = give[2 * (r - GIVE)], give[2 * (r - GIVE) + 1]
        x, y = halves(x, y, first)
        out[pl.ds(r, 8, stride=ROWS), :] = x
        out[pl.ds(8 * ROWS + r, 8, stride=ROWS), :] = y


def down_kernel(
    table, flags, got, leaf0, leaf1, store, here, send, tree, cs, bh, fl, sem
):
    chord, z, core = place()
    fetch = [
        pltpu.make_async_copy(store.at[level], tree.at[level], sem.at[level])
        for level in range(LEVELS)
    ]
    kinds = pltpu.make_async_copy(flags, fl, sem.at[LEVELS])
    for c in fetch[::-1]:
        c.start()
    kinds.start()
    lane = lane_iota()
    group = lane // 4
    for g in range(3):
        v = [got[s, 8 * g : 8 * g + 8, :] for s in range(16)]
        for bit in range(4):
            step = 1 << bit
            same = (group // step) % 2 == 0
            fresh = list(v)
            for s in range(16):
                if s & step:
                    continue
                a, b = v[s], v[s | step]
                fresh[s] = jnp.where(same, a, roll(b, 4 * step))
                fresh[s | step] = jnp.where(same, roll(a, -4 * step), b)
            v = fresh
        for lo in range(16):
            if 32 * g + lo < 85:
                cs[32 * g + lo] = v[lo]
            if 32 * g + 16 + lo < 85:
                cs[32 * g + 16 + lo] = roll(v[lo], 64)

    def chain(m, t, sign):
        for bit in range(4):
            step = 1 << bit
            ok = group >= step if sign > 0 else group < 16 - step
            far = [roll(x, sign * 4 * step) for x in t]
            t = [jnp.where(ok, new, old) for new, old in zip(mv(m, far, t), t)]
            if bit < 3:
                fm = [[roll(x, sign * 4 * step) for x in row] for row in m]
                new = mm(m, fm)
                m = [[jnp.where(ok, new[i][j], m[i][j]) for j in range(N)] for i in range(N)]
        return t

    zero = jnp.zeros((8, 128), F32)
    t = chain(square([cs[c] for c in range(25)]), [cs[25 + c] for c in range(N)], 1)
    a = [jnp.where(group >= 1, roll(x, 4), zero) for x in t]
    f = mv(square([cs[60 + c] for c in range(25)]), a, [cs[55 + c] for c in range(N)])
    t = chain(square([cs[30 + c] for c in range(25)]), f, -1)
    b = [jnp.where(group < 15, roll(x, -4), zero) for x in t]
    back = (128 - 4 * chord) % 128
    a = [pltpu.roll(x, back, 1) for x in a]
    b = [pltpu.roll(x, back, 1) for x in b]

    for level in range(5, -1, -1):
        dist = 2 << level
        fetch[level].wait()
        a_mid = mv(square([tree[level, c] for c in range(25)]), a, [tree[level, 25 + c] for c in range(N)])
        b_mid = mv(square([tree[level, 30 + c] for c in range(25)]), b, [tree[level, 55 + c] for c in range(N)])
        b_mid = mv(square([tree[level, 60 + c] for c in range(25)]), a_mid, b_mid)
        left = (lane // dist) % 2 == 0
        if level:
            a = [jnp.where(left, x, roll(y, dist)) for x, y in zip(a, a_mid)]
            b = [jnp.where(left, x, roll(y, dist)) for x, y in zip(b_mid, b)]
    even = lane % 2 == 0
    for r in range(2):
        if r == 0:
            ra = [jnp.where(left, x, roll(y, 2)) for x, y in zip(a, a_mid)]
            rb = [jnp.where(left, x, roll(y, 2)) for x, y in zip(b_mid, b)]
        else:
            ra = [jnp.where(left, roll(x, -2), y) for x, y in zip(a, a_mid)]
            rb = [jnp.where(left, roll(x, -2), y) for x, y in zip(b_mid, b)]

        def part(first, count):
            return [(leaf0, leaf1)[r][first + c] for c in range(count)]

        a1 = mv(square(part(0, 25)), ra, part(25, N))
        a2 = mv(square(part(30, 25)), a1, part(55, N))
        b2 = mv(square(part(85, 25)), rb, a2)
        b1 = mv(square(part(60, 25)), b2, a1)
        for c in range(N):
            bh[c, r, 0:8, :] = jnp.where(even, b1[c], roll(b2[c], 1))
            bh[c, r, 8:16, :] = jnp.where(even, roll(b1[c], -1), b2[c])

    kinds.wait()
    wall = (z == 0) & (core == 0)
    for half in range(2):
        kind = fl[8 * half : 8 * half + 8, :]
        for c in range(N):
            factor = zero
            for k in range(3):
                factor = jnp.where(kind == k, table[k, c], factor)
            row = bh[c, half, pl.ds(0, 8, stride=2), :]
            bh[c, half, pl.ds(0, 8, stride=2), :] = jnp.where(wall, factor, 1.0) * row
    for c in range(N):
        here[c] = bh[c, core]
        send[c] = bh[c, 1 - core]


def solve_kernel(got, back, turned, ain):
    for n in range(16 * ROWS // 8):
        turned[8 * n : 8 * n + 8, :] = pltpu.roll(got[8 * n : 8 * n + 8, :], 64, 1)

    def value(pair, c):
        odd = int(c > 37)
        c -= 37 * odd
        row = ROWS * (2 * pair + odd) + c % VEC
        return (turned if c >= VEC else got)[row : row + 1, :]

    def block(pair, first):
        return square([value(pair, first + c) for c in range(25)])

    def vec(pair, ref):
        row = 2 * ROWS * pair + VEC
        return [
            ref[row + c : row + c + 1, :] + ref[row + ROWS + c : row + ROWS + c + 1, :]
            for c in range(N)
        ]

    zero = jnp.zeros((1, 128), F32)
    for z in range(16):
        row = ROWS * (z ^ 1) + GIVE
        back[8 * z + N : 8 * z + 8, :] = got[row : row + 3, :]
    a = [zero] * N
    for m in range(8):
        for c in range(N):
            ain[8 * m + c : 8 * m + c + 1, :] = a[c]
        if m < 7:
            a = mv(block(m, 0), a, vec(m, got)) if m else vec(m, got)
    first = lax.broadcasted_iota(jnp.int32, (1, 128), 1) < 64
    b = [zero] * N
    for m in range(7, -1, -1):
        a = [ain[8 * m + c : 8 * m + c + 1, :] for c in range(N)]
        for c in range(N):
            x = jnp.where(first, a[c], pltpu.roll(b[c], 64, 1))
            back[16 * m + c : 16 * m + c + 1, :] = x
            back[16 * m + 8 + c : 16 * m + 8 + c + 1, :] = x
        if m:
            f = mv(block(m, 50), a, vec(m, turned))
            b = mv(block(m, 25), b, f)


def finish_kernel(
    got, here, there, keep, recv, hold, mine, other, own, send, sl, su, res, both, sem
):
    _, z, core = place()
    odd = z % 2
    even = odd == 0
    copies = eta_copies(keep, recv, sl, su, core, sem)
    pair = [
        pltpu.make_async_copy(mine, both.at[odd], sem.at[4]),
        pltpu.make_async_copy(other, both.at[1 - odd], sem.at[5]),
    ]
    for c in pair + copies:
        c.start()
    first = lane_iota() < 64
    a, b, taken = [], [], []
    for c in range(8):
        x = got[pl.ds(c, 8, stride=8), :]
        y = got[pl.ds(64 + c, 8, stride=8), :]
        x, y = jnp.where(first, x, roll(y, 64)), jnp.where(first, roll(x, 64), y)
        if c < N:
            a.append(x)
            b.append(y)
        else:
            taken += [x, y]
    for c in pair:
        c.wait()
    lv_e = [jnp.where(even, hold[c], taken[c]) for c in range(N)]
    mid = mv(square([both[0, c] for c in range(25)]), a, lv_e)
    low = mv(square([both[1, 50 + c] for c in range(25)]), mid, taken[:N])
    low = mv(square([both[1, 25 + c] for c in range(25)]), b, low)
    a = [jnp.where(even, x, y) for x, y in zip(a, mid)]
    b = [jnp.where(even, x, y) for x, y in zip(low, b)]
    for c in copies:
        c.wait()
    s = sources(here, there, res, core)
    lifted = []
    for j in range(4):
        a = mv(cell(sl, j), a, s[j])
        lifted.append(a)
    for j in range(3, -1, -1):
        b = mv(cell(su, j), b, lifted[j])
        for c in range(N):
            res[c, j // 2, pl.ds(j % 2, 8, stride=2), :] = b[c]
    for c in range(N):
        own[c] = res[c, core]
        send[c] = res[c, 1 - core]


def join_kernel(own, theirs, out):
    core = place()[2]
    for half, ref in ((core, own), (1 - core, theirs)):
        off = pl.multiple_of(half * 16, 16)
        for c in range(N):
            out[c, pl.ds(off, 16), :] = ref[c]


def dma(n):
    return pltpu.SemaphoreType.DMA((n,))


def per_device(
    rhs, jet_mask, jet_source, wall_flags, bc_table, xi_lower, xi_upper, eta_lower, eta_upper
):
    def far(x, *dims):
        return pltpu.with_memory_space_constraint(x.reshape(dims), pltpu.HBM)

    rhs, mask, flags = far(rhs, N, 32, 128), far(jet_mask, 32, 128), far(wall_flags, 16, 128)
    xl, xu, el, eu = (far(x, 25, 32, 128) for x in (xi_lower, xi_upper, eta_lower, eta_upper))
    swap = [(n, n ^ 1) for n in range(lax.axis_size("wall"))]
    near = [(n, n ^ 2) for n in range(lax.axis_size("wall"))]
    groups = [list(range(c, lax.axis_size("wall"), 2)) for c in range(2)]

    def over_z(x):
        return lax.all_to_all(x, "wall", 0, 0, tiled=True, axis_index_groups=groups)

    side = pltpu.VMEM((25, 2, 16, 128), F32)
    cells = pltpu.VMEM((N, 2, 16, 128), F32)
    both = pltpu.VMEM((2, 75, 8, 128), F32)
    msg, send, keep, leaf0, leaf1, store = pl.pallas_call(
        up_kernel,
        out_shape=(
            shape(16, 24, 128),
            shape(50, 16, 128),
            shape(50, 16, 128),
            shape(110, 8, 128),
            shape(110, 8, 128),
            pltpu.HBM((LEVELS, 85, 8, 128), F32),
        ),
        in_specs=[HBM] * 7,
        out_specs=(VM, VM, VM, VM, VM, HBM),
        scratch_shapes=[
            pltpu.VMEM((LEVELS, 85, 8, 128), F32),
            pltpu.VMEM((25, 32, 128), F32),
            pltpu.VMEM((25, 32, 128), F32),
            pltpu.VMEM((N, 32, 128), F32),
            pltpu.VMEM((32, 128), jnp.int32),
            pltpu.SMEM((N,), F32),
            pltpu.VMEM((2, 85, 8, 128), F32),
            pltpu.VMEM((85, 8, 128), F32),
            dma(17),
        ],
        compiler_params=params(),
        cost_estimate=cost(9000 * 1024, 4 << 20),
        name="chord_up",
    )(far(jet_source, N), rhs, mask, xl, xu, el, eu)
    recv = lax.ppermute(send, "wall", swap)
    mine = pl.pallas_call(
        wall_kernel,
        out_shape=shape(75, 8, 128),
        in_specs=[ANY, ANY],
        out_specs=VM,
        scratch_shapes=[side, side, dma(4)],
        compiler_params=params(),
        cost_estimate=cost(3 * 250 * 3 * 1024, 2 << 20),
        name="wall_blocks",
    )(keep, recv)
    other = lax.ppermute(mine, "wall", near)
    got = lax.all_to_all(msg, "chord", 0, 0, tiled=True)
    here, away = pl.pallas_call(
        down_kernel,
        out_shape=(shape(N, 16, 128), shape(N, 16, 128)),
        in_specs=[SM, HBM, VM, VM, VM, HBM],
        out_specs=(VM, VM),
        scratch_shapes=[
            pltpu.VMEM((LEVELS, 85, 8, 128), F32),
            pltpu.VMEM((85, 8, 128), F32),
            cells,
            pltpu.VMEM((16, 128), jnp.int32),
            dma(7),
        ],
        compiler_params=params(),
        cost_estimate=cost(50_000_000_000, 4 << 20),
        name="chord_down",
    )(bc_table, flags, got, leaf0, leaf1, far(store, LEVELS, 85, 8, 128))
    there = lax.ppermute(away, "wall", swap)
    zmsg, hold = pl.pallas_call(
        pair_kernel,
        out_shape=(shape(16 * ROWS, 128), shape(N, 8, 128)),
        in_specs=[VM, VM, ANY, ANY, ANY, ANY],
        out_specs=(VM, VM),
        scratch_shapes=[side, side, cells, both, pltpu.VMEM((75, 8, 128), F32), dma(6)],
        compiler_params=params(),
        name="wall_pair",
    )(here, there, keep, recv, mine, other)
    zgot = over_z(zmsg.reshape(16, ROWS, 128)).reshape(16 * ROWS, 128)
    back = pl.pallas_call(
        solve_kernel,
        out_shape=shape(128, 128),
        in_specs=[VM],
        out_specs=VM,
        scratch_shapes=[pltpu.VMEM((16 * ROWS, 128), F32), pltpu.VMEM((128, 128), F32)],
        compiler_params=params(),
        name="wall_solve",
    )(zgot)
    inflow = over_z(back.reshape(16, 8, 128)).reshape(128, 128)
    own, theirs = pl.pallas_call(
        finish_kernel,
        out_shape=(shape(N, 16, 128), shape(N, 16, 128)),
        in_specs=[VM, VM, VM, ANY, ANY, VM, ANY, ANY],
        out_specs=(VM, VM),
        scratch_shapes=[side, side, cells, both, dma(6)],
        compiler_params=params(),
        name="finish",
    )(inflow, here, there, keep, recv, hold, mine, other)
    theirs = lax.ppermute(theirs, "wall", swap)
    out = pl.pallas_call(
        join_kernel,
        out_shape=shape(N, 32, 128),
        in_specs=[VM, VM],
        out_specs=VM,
        compiler_params=params(),
        name="join",
    )(own, theirs)
    return out.reshape(N, 16, 2, 128)


def solution(mesh):
    placed = (
        P(None, None, "wall", "chord"),
        P(None, "wall", "chord"),
        P(),
        P(None, "chord"),
        P(),
        P(None, None, None, "wall", "chord"),
        P(None, None, None, "wall", "chord"),
        P(None, None, None, "wall", "chord"),
        P(None, None, None, "wall", "chord"),
    )
    return jax.shard_map(
        per_device,
        mesh=mesh,
        in_specs=placed,
        out_specs=P(None, None, "wall", "chord"),
        check_vma=False,
    )
```

```python
import functools

import jax
import jax.numpy as jnp
from jax import lax
from jax.experimental import pallas as pl
from jax.experimental.pallas import tpu as pltpu
from jax.sharding import PartitionSpec as P

F32 = jnp.float32
N = 5
ROWS = 24
VEC = 19
ANY = pl.BlockSpec(memory_space=pl.ANY)
HBM = pl.BlockSpec(memory_space=pltpu.HBM)
VM = pl.BlockSpec(memory_space=pltpu.VMEM)
LIMIT = 32 << 20
LEVELS = 6


def shape(*dims):
    return jax.ShapeDtypeStruct(dims, F32)


def params(limit=LIMIT):
    return pltpu.CompilerParams(vmem_limit_bytes=limit)


def cost(flops, nbytes):
    return pl.CostEstimate(flops=flops, bytes_accessed=nbytes, transcendentals=0)


def square(flat):
    return [[flat[N * i + j] for j in range(N)] for i in range(N)]


def flat(m):
    return [x for row in m for x in row]


def dot(xs, ys, start=None):
    total = start
    for x, y in zip(xs, ys):
        total = x * y if total is None else total + x * y
    return total


def mm(a, b, c=None):
    cols = list(zip(*b))
    return [
        [dot(a[i], cols[j], None if c is None else c[i][j]) for j in range(N)] for i in range(N)
    ]


def mv(a, x, c=None):
    return [dot(a[i], x, None if c is None else c[i]) for i in range(N)]


def lane_iota():
    return lax.broadcasted_iota(jnp.int32, (8, 128), 1)


def roll(x, by):
    return pltpu.roll(x, by % 128, 1)


def place():
    wall = lax.axis_index("wall")
    return lax.axis_index("chord"), wall // 2, wall % 2


def copy_all(copies):
    for c in copies:
        c.start()
    for c in copies:
        c.wait()


def pack_kernel(away, jet, rhs, mask, xl, xu, el, eu, dst, rv, mk, jt, sem):
    core = place()[2]
    off = pl.multiple_of((1 - core if away else core) * 16, 16)
    copies = [
        pltpu.make_async_copy(jet, jt, sem.at[4]),
        pltpu.make_async_copy(rhs.at[:, pl.ds(off, 16), :], rv, sem.at[5]),
        pltpu.make_async_copy(mask.at[pl.ds(off, 16), :], mk, sem.at[6]),
    ]
    for n, ref in enumerate((xl, xu, el, eu)):
        part = dst.at[pl.ds(25 * n, 25)]
        copies.append(pltpu.make_async_copy(ref.at[:, pl.ds(off, 16), :], part, sem.at[n]))
    for c in copies:
        c.start()
    for c in copies[:3]:
        c.wait()
    m = mk[...].astype(F32)
    for c in range(N):
        dst[100 + c] = rv[c] + m * jt[c]
    for c in copies[3:]:
        c.wait()


def compose(left, right):
    lb1, lv1, ub1, uv1, w1 = left
    lb2, lv2, ub2, uv2, w2 = right
    lb = mm(lb2, lb1)
    lv = mv(lb2, lv1, lv2)
    ub = mm(ub1, ub2)
    uv = mv(ub1, mv(w2, lv1, uv2), uv1)
    w = mm(ub1, mm(w2, lb1), w1)
    return lb, lv, ub, uv, w


def node(values):
    return (
        square(values[0:25]),
        list(values[25:30]),
        square(values[30:55]),
        list(values[55:60]),
        square(values[60:85]),
    )


def values_of(n):
    return flat(n[0]) + list(n[1]) + flat(n[2]) + list(n[3]) + flat(n[4])


def up_kernel(keep, recv, msg, leaf0, leaf1, store, sl, su, ss, n1, n2, tree, sem):
    _, _, core = place()
    copies = []
    for n, (dst, first, count) in enumerate(((sl, 0, 25), (su, 25, 25), (ss, 100, N))):
        part = pl.ds(first, count)
        copies.append(pltpu.make_async_copy(keep.at[part], dst.at[:, core], sem.at[2 * n]))
        copies.append(pltpu.make_async_copy(recv.at[part], dst.at[:, 1 - core], sem.at[2 * n + 1]))
    copy_all(copies)
    lane = lane_iota()
    even = lane % 2 == 0
    low = (lane // 2) % 2 == 0

    def split(ref, c, r):
        a = ref[c, r, 0:8, :]
        b = ref[c, r, 8:16, :]
        return jnp.where(even, a, roll(b, 1)), jnp.where(even, roll(a, -1), b)

    saves = []
    for r in range(2):
        l1, l2 = zip(*[split(sl, c, r) for c in range(25)])
        v1, v2 = zip(*[split(ss, c, r) for c in range(N)])
        u1, u2 = zip(*[split(su, c, r) for c in range(25)])
        for c, x in enumerate(l1 + v1 + l2 + v2 + u1 + u2):
            (leaf0, leaf1)[r][c] = x
        l1, l2, u1, u2 = square(l1), square(l2), square(u1), square(u2)
        lb = mm(l2, l1)
        lv = mv(l2, v1, v2)
        out = (lb, lv, mm(u1, u2), mv(u1, lv, v1), mm(u1, lb, l1))
        for c, x in enumerate(values_of(out)):
            n1[r, c] = x

    left, right = [], []
    for c in range(85):
        a, b = n1[0, c], n1[1, c]
        left.append(jnp.where(low, a, roll(b, 2)))
        right.append(jnp.where(low, roll(a, -2), b))
    for level in range(6):
        if level:
            left = [n2[c] for c in range(85)]
            right = [roll(x, -(2 << level)) for x in left]
        for c in range(30):
            tree[level, c] = left[c]
        for c in range(30, 85):
            tree[level, c] = right[c]
        saves.append(pltpu.make_async_copy(tree.at[level], store.at[level], sem.at[6 + level]))
        saves[-1].start()
        for c, x in enumerate(values_of(compose(node(left), node(right)))):
            n2[c] = x
    group = lane // 4
    for g in range(3):
        acc = None
        for pos in range(min(32, 85 - 32 * g)):
            x = n2[32 * g + pos]
            acc = x if acc is None else jnp.where(group == pos, roll(x, 4 * pos), acc)
        for d in range(16):
            msg[d, 8 * g : 8 * g + 8, :] = acc
    for c in saves:
        c.wait()


def eta_copies(keep, recv, sl, su, core, sem):
    return [
        pltpu.make_async_copy(keep.at[pl.ds(50, 25)], sl.at[:, core], sem.at[0]),
        pltpu.make_async_copy(keep.at[pl.ds(75, 25)], su.at[:, core], sem.at[1]),
        pltpu.make_async_copy(recv.at[pl.ds(50, 25)], sl.at[:, 1 - core], sem.at[2]),
        pltpu.make_async_copy(recv.at[pl.ds(75, 25)], su.at[:, 1 - core], sem.at[3]),
    ]


def cell(ref, j):
    return square([ref[c, j // 2, pl.ds(j % 2, 8, stride=2), :] for c in range(25)])


def halves(x, y, first):
    return jnp.where(first, x, roll(y, 64)), jnp.where(first, roll(x, 64), y)


def wall_kernel(keep, recv, out, sl, su, sem):
    _, _, core = place()
    copy_all(eta_copies(keep, recv, sl, su, core, sem))
    lb = cell(sl, 0)
    w = lb
    ub = cell(su, 0)
    for j in range(1, 4):
        lb = mm(cell(sl, j), lb)
        w = mm(ub, lb, w)
        ub = mm(ub, cell(su, j))
    for c, x in enumerate(flat(lb) + flat(ub) + flat(w)):
        out[c] = x


def pair_copies(mine, other, both, odd, sem):
    return [
        pltpu.make_async_copy(mine, both.at[odd], sem.at[0]),
        pltpu.make_async_copy(other, both.at[1 - odd], sem.at[1]),
    ]


def pair_kernel(vecs, mine, other, out, give, both, comp, sem):
    _, z, _ = place()
    odd = z % 2
    even = odd == 0
    copy_all(pair_copies(mine, other, both, odd, sem))
    lb_e, ub_e, w_e = [square([both[0, 25 * n + c] for c in range(25)]) for n in range(3)]
    lb_o, ub_o, w_o = [square([both[1, 25 * n + c] for c in range(25)]) for n in range(3)]
    w = mm(ub_e, mm(w_o, lb_e), w_e)
    for c, x in enumerate(flat(mm(lb_o, lb_e)) + flat(mm(ub_e, ub_o)) + flat(w)):
        comp[c] = x
    lv = [vecs[c] for c in range(N)]
    uv = [vecs[N + c] for c in range(N)]
    for c in range(N):
        give[c] = jnp.where(even, lv[c], uv[c])
    new_lv = [jnp.where(even, x, y) for x, y in zip(mv(lb_o, lv), lv)]
    inner = [jnp.where(even, x, y) for x, y in zip(mv(w_o, lv), uv)]
    new_uv = [jnp.where(even, x + y, x) for x, y in zip(mv(ub_e, inner), uv)]
    first = lane_iota() < 64
    base = 37 * odd
    for r in range(ROWS):
        if r < VEC:
            x, y = comp[base + r], comp[base + VEC + r]
        else:
            x, y = new_lv[r - VEC], new_uv[r - VEC]
        x, y = halves(x, y, first)
        out[pl.ds(r, 8, stride=ROWS), :] = x
        out[pl.ds(8 * ROWS + r, 8, stride=ROWS), :] = y


def down_kernel(
    table, flags, got, leaf0, leaf1, store, keep, recv, scaled, vecs,
    sl, su, tree, cs, bh, fl, tb, sem,
):
    chord, z, core = place()
    eta = eta_copies(keep, recv, sl, su, core, sem)
    fetch = [
        pltpu.make_async_copy(store.at[level], tree.at[level], sem.at[4 + level])
        for level in range(LEVELS)
    ]
    kinds = [
        pltpu.make_async_copy(flags, fl, sem.at[4 + LEVELS]),
        pltpu.make_async_copy(table, tb, sem.at[5 + LEVELS]),
    ]
    for c in fetch[::-1] + kinds + eta:
        c.start()
    lane = lane_iota()
    group = lane // 4
    for g in range(3):
        v = [got[s, 8 * g : 8 * g + 8, :] for s in range(16)]
        for bit in range(4):
            step = 1 << bit
            same = (group // step) % 2 == 0
            fresh = list(v)
            for s in range(16):
                if s & step:
                    continue
                a, b = v[s], v[s | step]
                fresh[s] = jnp.where(same, a, roll(b, 4 * step))
                fresh[s | step] = jnp.where(same, roll(a, -4 * step), b)
            v = fresh
        for lo in range(16):
            if 32 * g + lo < 85:
                cs[32 * g + lo] = v[lo]
            if 32 * g + 16 + lo < 85:
                cs[32 * g + 16 + lo] = roll(v[lo], 64)

    def chain(m, t, sign):
        for bit in range(4):
            step = 1 << bit
            ok = group >= step if sign > 0 else group < 16 - step
            far = [roll(x, sign * 4 * step) for x in t]
            t = [jnp.where(ok, new, old) for new, old in zip(mv(m, far, t), t)]
            if bit < 3:
                fm = [[roll(x, sign * 4 * step) for x in row] for row in m]
                new = mm(m, fm)
                m = [[jnp.where(ok, new[i][j], m[i][j]) for j in range(N)] for i in range(N)]
        return t

    zero = jnp.zeros((8, 128), F32)
    t = chain(square([cs[c] for c in range(25)]), [cs[25 + c] for c in range(N)], 1)
    a = [jnp.where(group >= 1, roll(x, 4), zero) for x in t]
    f = mv(square([cs[60 + c] for c in range(25)]), a, [cs[55 + c] for c in range(N)])
    t = chain(square([cs[30 + c] for c in range(25)]), f, -1)
    b = [jnp.where(group < 15, roll(x, -4), zero) for x in t]
    back = (128 - 4 * chord) % 128
    a = [pltpu.roll(x, back, 1) for x in a]
    b = [pltpu.roll(x, back, 1) for x in b]

    for level in range(5, -1, -1):
        dist = 2 << level
        fetch[level].wait()
        a_mid = mv(square([tree[level, c] for c in range(25)]), a, [tree[level, 25 + c] for c in range(N)])
        b_mid = mv(square([tree[level, 30 + c] for c in range(25)]), b, [tree[level, 55 + c] for c in range(N)])
        b_mid = mv(square([tree[level, 60 + c] for c in range(25)]), a_mid, b_mid)
        left = (lane // dist) % 2 == 0
        if level:
            a = [jnp.where(left, x, roll(y, dist)) for x, y in zip(a, a_mid)]
            b = [jnp.where(left, x, roll(y, dist)) for x, y in zip(b_mid, b)]
    even = lane % 2 == 0
    for r in range(2):
        if r == 0:
            ra = [jnp.where(left, x, roll(y, 2)) for x, y in zip(a, a_mid)]
            rb = [jnp.where(left, x, roll(y, 2)) for x, y in zip(b_mid, b)]
        else:
            ra = [jnp.where(left, roll(x, -2), y) for x, y in zip(a, a_mid)]
            rb = [jnp.where(left, roll(x, -2), y) for x, y in zip(b_mid, b)]

        def part(first, count):
            return [(leaf0, leaf1)[r][first + c] for c in range(count)]

        a1 = mv(square(part(0, 25)), ra, part(25, N))
        a2 = mv(square(part(30, 25)), a1, part(55, N))
        b2 = mv(square(part(85, 25)), rb, a2)
        b1 = mv(square(part(60, 25)), b2, a1)
        for c in range(N):
            bh[c, r, 0:8, :] = jnp.where(even, b1[c], roll(b2[c], 1))
            bh[c, r, 8:16, :] = jnp.where(even, roll(b1[c], -1), b2[c])

    for c in kinds:
        c.wait()
    kind = fl[pl.ds(pl.multiple_of(core * 8, 8), 8), :]
    s = []
    for j in range(4):
        s.append([bh[c, j // 2, pl.ds(j % 2, 8, stride=2), :] for c in range(N)])
    for c in range(N):
        factor = zero
        for k in range(3):
            factor = jnp.where(kind == k, tb[k : k + 1, c : c + 1], factor)
        s[0][c] = jnp.where(z == 0, factor, 1.0) * s[0][c]
    for j in range(4):
        for c in range(N):
            scaled[j, c] = s[j][c]
    for c in eta:
        c.wait()
    t = [s[0]]
    for j in range(1, 4):
        t.append(mv(cell(sl, j), t[-1], s[j]))
    u = t[3]
    for j in range(2, -1, -1):
        u = mv(cell(su, j), u, t[j])
    for c in range(N):
        vecs[c] = t[3][c]
        vecs[N + c] = u[c]


def solve_kernel(got, back, turned, ain):
    for n in range(16 * ROWS // 8):
        turned[8 * n : 8 * n + 8, :] = pltpu.roll(got[8 * n : 8 * n + 8, :], 64, 1)

    def value(pair, c):
        odd = int(c > 37)
        c -= 37 * odd
        row = ROWS * (2 * pair + odd) + c % VEC
        return (turned if c >= VEC else got)[row : row + 1, :]

    def block(pair, first):
        return square([value(pair, first + c) for c in range(25)])

    def vec(pair, ref):
        row = 2 * ROWS * pair + VEC
        return [
            ref[row + c : row + c + 1, :] + ref[row + ROWS + c : row + ROWS + c + 1, :]
            for c in range(N)
        ]

    zero = jnp.zeros((1, 128), F32)
    for n in range(16):
        back[8 * n : 8 * n + 8, :] = jnp.zeros((8, 128), F32)
    a = [zero] * N
    for m in range(8):
        for c in range(N):
            ain[8 * m + c : 8 * m + c + 1, :] = a[c]
        if m < 7:
            a = mv(block(m, 0), a, vec(m, got)) if m else vec(m, got)
    first = lax.broadcasted_iota(jnp.int32, (1, 128), 1) < 64
    b = [zero] * N
    for m in range(7, -1, -1):
        a = [ain[8 * m + c : 8 * m + c + 1, :] for c in range(N)]
        for c in range(N):
            x = jnp.where(first, a[c], pltpu.roll(b[c], 64, 1))
            back[16 * m + c : 16 * m + c + 1, :] = x
            back[16 * m + 8 + c : 16 * m + 8 + c + 1, :] = x
        if m:
            f = mv(block(m, 50), a, vec(m, turned))
            b = mv(block(m, 25), b, f)


def finish_kernel(
    got, scaled, keep, recv, vecs, taken, mine, other, own, send, sl, su, res, both, sem
):
    _, z, core = place()
    odd = z % 2
    even = odd == 0
    copies = eta_copies(keep, recv, sl, su, core, sem)
    pair = [
        pltpu.make_async_copy(mine, both.at[odd], sem.at[4]),
        pltpu.make_async_copy(other, both.at[1 - odd], sem.at[5]),
    ]
    for c in pair + copies:
        c.start()
    first = lane_iota() < 64
    a, b = [], []
    for c in range(N):
        x = got[pl.ds(c, 8, stride=8), :]
        y = got[pl.ds(64 + c, 8, stride=8), :]
        a.append(jnp.where(first, x, roll(y, 64)))
        b.append(jnp.where(first, roll(x, 64), y))
    for c in pair:
        c.wait()
    lv_e = [jnp.where(even, vecs[c], taken[c]) for c in range(N)]
    mid = mv(square([both[0, c] for c in range(25)]), a, lv_e)
    low = mv(square([both[1, 50 + c] for c in range(25)]), mid, [taken[c] for c in range(N)])
    low = mv(square([both[1, 25 + c] for c in range(25)]), b, low)
    a = [jnp.where(even, x, y) for x, y in zip(a, mid)]
    b = [jnp.where(even, x, y) for x, y in zip(low, b)]
    for c in copies:
        c.wait()
    lifted = []
    for j in range(4):
        a = mv(cell(sl, j), a, [scaled[j, c] for c in range(N)])
        lifted.append(a)
    for j in range(3, -1, -1):
        b = mv(cell(su, j), b, lifted[j])
        for c in range(N):
            res[c, j // 2, pl.ds(j % 2, 8, stride=2), :] = b[c]
    for c in range(N):
        own[c] = res[c, core]
        send[c] = res[c, 1 - core]


def dma(n):
    return pltpu.SemaphoreType.DMA((n,))


def per_device(
    rhs, jet_mask, jet_source, wall_flags, bc_table, xi_lower, xi_upper, eta_lower, eta_upper
):
    def far(x, *dims):
        return pltpu.with_memory_space_constraint(x.reshape(dims), pltpu.HBM)

    rhs, mask, flags = far(rhs, N, 32, 128), far(jet_mask, 32, 128), far(wall_flags, 16, 128)
    xl, xu, el, eu = (far(x, 25, 32, 128) for x in (xi_lower, xi_upper, eta_lower, eta_upper))
    swap = [(n, n ^ 1) for n in range(lax.axis_size("wall"))]
    near = [(n, n ^ 2) for n in range(lax.axis_size("wall"))]
    groups = [list(range(c, lax.axis_size("wall"), 2)) for c in range(2)]

    def over_z(x):
        return lax.all_to_all(x, "wall", 0, 0, tiled=True, axis_index_groups=groups)

    side = pltpu.VMEM((25, 2, 16, 128), F32)
    def pack(away):
        return pl.pallas_call(
            functools.partial(pack_kernel, away),
            out_shape=shape(105, 16, 128),
            in_specs=[HBM] * 7,
            out_specs=VM,
            scratch_shapes=[
                pltpu.VMEM((N, 16, 128), F32),
                pltpu.VMEM((16, 128), jnp.int32),
                pltpu.SMEM((N,), F32),
                dma(7),
            ],
            compiler_params=params(),
            cost_estimate=cost(0, 2 << 20),
            name="pack_away" if away else "pack_here",
        )(far(jet_source, N), rhs, mask, xl, xu, el, eu)

    recv = lax.ppermute(pack(True), "wall", swap)
    keep = pack(False)
    msg, leaf0, leaf1, store = pl.pallas_call(
        up_kernel,
        out_shape=(
            shape(16, 24, 128),
            shape(110, 8, 128),
            shape(110, 8, 128),
            pltpu.HBM((LEVELS, 85, 8, 128), F32),
        ),
        in_specs=[ANY, ANY],
        out_specs=(VM, VM, VM, HBM),
        scratch_shapes=[
            side,
            side,
            pltpu.VMEM((N, 2, 16, 128), F32),
            pltpu.VMEM((2, 85, 8, 128), F32),
            pltpu.VMEM((85, 8, 128), F32),
            pltpu.VMEM((LEVELS, 85, 8, 128), F32),
            dma(12),
        ],
        compiler_params=params(),
        cost_estimate=cost(9000 * 1024, 4 << 20),
        name="chord_up",
    )(keep, recv)
    mine = pl.pallas_call(
        wall_kernel,
        out_shape=shape(75, 8, 128),
        in_specs=[ANY, ANY],
        out_specs=VM,
        scratch_shapes=[side, side, dma(4)],
        compiler_params=params(),
        cost_estimate=cost(3 * 250 * 3 * 1024, 2 << 20),
        name="wall_blocks",
    )(keep, recv)
    other = lax.ppermute(mine, "wall", near)
    got = lax.all_to_all(msg, "chord", 0, 0, tiled=True)
    scaled, vecs = pl.pallas_call(
        down_kernel,
        out_shape=(shape(4, N, 8, 128), shape(2 * N, 8, 128)),
        in_specs=[HBM, HBM, VM, VM, VM, HBM, ANY, ANY],
        out_specs=(VM, VM),
        scratch_shapes=[
            side,
            side,
            pltpu.VMEM((LEVELS, 85, 8, 128), F32),
            pltpu.VMEM((85, 8, 128), F32),
            pltpu.VMEM((N, 2, 16, 128), F32),
            pltpu.VMEM((16, 128), jnp.int32),
            pltpu.VMEM((3, N), F32),
            dma(12),
        ],
        compiler_params=params(),
        cost_estimate=cost(50_000_000_000, 4 << 20),
        name="chord_down",
    )(far(bc_table, 3, N), flags, got, leaf0, leaf1, far(store, LEVELS, 85, 8, 128), keep, recv)
    both = pltpu.VMEM((2, 75, 8, 128), F32)
    zmsg, give = pl.pallas_call(
        pair_kernel,
        out_shape=(shape(16 * ROWS, 128), shape(N, 8, 128)),
        in_specs=[VM, ANY, ANY],
        out_specs=(VM, VM),
        scratch_shapes=[both, pltpu.VMEM((75, 8, 128), F32), dma(2)],
        compiler_params=params(),
        name="wall_pair",
    )(vecs, mine, other)
    zgot = over_z(zmsg.reshape(16, ROWS, 128)).reshape(16 * ROWS, 128)
    taken = lax.ppermute(give, "wall", near)
    back = pl.pallas_call(
        solve_kernel,
        out_shape=shape(128, 128),
        in_specs=[VM],
        out_specs=VM,
        scratch_shapes=[pltpu.VMEM((16 * ROWS, 128), F32), pltpu.VMEM((128, 128), F32)],
        compiler_params=params(),
        name="wall_solve",
    )(zgot)
    inflow = over_z(back.reshape(16, 8, 128)).reshape(128, 128)
    own, theirs = pl.pallas_call(
        finish_kernel,
        out_shape=(shape(N, 16, 128), shape(N, 16, 128)),
        in_specs=[VM, VM, ANY, ANY, VM, VM, ANY, ANY],
        out_specs=(VM, VM),
        scratch_shapes=[side, side, pltpu.VMEM((N, 2, 16, 128), F32), both, dma(6)],
        compiler_params=params(),
        name="finish",
    )(inflow, scaled, keep, recv, vecs, taken, mine, other)
    theirs = lax.ppermute(theirs, "wall", swap)
    core = lax.axis_index("wall") % 2
    low = jnp.where(core == 0, own, theirs)
    high = jnp.where(core == 0, theirs, own)
    return jnp.concatenate([low, high], axis=1).reshape(N, 16, 2, 128)


def solution(mesh):
    placed = (
        P(None, None, "wall", "chord"),
        P(None, "wall", "chord"),
        P(),
        P(None, "chord"),
        P(),
        P(None, None, None, "wall", "chord"),
        P(None, None, None, "wall", "chord"),
        P(None, None, None, "wall", "chord"),
        P(None, None, None, "wall", "chord"),
    )
    return jax.shard_map(
        per_device,
        mesh=mesh,
        in_specs=placed,
        out_specs=P(None, None, "wall", "chord"),
        check_vma=False,
    )
```

```python
import functools

import jax
import jax.numpy as jnp
from jax import lax
from jax.experimental import pallas as pl
from jax.experimental.pallas import tpu as pltpu
from jax.sharding import PartitionSpec as P

F32 = jnp.float32
N = 5
ROWS = 24
VEC = 19
ANY = pl.BlockSpec(memory_space=pl.ANY)
HBM = pl.BlockSpec(memory_space=pltpu.HBM)
VM = pl.BlockSpec(memory_space=pltpu.VMEM)
LIMIT = 32 << 20
LEVELS = 6


def shape(*dims):
    return jax.ShapeDtypeStruct(dims, F32)


def params(limit=LIMIT):
    return pltpu.CompilerParams(vmem_limit_bytes=limit)


def cost(flops, nbytes):
    return pl.CostEstimate(flops=flops, bytes_accessed=nbytes, transcendentals=0)


def square(flat):
    return [[flat[N * i + j] for j in range(N)] for i in range(N)]


def flat(m):
    return [x for row in m for x in row]


def dot(xs, ys, start=None):
    total = start
    for x, y in zip(xs, ys):
        total = x * y if total is None else total + x * y
    return total


def mm(a, b, c=None):
    cols = list(zip(*b))
    return [
        [dot(a[i], cols[j], None if c is None else c[i][j]) for j in range(N)] for i in range(N)
    ]


def mv(a, x, c=None):
    return [dot(a[i], x, None if c is None else c[i]) for i in range(N)]


def lane_iota():
    return lax.broadcasted_iota(jnp.int32, (8, 128), 1)


def roll(x, by):
    return pltpu.roll(x, by % 128, 1)


def place():
    wall = lax.axis_index("wall")
    return lax.axis_index("chord"), wall // 2, wall % 2


def copy_all(copies):
    for c in copies:
        c.start()
    for c in copies:
        c.wait()


def pack_kernel(away, jet, rhs, mask, xl, xu, el, eu, dst, rv, mk, jt, sem):
    core = place()[2]
    off = pl.multiple_of((1 - core if away else core) * 16, 16)
    copies = [
        pltpu.make_async_copy(jet, jt, sem.at[20]),
        pltpu.make_async_copy(rhs.at[:, pl.ds(off, 16), :], rv, sem.at[21]),
        pltpu.make_async_copy(mask.at[pl.ds(off, 16), :], mk, sem.at[22]),
    ]
    for n in range(20):
        ref = (xl, xu, el, eu)[n // 5]
        part = ref.at[pl.ds(N * (n % 5), N), pl.ds(off, 16), :]
        copies.append(pltpu.make_async_copy(part, dst.at[pl.ds(N * n, N)], sem.at[n]))
    for c in copies:
        c.start()
    for c in copies[:3]:
        c.wait()
    m = mk[...].astype(F32)
    for c in range(N):
        dst[100 + c] = rv[c] + m * jt[c]
    for c in copies[3:]:
        c.wait()


def compose(left, right):
    lb1, lv1, ub1, uv1, w1 = left
    lb2, lv2, ub2, uv2, w2 = right
    lb = mm(lb2, lb1)
    lv = mv(lb2, lv1, lv2)
    ub = mm(ub1, ub2)
    uv = mv(ub1, mv(w2, lv1, uv2), uv1)
    w = mm(ub1, mm(w2, lb1), w1)
    return lb, lv, ub, uv, w


def node(values):
    return (
        square(values[0:25]),
        list(values[25:30]),
        square(values[30:55]),
        list(values[55:60]),
        square(values[60:85]),
    )


def values_of(n):
    return flat(n[0]) + list(n[1]) + flat(n[2]) + list(n[3]) + flat(n[4])


def up_kernel(keep, recv, msg, leaf0, leaf1, store, n1, n2, tree, sem):
    core = place()[2]
    lane = lane_iota()
    even = lane % 2 == 0
    low = (lane // 2) % 2 == 0

    def split(c, r):
        stays = core == r
        a = jnp.where(stays, keep[c, 0:8, :], recv[c, 0:8, :])
        b = jnp.where(stays, keep[c, 8:16, :], recv[c, 8:16, :])
        return jnp.where(even, a, roll(b, 1)), jnp.where(even, roll(a, -1), b)

    saves = []
    for r in range(2):
        l1, l2 = zip(*[split(c, r) for c in range(25)])
        v1, v2 = zip(*[split(100 + c, r) for c in range(N)])
        u1, u2 = zip(*[split(25 + c, r) for c in range(25)])
        for c, x in enumerate(l1 + v1 + l2 + v2 + u1 + u2):
            (leaf0, leaf1)[r][c] = x
        l1, l2, u1, u2 = square(l1), square(l2), square(u1), square(u2)
        lb = mm(l2, l1)
        lv = mv(l2, v1, v2)
        out = (lb, lv, mm(u1, u2), mv(u1, lv, v1), mm(u1, lb, l1))
        for c, x in enumerate(values_of(out)):
            n1[r, c] = x

    left, right = [], []
    for c in range(85):
        a, b = n1[0, c], n1[1, c]
        left.append(jnp.where(low, a, roll(b, 2)))
        right.append(jnp.where(low, roll(a, -2), b))
    for level in range(6):
        if level:
            left = [n2[c] for c in range(85)]
            right = [roll(x, -(2 << level)) for x in left]
        for c in range(30):
            tree[level, c] = left[c]
        for c in range(30, 85):
            tree[level, c] = right[c]
        saves.append(pltpu.make_async_copy(tree.at[level], store.at[level], sem.at[level]))
        saves[-1].start()
        for c, x in enumerate(values_of(compose(node(left), node(right)))):
            n2[c] = x
    group = lane // 4
    for g in range(3):
        acc = None
        for pos in range(min(32, 85 - 32 * g)):
            x = n2[32 * g + pos]
            acc = x if acc is None else jnp.where(group == pos, roll(x, 4 * pos), acc)
        for d in range(16):
            msg[d, 8 * g : 8 * g + 8, :] = acc
    for c in saves:
        c.wait()


def eta_copies(keep, recv, sl, su, core, sem):
    return [
        pltpu.make_async_copy(keep.at[pl.ds(50, 25)], sl.at[:, core], sem.at[0]),
        pltpu.make_async_copy(keep.at[pl.ds(75, 25)], su.at[:, core], sem.at[1]),
        pltpu.make_async_copy(recv.at[pl.ds(50, 25)], sl.at[:, 1 - core], sem.at[2]),
        pltpu.make_async_copy(recv.at[pl.ds(75, 25)], su.at[:, 1 - core], sem.at[3]),
    ]


def cell(ref, j):
    return square([ref[c, j // 2, pl.ds(j % 2, 8, stride=2), :] for c in range(25)])


def halves(x, y, first):
    return jnp.where(first, x, roll(y, 64)), jnp.where(first, roll(x, 64), y)


def wall_kernel(keep, recv, out, sl, su, sem):
    _, _, core = place()
    copy_all(eta_copies(keep, recv, sl, su, core, sem))
    lb = cell(sl, 0)
    w = lb
    ub = cell(su, 0)
    for j in range(1, 4):
        lb = mm(cell(sl, j), lb)
        w = mm(ub, lb, w)
        ub = mm(ub, cell(su, j))
    for c, x in enumerate(flat(lb) + flat(ub) + flat(w)):
        out[c] = x


def pair_copies(mine, other, both, odd, sem):
    return [
        pltpu.make_async_copy(mine, both.at[odd], sem.at[0]),
        pltpu.make_async_copy(other, both.at[1 - odd], sem.at[1]),
    ]


def pair_kernel(vecs, mine, other, out, give, both, comp, sem):
    _, z, _ = place()
    odd = z % 2
    even = odd == 0
    copy_all(pair_copies(mine, other, both, odd, sem))
    lb_e, ub_e, w_e = [square([both[0, 25 * n + c] for c in range(25)]) for n in range(3)]
    lb_o, ub_o, w_o = [square([both[1, 25 * n + c] for c in range(25)]) for n in range(3)]
    w = mm(ub_e, mm(w_o, lb_e), w_e)
    for c, x in enumerate(flat(mm(lb_o, lb_e)) + flat(mm(ub_e, ub_o)) + flat(w)):
        comp[c] = x
    lv = [vecs[c] for c in range(N)]
    uv = [vecs[N + c] for c in range(N)]
    for c in range(N):
        give[c] = jnp.where(even, lv[c], uv[c])
    new_lv = [jnp.where(even, x, y) for x, y in zip(mv(lb_o, lv), lv)]
    inner = [jnp.where(even, x, y) for x, y in zip(mv(w_o, lv), uv)]
    new_uv = [jnp.where(even, x + y, x) for x, y in zip(mv(ub_e, inner), uv)]
    first = lane_iota() < 64
    base = 37 * odd
    for r in range(ROWS):
        if r < VEC:
            x, y = comp[base + r], comp[base + VEC + r]
        else:
            x, y = new_lv[r - VEC], new_uv[r - VEC]
        x, y = halves(x, y, first)
        out[pl.ds(r, 8, stride=ROWS), :] = x
        out[pl.ds(8 * ROWS + r, 8, stride=ROWS), :] = y


def down_kernel(
    table, flags, got, leaf0, leaf1, store, keep, recv, scaled, vecs,
    sl, su, tree, cs, bh, fl, tb, sem,
):
    chord, z, core = place()
    eta = eta_copies(keep, recv, sl, su, core, sem)
    fetch = [
        pltpu.make_async_copy(store.at[level], tree.at[level], sem.at[4 + level])
        for level in range(LEVELS)
    ]
    kinds = [
        pltpu.make_async_copy(flags, fl, sem.at[4 + LEVELS]),
        pltpu.make_async_copy(table, tb, sem.at[5 + LEVELS]),
    ]
    for c in fetch[::-1] + kinds + eta:
        c.start()
    lane = lane_iota()
    group = lane // 4
    for g in range(3):
        v = [got[s, 8 * g : 8 * g + 8, :] for s in range(16)]
        for bit in range(4):
            step = 1 << bit
            same = (group // step) % 2 == 0
            fresh = list(v)
            for s in range(16):
                if s & step:
                    continue
                a, b = v[s], v[s | step]
                fresh[s] = jnp.where(same, a, roll(b, 4 * step))
                fresh[s | step] = jnp.where(same, roll(a, -4 * step), b)
            v = fresh
        for lo in range(16):
            if 32 * g + lo < 85:
                cs[32 * g + lo] = v[lo]
            if 32 * g + 16 + lo < 85:
                cs[32 * g + 16 + lo] = roll(v[lo], 64)

    def chain(m, t, sign):
        for bit in range(4):
            step = 1 << bit
            ok = group >= step if sign > 0 else group < 16 - step
            far = [roll(x, sign * 4 * step) for x in t]
            t = [jnp.where(ok, new, old) for new, old in zip(mv(m, far, t), t)]
            if bit < 3:
                fm = [[roll(x, sign * 4 * step) for x in row] for row in m]
                new = mm(m, fm)
                m = [[jnp.where(ok, new[i][j], m[i][j]) for j in range(N)] for i in range(N)]
        return t

    zero = jnp.zeros((8, 128), F32)
    t = chain(square([cs[c] for c in range(25)]), [cs[25 + c] for c in range(N)], 1)
    a = [jnp.where(group >= 1, roll(x, 4), zero) for x in t]
    f = mv(square([cs[60 + c] for c in range(25)]), a, [cs[55 + c] for c in range(N)])
    t = chain(square([cs[30 + c] for c in range(25)]), f, -1)
    b = [jnp.where(group < 15, roll(x, -4), zero) for x in t]
    back = (128 - 4 * chord) % 128
    a = [pltpu.roll(x, back, 1) for x in a]
    b = [pltpu.roll(x, back, 1) for x in b]

    for level in range(5, -1, -1):
        dist = 2 << level
        fetch[level].wait()
        a_mid = mv(square([tree[level, c] for c in range(25)]), a, [tree[level, 25 + c] for c in range(N)])
        b_mid = mv(square([tree[level, 30 + c] for c in range(25)]), b, [tree[level, 55 + c] for c in range(N)])
        b_mid = mv(square([tree[level, 60 + c] for c in range(25)]), a_mid, b_mid)
        left = (lane // dist) % 2 == 0
        if level:
            a = [jnp.where(left, x, roll(y, dist)) for x, y in zip(a, a_mid)]
            b = [jnp.where(left, x, roll(y, dist)) for x, y in zip(b_mid, b)]
    even = lane % 2 == 0
    for r in range(2):
        if r == 0:
            ra = [jnp.where(left, x, roll(y, 2)) for x, y in zip(a, a_mid)]
            rb = [jnp.where(left, x, roll(y, 2)) for x, y in zip(b_mid, b)]
        else:
            ra = [jnp.where(left, roll(x, -2), y) for x, y in zip(a, a_mid)]
            rb = [jnp.where(left, roll(x, -2), y) for x, y in zip(b_mid, b)]

        def part(first, count):
            return [(leaf0, leaf1)[r][first + c] for c in range(count)]

        a1 = mv(square(part(0, 25)), ra, part(25, N))
        a2 = mv(square(part(30, 25)), a1, part(55, N))
        b2 = mv(square(part(85, 25)), rb, a2)
        b1 = mv(square(part(60, 25)), b2, a1)
        for c in range(N):
            bh[c, r, 0:8, :] = jnp.where(even, b1[c], roll(b2[c], 1))
            bh[c, r, 8:16, :] = jnp.where(even, roll(b1[c], -1), b2[c])

    for c in kinds:
        c.wait()
    kind = fl[pl.ds(pl.multiple_of(core * 8, 8), 8), :]
    s = []
    for j in range(4):
        s.append([bh[c, j // 2, pl.ds(j % 2, 8, stride=2), :] for c in range(N)])
    for c in range(N):
        factor = zero
        for k in range(3):
            factor = jnp.where(kind == k, tb[k : k + 1, c : c + 1], factor)
        s[0][c] = jnp.where(z == 0, factor, 1.0) * s[0][c]
    for j in range(4):
        for c in range(N):
            scaled[j, c] = s[j][c]
    for c in eta:
        c.wait()
    t = [s[0]]
    for j in range(1, 4):
        t.append(mv(cell(sl, j), t[-1], s[j]))
    u = t[3]
    for j in range(2, -1, -1):
        u = mv(cell(su, j), u, t[j])
    for c in range(N):
        vecs[c] = t[3][c]
        vecs[N + c] = u[c]


def solve_kernel(got, back, turned, ain):
    for n in range(16 * ROWS // 8):
        turned[8 * n : 8 * n + 8, :] = pltpu.roll(got[8 * n : 8 * n + 8, :], 64, 1)

    def value(pair, c):
        odd = int(c > 37)
        c -= 37 * odd
        row = ROWS * (2 * pair + odd) + c % VEC
        return (turned if c >= VEC else got)[row : row + 1, :]

    def block(pair, first):
        return square([value(pair, first + c) for c in range(25)])

    def vec(pair, ref):
        row = 2 * ROWS * pair + VEC
        return [
            ref[row + c : row + c + 1, :] + ref[row + ROWS + c : row + ROWS + c + 1, :]
            for c in range(N)
        ]

    zero = jnp.zeros((1, 128), F32)
    for n in range(16):
        back[8 * n : 8 * n + 8, :] = jnp.zeros((8, 128), F32)
    a = [zero] * N
    for m in range(8):
        for c in range(N):
            ain[8 * m + c : 8 * m + c + 1, :] = a[c]
        if m < 7:
            a = mv(block(m, 0), a, vec(m, got)) if m else vec(m, got)
    first = lax.broadcasted_iota(jnp.int32, (1, 128), 1) < 64
    b = [zero] * N
    for m in range(7, -1, -1):
        a = [ain[8 * m + c : 8 * m + c + 1, :] for c in range(N)]
        for c in range(N):
            x = jnp.where(first, a[c], pltpu.roll(b[c], 64, 1))
            back[16 * m + c : 16 * m + c + 1, :] = x
            back[16 * m + 8 + c : 16 * m + 8 + c + 1, :] = x
        if m:
            f = mv(block(m, 50), a, vec(m, turned))
            b = mv(block(m, 25), b, f)


def finish_kernel(
    got, scaled, keep, recv, vecs, taken, mine, other, own, send, sl, su, res, both, sem
):
    _, z, core = place()
    odd = z % 2
    even = odd == 0
    copies = eta_copies(keep, recv, sl, su, core, sem)
    pair = [
        pltpu.make_async_copy(mine, both.at[odd], sem.at[4]),
        pltpu.make_async_copy(other, both.at[1 - odd], sem.at[5]),
    ]
    for c in pair + copies:
        c.start()
    first = lane_iota() < 64
    a, b = [], []
    for c in range(N):
        x = got[pl.ds(c, 8, stride=8), :]
        y = got[pl.ds(64 + c, 8, stride=8), :]
        a.append(jnp.where(first, x, roll(y, 64)))
        b.append(jnp.where(first, roll(x, 64), y))
    for c in pair:
        c.wait()
    lv_e = [jnp.where(even, vecs[c], taken[c]) for c in range(N)]
    mid = mv(square([both[0, c] for c in range(25)]), a, lv_e)
    low = mv(square([both[1, 50 + c] for c in range(25)]), mid, [taken[c] for c in range(N)])
    low = mv(square([both[1, 25 + c] for c in range(25)]), b, low)
    a = [jnp.where(even, x, y) for x, y in zip(a, mid)]
    b = [jnp.where(even, x, y) for x, y in zip(low, b)]
    for c in copies:
        c.wait()
    lifted = []
    for j in range(4):
        a = mv(cell(sl, j), a, [scaled[j, c] for c in range(N)])
        lifted.append(a)
    for j in range(3, -1, -1):
        b = mv(cell(su, j), b, lifted[j])
        for c in range(N):
            res[c, j // 2, pl.ds(j % 2, 8, stride=2), :] = b[c]
    for c in range(N):
        own[c] = res[c, core]
        send[c] = res[c, 1 - core]


def dma(n):
    return pltpu.SemaphoreType.DMA((n,))


def per_device(
    rhs, jet_mask, jet_source, wall_flags, bc_table, xi_lower, xi_upper, eta_lower, eta_upper
):
    def far(x, *dims):
        return pltpu.with_memory_space_constraint(x.reshape(dims), pltpu.HBM)

    rhs, mask, flags = far(rhs, N, 32, 128), far(jet_mask, 32, 128), far(wall_flags, 16, 128)
    xl, xu, el, eu = (far(x, 25, 32, 128) for x in (xi_lower, xi_upper, eta_lower, eta_upper))
    swap = [(n, n ^ 1) for n in range(lax.axis_size("wall"))]
    near = [(n, n ^ 2) for n in range(lax.axis_size("wall"))]
    groups = [list(range(c, lax.axis_size("wall"), 2)) for c in range(2)]

    def over_z(x):
        return lax.all_to_all(x, "wall", 0, 0, tiled=True, axis_index_groups=groups)

    side = pltpu.VMEM((25, 2, 16, 128), F32)
    def pack(away):
        return pl.pallas_call(
            functools.partial(pack_kernel, away),
            out_shape=shape(105, 16, 128),
            in_specs=[HBM] * 7,
            out_specs=VM,
            scratch_shapes=[
                pltpu.VMEM((N, 16, 128), F32),
                pltpu.VMEM((16, 128), jnp.int32),
                pltpu.SMEM((N,), F32),
                dma(23),
            ],
            compiler_params=params(),
            cost_estimate=cost(0, 2 << 20),
            name="pack_away" if away else "pack_here",
        )(far(jet_source, N), rhs, mask, xl, xu, el, eu)

    recv = lax.ppermute(pack(True), "wall", swap)
    keep = pack(False)
    msg, leaf0, leaf1, store = pl.pallas_call(
        up_kernel,
        out_shape=(
            shape(16, 24, 128),
            shape(110, 8, 128),
            shape(110, 8, 128),
            pltpu.HBM((LEVELS, 85, 8, 128), F32),
        ),
        in_specs=[VM, VM],
        out_specs=(VM, VM, VM, HBM),
        scratch_shapes=[
            pltpu.VMEM((2, 85, 8, 128), F32),
            pltpu.VMEM((85, 8, 128), F32),
            pltpu.VMEM((LEVELS, 85, 8, 128), F32),
            dma(LEVELS),
        ],
        compiler_params=params(),
        cost_estimate=cost(9000 * 1024, 4 << 20),
        name="chord_up",
    )(keep, recv)
    mine = pl.pallas_call(
        wall_kernel,
        out_shape=shape(75, 8, 128),
        in_specs=[ANY, ANY],
        out_specs=VM,
        scratch_shapes=[side, side, dma(4)],
        compiler_params=params(),
        cost_estimate=cost(3 * 250 * 3 * 1024, 2 << 20),
        name="wall_blocks",
    )(keep, recv)
    other = lax.ppermute(mine, "wall", near)
    got = lax.all_to_all(msg, "chord", 0, 0, tiled=True)
    scaled, vecs = pl.pallas_call(
        down_kernel,
        out_shape=(shape(4, N, 8, 128), shape(2 * N, 8, 128)),
        in_specs=[HBM, HBM, VM, VM, VM, HBM, ANY, ANY],
        out_specs=(VM, VM),
        scratch_shapes=[
            side,
            side,
            pltpu.VMEM((LEVELS, 85, 8, 128), F32),
            pltpu.VMEM((85, 8, 128), F32),
            pltpu.VMEM((N, 2, 16, 128), F32),
            pltpu.VMEM((16, 128), jnp.int32),
            pltpu.VMEM((3, N), F32),
            dma(12),
        ],
        compiler_params=params(),
        cost_estimate=cost(50_000_000_000, 4 << 20),
        name="chord_down",
    )(far(bc_table, 3, N), flags, got, leaf0, leaf1, far(store, LEVELS, 85, 8, 128), keep, recv)
    both = pltpu.VMEM((2, 75, 8, 128), F32)
    zmsg, give = pl.pallas_call(
        pair_kernel,
        out_shape=(shape(16 * ROWS, 128), shape(N, 8, 128)),
        in_specs=[VM, ANY, ANY],
        out_specs=(VM, VM),
        scratch_shapes=[both, pltpu.VMEM((75, 8, 128), F32), dma(2)],
        compiler_params=params(),
        name="wall_pair",
    )(vecs, mine, other)
    zgot = over_z(zmsg.reshape(16, ROWS, 128)).reshape(16 * ROWS, 128)
    taken = lax.ppermute(give, "wall", near)
    back = pl.pallas_call(
        solve_kernel,
        out_shape=shape(128, 128),
        in_specs=[VM],
        out_specs=VM,
        scratch_shapes=[pltpu.VMEM((16 * ROWS, 128), F32), pltpu.VMEM((128, 128), F32)],
        compiler_params=params(),
        name="wall_solve",
    )(zgot)
    inflow = over_z(back.reshape(16, 8, 128)).reshape(128, 128)
    own, theirs = pl.pallas_call(
        finish_kernel,
        out_shape=(shape(N, 16, 128), shape(N, 16, 128)),
        in_specs=[VM, VM, ANY, ANY, VM, VM, ANY, ANY],
        out_specs=(VM, VM),
        scratch_shapes=[side, side, pltpu.VMEM((N, 2, 16, 128), F32), both, dma(6)],
        compiler_params=params(),
        name="finish",
    )(inflow, scaled, keep, recv, vecs, taken, mine, other)
    theirs = lax.ppermute(theirs, "wall", swap)
    core = lax.axis_index("wall") % 2
    low = jnp.where(core == 0, own, theirs)
    high = jnp.where(core == 0, theirs, own)
    return jnp.concatenate([low, high], axis=1).reshape(N, 16, 2, 128)


def solution(mesh):
    placed = (
        P(None, None, "wall", "chord"),
        P(None, "wall", "chord"),
        P(),
        P(None, "chord"),
        P(),
        P(None, None, None, "wall", "chord"),
        P(None, None, None, "wall", "chord"),
        P(None, None, None, "wall", "chord"),
        P(None, None, None, "wall", "chord"),
    )
    return jax.shard_map(
        per_device,
        mesh=mesh,
        in_specs=placed,
        out_specs=P(None, None, "wall", "chord"),
        check_vma=False,
    )
```

```python
import functools

import jax
import jax.numpy as jnp
from jax import lax
from jax.experimental import pallas as pl
from jax.experimental.pallas import tpu as pltpu
from jax.sharding import PartitionSpec as P

F32 = jnp.float32
N = 5
ROWS = 24
VEC = 19
ANY = pl.BlockSpec(memory_space=pl.ANY)
HBM = pl.BlockSpec(memory_space=pltpu.HBM)
VM = pl.BlockSpec(memory_space=pltpu.VMEM)
LIMIT = 32 << 20
LEVELS = 6


def shape(*dims):
    return jax.ShapeDtypeStruct(dims, F32)


def params(limit=LIMIT):
    return pltpu.CompilerParams(vmem_limit_bytes=limit)


def cost(flops, nbytes):
    return pl.CostEstimate(flops=flops, bytes_accessed=nbytes, transcendentals=0)


def square(flat):
    return [[flat[N * i + j] for j in range(N)] for i in range(N)]


def flat(m):
    return [x for row in m for x in row]


def dot(xs, ys, start=None):
    total = start
    for x, y in zip(xs, ys):
        total = x * y if total is None else total + x * y
    return total


def mm(a, b, c=None):
    cols = list(zip(*b))
    return [
        [dot(a[i], cols[j], None if c is None else c[i][j]) for j in range(N)] for i in range(N)
    ]


def mv(a, x, c=None):
    return [dot(a[i], x, None if c is None else c[i]) for i in range(N)]


def lane_iota():
    return lax.broadcasted_iota(jnp.int32, (8, 128), 1)


def roll(x, by):
    return pltpu.roll(x, by % 128, 1)


def place():
    wall = lax.axis_index("wall")
    return lax.axis_index("chord"), wall // 2, wall % 2


def copy_all(copies):
    for c in copies:
        c.start()
    for c in copies:
        c.wait()


def pack_kernel(away, jet, rhs, mask, xl, xu, el, eu, dst, rv, mk, jt, sem):
    core = place()[2]
    off = pl.multiple_of((1 - core if away else core) * 16, 16)
    copies = [
        pltpu.make_async_copy(jet, jt, sem.at[20]),
        pltpu.make_async_copy(rhs.at[:, pl.ds(off, 16), :], rv, sem.at[21]),
        pltpu.make_async_copy(mask.at[pl.ds(off, 16), :], mk, sem.at[22]),
    ]
    for n in range(20):
        ref = (xl, xu, el, eu)[n // 5]
        part = ref.at[pl.ds(N * (n % 5), N), pl.ds(off, 16), :]
        copies.append(pltpu.make_async_copy(part, dst.at[pl.ds(N * n, N)], sem.at[n]))
    for c in copies:
        c.start()
    for c in copies[:3]:
        c.wait()
    m = mk[...].astype(F32)
    for c in range(N):
        dst[100 + c] = rv[c] + m * jt[c]
    for c in copies[3:]:
        c.wait()


def compose(left, right):
    lb1, lv1, ub1, uv1, w1 = left
    lb2, lv2, ub2, uv2, w2 = right
    lb = mm(lb2, lb1)
    lv = mv(lb2, lv1, lv2)
    ub = mm(ub1, ub2)
    uv = mv(ub1, mv(w2, lv1, uv2), uv1)
    w = mm(ub1, mm(w2, lb1), w1)
    return lb, lv, ub, uv, w


def node(values):
    return (
        square(values[0:25]),
        list(values[25:30]),
        square(values[30:55]),
        list(values[55:60]),
        square(values[60:85]),
    )


def values_of(n):
    return flat(n[0]) + list(n[1]) + flat(n[2]) + list(n[3]) + flat(n[4])


def up_kernel(keep, recv, msg, leaf0, leaf1, store, n1, n2, tree, sem):
    core = place()[2]
    lane = lane_iota()
    even = lane % 2 == 0
    low = (lane // 2) % 2 == 0

    def split(c, r):
        stays = core == r
        a = jnp.where(stays, keep[c, 0:8, :], recv[c, 0:8, :])
        b = jnp.where(stays, keep[c, 8:16, :], recv[c, 8:16, :])
        return jnp.where(even, a, roll(b, 1)), jnp.where(even, roll(a, -1), b)

    saves = []
    for r in range(2):
        l1, l2 = zip(*[split(c, r) for c in range(25)])
        v1, v2 = zip(*[split(100 + c, r) for c in range(N)])
        u1, u2 = zip(*[split(25 + c, r) for c in range(25)])
        for c, x in enumerate(l1 + v1 + l2 + v2 + u1 + u2):
            (leaf0, leaf1)[r][c] = x
        l1, l2, u1, u2 = square(l1), square(l2), square(u1), square(u2)
        lb = mm(l2, l1)
        lv = mv(l2, v1, v2)
        out = (lb, lv, mm(u1, u2), mv(u1, lv, v1), mm(u1, lb, l1))
        for c, x in enumerate(values_of(out)):
            n1[r, c] = x

    left, right = [], []
    for c in range(85):
        a, b = n1[0, c], n1[1, c]
        left.append(jnp.where(low, a, roll(b, 2)))
        right.append(jnp.where(low, roll(a, -2), b))
    for level in range(6):
        if level:
            left = [n2[c] for c in range(85)]
            right = [roll(x, -(2 << level)) for x in left]
        for c in range(30):
            tree[level, c] = left[c]
        for c in range(30, 85):
            tree[level, c] = right[c]
        saves.append(pltpu.make_async_copy(tree.at[level], store.at[level], sem.at[level]))
        saves[-1].start()
        for c, x in enumerate(values_of(compose(node(left), node(right)))):
            n2[c] = x
    group = lane // 4
    for g in range(3):
        acc = None
        for pos in range(min(32, 85 - 32 * g)):
            x = n2[32 * g + pos]
            acc = x if acc is None else jnp.where(group == pos, roll(x, 4 * pos), acc)
        for d in range(16):
            msg[d, 8 * g : 8 * g + 8, :] = acc
    for c in saves:
        c.wait()


def eta_copies(keep, recv, sl, su, core, sem):
    return [
        pltpu.make_async_copy(keep.at[pl.ds(50, 25)], sl.at[:, core], sem.at[0]),
        pltpu.make_async_copy(keep.at[pl.ds(75, 25)], su.at[:, core], sem.at[1]),
        pltpu.make_async_copy(recv.at[pl.ds(50, 25)], sl.at[:, 1 - core], sem.at[2]),
        pltpu.make_async_copy(recv.at[pl.ds(75, 25)], su.at[:, 1 - core], sem.at[3]),
    ]


def cell(ref, j):
    return square([ref[c, j // 2, pl.ds(j % 2, 8, stride=2), :] for c in range(25)])


def halves(x, y, first):
    return jnp.where(first, x, roll(y, 64)), jnp.where(first, roll(x, 64), y)


def wall_kernel(keep, recv, out, sl, su, sem):
    _, _, core = place()
    copy_all(eta_copies(keep, recv, sl, su, core, sem))
    lb = cell(sl, 0)
    w = lb
    ub = cell(su, 0)
    for j in range(1, 4):
        lb = mm(cell(sl, j), lb)
        w = mm(ub, lb, w)
        ub = mm(ub, cell(su, j))
    for c, x in enumerate(flat(lb) + flat(ub) + flat(w)):
        out[c] = x


def pair_copies(mine, other, both, odd, sem):
    return [
        pltpu.make_async_copy(mine, both.at[odd], sem.at[0]),
        pltpu.make_async_copy(other, both.at[1 - odd], sem.at[1]),
    ]


def pair_kernel(vecs, mine, other, out, give, both, comp, sem):
    _, z, _ = place()
    odd = z % 2
    even = odd == 0
    copy_all(pair_copies(mine, other, both, odd, sem))
    lb_e, ub_e, w_e = [square([both[0, 25 * n + c] for c in range(25)]) for n in range(3)]
    lb_o, ub_o, w_o = [square([both[1, 25 * n + c] for c in range(25)]) for n in range(3)]
    w = mm(ub_e, mm(w_o, lb_e), w_e)
    for c, x in enumerate(flat(mm(lb_o, lb_e)) + flat(mm(ub_e, ub_o)) + flat(w)):
        comp[c] = x
    lv = [vecs[c] for c in range(N)]
    uv = [vecs[N + c] for c in range(N)]
    for c in range(N):
        give[c] = jnp.where(even, lv[c], uv[c])
    new_lv = [jnp.where(even, x, y) for x, y in zip(mv(lb_o, lv), lv)]
    inner = [jnp.where(even, x, y) for x, y in zip(mv(w_o, lv), uv)]
    new_uv = [jnp.where(even, x + y, x) for x, y in zip(mv(ub_e, inner), uv)]
    first = lane_iota() < 64
    base = 37 * odd
    for r in range(ROWS):
        if r < VEC:
            x, y = comp[base + r], comp[base + VEC + r]
        else:
            x, y = new_lv[r - VEC], new_uv[r - VEC]
        x, y = halves(x, y, first)
        out[pl.ds(r, 8, stride=ROWS), :] = x
        out[pl.ds(8 * ROWS + r, 8, stride=ROWS), :] = y


def down_kernel(
    table, flags, got, leaf0, leaf1, store, keep, recv, scaled, vecs,
    sl, su, tree, cs, bh, fl, tb, sem,
):
    chord, z, core = place()
    eta = eta_copies(keep, recv, sl, su, core, sem)
    fetch = [
        pltpu.make_async_copy(store.at[level], tree.at[level], sem.at[4 + level])
        for level in range(LEVELS)
    ]
    kinds = [
        pltpu.make_async_copy(flags, fl, sem.at[4 + LEVELS]),
        pltpu.make_async_copy(table, tb, sem.at[5 + LEVELS]),
    ]
    for c in fetch[::-1] + kinds + eta:
        c.start()
    lane = lane_iota()
    group = lane // 4
    for g in range(3):
        v = [got[s, 8 * g : 8 * g + 8, :] for s in range(16)]
        for bit in range(4):
            step = 1 << bit
            same = (group // step) % 2 == 0
            fresh = list(v)
            for s in range(16):
                if s & step:
                    continue
                a, b = v[s], v[s | step]
                fresh[s] = jnp.where(same, a, roll(b, 4 * step))
                fresh[s | step] = jnp.where(same, roll(a, -4 * step), b)
            v = fresh
        for lo in range(16):
            if 32 * g + lo < 85:
                cs[32 * g + lo] = v[lo]
            if 32 * g + 16 + lo < 85:
                cs[32 * g + 16 + lo] = roll(v[lo], 64)

    def chain(m, t, sign):
        for bit in range(4):
            step = 1 << bit
            ok = group >= step if sign > 0 else group < 16 - step
            far = [roll(x, sign * 4 * step) for x in t]
            t = [jnp.where(ok, new, old) for new, old in zip(mv(m, far, t), t)]
            if bit < 3:
                fm = [[roll(x, sign * 4 * step) for x in row] for row in m]
                new = mm(m, fm)
                m = [[jnp.where(ok, new[i][j], m[i][j]) for j in range(N)] for i in range(N)]
        return t

    zero = jnp.zeros((8, 128), F32)
    t = chain(square([cs[c] for c in range(25)]), [cs[25 + c] for c in range(N)], 1)
    a = [jnp.where(group >= 1, roll(x, 4), zero) for x in t]
    f = mv(square([cs[60 + c] for c in range(25)]), a, [cs[55 + c] for c in range(N)])
    t = chain(square([cs[30 + c] for c in range(25)]), f, -1)
    b = [jnp.where(group < 15, roll(x, -4), zero) for x in t]
    back = (128 - 4 * chord) % 128
    a = [pltpu.roll(x, back, 1) for x in a]
    b = [pltpu.roll(x, back, 1) for x in b]

    for level in range(5, -1, -1):
        dist = 2 << level
        fetch[level].wait()
        a_mid = mv(square([tree[level, c] for c in range(25)]), a, [tree[level, 25 + c] for c in range(N)])
        b_mid = mv(square([tree[level, 30 + c] for c in range(25)]), b, [tree[level, 55 + c] for c in range(N)])
        b_mid = mv(square([tree[level, 60 + c] for c in range(25)]), a_mid, b_mid)
        left = (lane // dist) % 2 == 0
        if level:
            a = [jnp.where(left, x, roll(y, dist)) for x, y in zip(a, a_mid)]
            b = [jnp.where(left, x, roll(y, dist)) for x, y in zip(b_mid, b)]
    even = lane % 2 == 0
    for r in range(2):
        if r == 0:
            ra = [jnp.where(left, x, roll(y, 2)) for x, y in zip(a, a_mid)]
            rb = [jnp.where(left, x, roll(y, 2)) for x, y in zip(b_mid, b)]
        else:
            ra = [jnp.where(left, roll(x, -2), y) for x, y in zip(a, a_mid)]
            rb = [jnp.where(left, roll(x, -2), y) for x, y in zip(b_mid, b)]

        def part(first, count):
            return [(leaf0, leaf1)[r][first + c] for c in range(count)]

        a1 = mv(square(part(0, 25)), ra, part(25, N))
        a2 = mv(square(part(30, 25)), a1, part(55, N))
        b2 = mv(square(part(85, 25)), rb, a2)
        b1 = mv(square(part(60, 25)), b2, a1)
        for c in range(N):
            bh[c, r, 0:8, :] = jnp.where(even, b1[c], roll(b2[c], 1))
            bh[c, r, 8:16, :] = jnp.where(even, roll(b1[c], -1), b2[c])

    for c in kinds:
        c.wait()
    kind = fl[pl.ds(pl.multiple_of(core * 8, 8), 8), :]
    s = []
    for j in range(4):
        s.append([bh[c, j // 2, pl.ds(j % 2, 8, stride=2), :] for c in range(N)])
    for c in range(N):
        factor = zero
        for k in range(3):
            factor = jnp.where(kind == k, tb[k : k + 1, c : c + 1], factor)
        s[0][c] = jnp.where(z == 0, factor, 1.0) * s[0][c]
    for j in range(4):
        for c in range(N):
            scaled[j, c] = s[j][c]
    for c in eta:
        c.wait()
    t = [s[0]]
    for j in range(1, 4):
        t.append(mv(cell(sl, j), t[-1], s[j]))
    u = t[3]
    for j in range(2, -1, -1):
        u = mv(cell(su, j), u, t[j])
    for c in range(N):
        vecs[c] = t[3][c]
        vecs[N + c] = u[c]


def solve_kernel(got, back, turned, ain):
    for n in range(16 * ROWS // 8):
        turned[8 * n : 8 * n + 8, :] = pltpu.roll(got[8 * n : 8 * n + 8, :], 64, 1)

    def value(pair, c):
        odd = int(c > 37)
        c -= 37 * odd
        row = ROWS * (2 * pair + odd) + c % VEC
        return (turned if c >= VEC else got)[row : row + 1, :]

    def block(pair, first):
        return square([value(pair, first + c) for c in range(25)])

    def vec(pair, ref):
        row = 2 * ROWS * pair + VEC
        return [
            ref[row + c : row + c + 1, :] + ref[row + ROWS + c : row + ROWS + c + 1, :]
            for c in range(N)
        ]

    zero = jnp.zeros((1, 128), F32)
    for n in range(16):
        back[8 * n : 8 * n + 8, :] = jnp.zeros((8, 128), F32)
    a = [zero] * N
    for m in range(8):
        for c in range(N):
            ain[8 * m + c : 8 * m + c + 1, :] = a[c]
        if m < 7:
            a = mv(block(m, 0), a, vec(m, got)) if m else vec(m, got)
    first = lax.broadcasted_iota(jnp.int32, (1, 128), 1) < 64
    b = [zero] * N
    for m in range(7, -1, -1):
        a = [ain[8 * m + c : 8 * m + c + 1, :] for c in range(N)]
        for c in range(N):
            x = jnp.where(first, a[c], pltpu.roll(b[c], 64, 1))
            back[16 * m + c : 16 * m + c + 1, :] = x
            back[16 * m + 8 + c : 16 * m + 8 + c + 1, :] = x
        if m:
            f = mv(block(m, 50), a, vec(m, turned))
            b = mv(block(m, 25), b, f)


def finish_kernel(
    got, scaled, keep, recv, vecs, taken, mine, other, own, send, res
):
    _, z, core = place()
    odd = z % 2
    even = odd == 0

    def block(head, j):
        stays = core == j // 2
        at = pl.ds(j % 2, 8, stride=2)
        return square(
            [jnp.where(stays, keep[head + c, at, :], recv[head + c, at, :]) for c in range(25)]
        )

    first = lane_iota() < 64
    a, b = [], []
    for c in range(N):
        x = got[pl.ds(c, 8, stride=8), :]
        y = got[pl.ds(64 + c, 8, stride=8), :]
        a.append(jnp.where(first, x, roll(y, 64)))
        b.append(jnp.where(first, roll(x, 64), y))
    lv_e = [jnp.where(even, vecs[c], taken[c]) for c in range(N)]
    mid = mv(square([jnp.where(even, mine[c], other[c]) for c in range(25)]), a, lv_e)
    low = mv(square([jnp.where(even, other[50 + c], mine[50 + c]) for c in range(25)]), mid, [taken[c] for c in range(N)])
    low = mv(square([jnp.where(even, other[25 + c], mine[25 + c]) for c in range(25)]), b, low)
    a = [jnp.where(even, x, y) for x, y in zip(a, mid)]
    b = [jnp.where(even, x, y) for x, y in zip(low, b)]
    lifted = []
    for j in range(4):
        a = mv(block(50, j), a, [scaled[j, c] for c in range(N)])
        lifted.append(a)
    for j in range(3, -1, -1):
        b = mv(block(75, j), b, lifted[j])
        for c in range(N):
            res[c, j // 2, pl.ds(j % 2, 8, stride=2), :] = b[c]
    for c in range(N):
        own[c] = res[c, core]
        send[c] = res[c, 1 - core]


def dma(n):
    return pltpu.SemaphoreType.DMA((n,))


def per_device(
    rhs, jet_mask, jet_source, wall_flags, bc_table, xi_lower, xi_upper, eta_lower, eta_upper
):
    def far(x, *dims):
        return pltpu.with_memory_space_constraint(x.reshape(dims), pltpu.HBM)

    rhs, mask, flags = far(rhs, N, 32, 128), far(jet_mask, 32, 128), far(wall_flags, 16, 128)
    xl, xu, el, eu = (far(x, 25, 32, 128) for x in (xi_lower, xi_upper, eta_lower, eta_upper))
    swap = [(n, n ^ 1) for n in range(lax.axis_size("wall"))]
    near = [(n, n ^ 2) for n in range(lax.axis_size("wall"))]
    groups = [list(range(c, lax.axis_size("wall"), 2)) for c in range(2)]

    def over_z(x):
        return lax.all_to_all(x, "wall", 0, 0, tiled=True, axis_index_groups=groups)

    side = pltpu.VMEM((25, 2, 16, 128), F32)
    def pack(away):
        return pl.pallas_call(
            functools.partial(pack_kernel, away),
            out_shape=shape(105, 16, 128),
            in_specs=[HBM] * 7,
            out_specs=VM,
            scratch_shapes=[
                pltpu.VMEM((N, 16, 128), F32),
                pltpu.VMEM((16, 128), jnp.int32),
                pltpu.SMEM((N,), F32),
                dma(23),
            ],
            compiler_params=params(),
            cost_estimate=cost(0, 2 << 20),
            name="pack_away" if away else "pack_here",
        )(far(jet_source, N), rhs, mask, xl, xu, el, eu)

    recv = lax.ppermute(pack(True), "wall", swap)
    keep = pack(False)
    msg, leaf0, leaf1, store = pl.pallas_call(
        up_kernel,
        out_shape=(
            shape(16, 24, 128),
            shape(110, 8, 128),
            shape(110, 8, 128),
            pltpu.HBM((LEVELS, 85, 8, 128), F32),
        ),
        in_specs=[VM, VM],
        out_specs=(VM, VM, VM, HBM),
        scratch_shapes=[
            pltpu.VMEM((2, 85, 8, 128), F32),
            pltpu.VMEM((85, 8, 128), F32),
            pltpu.VMEM((LEVELS, 85, 8, 128), F32),
            dma(LEVELS),
        ],
        compiler_params=params(),
        cost_estimate=cost(9000 * 1024, 4 << 20),
        name="chord_up",
    )(keep, recv)
    mine = pl.pallas_call(
        wall_kernel,
        out_shape=shape(75, 8, 128),
        in_specs=[ANY, ANY],
        out_specs=VM,
        scratch_shapes=[side, side, dma(4)],
        compiler_params=params(),
        cost_estimate=cost(3 * 250 * 3 * 1024, 2 << 20),
        name="wall_blocks",
    )(keep, recv)
    other = lax.ppermute(mine, "wall", near)
    got = lax.all_to_all(msg, "chord", 0, 0, tiled=True)
    scaled, vecs = pl.pallas_call(
        down_kernel,
        out_shape=(shape(4, N, 8, 128), shape(2 * N, 8, 128)),
        in_specs=[HBM, HBM, VM, VM, VM, HBM, ANY, ANY],
        out_specs=(VM, VM),
        scratch_shapes=[
            side,
            side,
            pltpu.VMEM((LEVELS, 85, 8, 128), F32),
            pltpu.VMEM((85, 8, 128), F32),
            pltpu.VMEM((N, 2, 16, 128), F32),
            pltpu.VMEM((16, 128), jnp.int32),
            pltpu.VMEM((3, N), F32),
            dma(12),
        ],
        compiler_params=params(),
        cost_estimate=cost(50_000_000_000, 4 << 20),
        name="chord_down",
    )(far(bc_table, 3, N), flags, got, leaf0, leaf1, far(store, LEVELS, 85, 8, 128), keep, recv)
    both = pltpu.VMEM((2, 75, 8, 128), F32)
    zmsg, give = pl.pallas_call(
        pair_kernel,
        out_shape=(shape(16 * ROWS, 128), shape(N, 8, 128)),
        in_specs=[VM, ANY, ANY],
        out_specs=(VM, VM),
        scratch_shapes=[both, pltpu.VMEM((75, 8, 128), F32), dma(2)],
        compiler_params=params(),
        name="wall_pair",
    )(vecs, mine, other)
    zgot = over_z(zmsg.reshape(16, ROWS, 128)).reshape(16 * ROWS, 128)
    taken = lax.ppermute(give, "wall", near)
    back = pl.pallas_call(
        solve_kernel,
        out_shape=shape(128, 128),
        in_specs=[VM],
        out_specs=VM,
        scratch_shapes=[pltpu.VMEM((16 * ROWS, 128), F32), pltpu.VMEM((128, 128), F32)],
        compiler_params=params(),
        name="wall_solve",
    )(zgot)
    inflow = over_z(back.reshape(16, 8, 128)).reshape(128, 128)
    own, theirs = pl.pallas_call(
        finish_kernel,
        out_shape=(shape(N, 16, 128), shape(N, 16, 128)),
        in_specs=[VM] * 8,
        out_specs=(VM, VM),
        scratch_shapes=[pltpu.VMEM((N, 2, 16, 128), F32)],
        compiler_params=params(),
        name="finish",
    )(inflow, scaled, keep, recv, vecs, taken, mine, other)
    theirs = lax.ppermute(theirs, "wall", swap)
    core = lax.axis_index("wall") % 2
    low = jnp.where(core == 0, own, theirs)
    high = jnp.where(core == 0, theirs, own)
    return jnp.concatenate([low, high], axis=1).reshape(N, 16, 2, 128)


def solution(mesh):
    placed = (
        P(None, None, "wall", "chord"),
        P(None, "wall", "chord"),
        P(),
        P(None, "chord"),
        P(),
        P(None, None, None, "wall", "chord"),
        P(None, None, None, "wall", "chord"),
        P(None, None, None, "wall", "chord"),
        P(None, None, None, "wall", "chord"),
    )
    return jax.shard_map(
        per_device,
        mesh=mesh,
        in_specs=placed,
        out_specs=P(None, None, "wall", "chord"),
        check_vma=False,
    )
```
